32 devices in a mesh: fsdp: 4 (over z), ctx: 4 (over y, x), tp: 2 (over core).
Axes of the slice: x: 2, y: 2, z: 4, core: 2. Of those that a mesh axis runs over, the one named last changes fastest.
Arguments:
- tokens: bfloat16 [4096, 1024], P(('fsdp', 'ctx')), may hold values from -6 to 6
- lengths: int32 [4, 4], P('fsdp'), may hold values from 1 to 959, as said below
- norm_gain: bfloat16 [1024], P('fsdp'), may hold values from 0.5 to 1.5
- qkv_weight: bfloat16 [3, 1024, 1024], P(None, 'fsdp', 'tp'), may hold values from -0.1875 to 0.1875
- beta_weight: bfloat16 [1024, 8], P('fsdp', 'tp'), may hold values from -0.1875 to 0.1875
- conv_weight: bfloat16 [3, 4, 8, 128], P(None, None, 'tp', 'fsdp'), may hold values from -3 to 3
- head_gain: bfloat16 [128], P('fsdp'), may hold values from 0.5 to 1.5
- out_weight: bfloat16 [1024, 1024], P('tp', 'fsdp'), may hold values from -0.1875 to 0.1875
- mlp_gain: bfloat16 [1024], P('fsdp'), may hold values from 0.5 to 1.5
- gate_up_weight: bfloat16 [2, 1024, 2816], P(None, 'fsdp', 'tp'), may hold values from -0.1875 to 0.1875
- down_weight: bfloat16 [2816, 1024], P('tp', 'fsdp'), may hold values from -0.15625 to 0.15625
- cotangent: bfloat16 [4096, 1024], P(('fsdp', 'ctx')), may hold values from -6 to 6
Outputs:
- layer_out: bfloat16 [4096, 1024], P(('fsdp', 'ctx'))
- input_grad: float32 [4096, 1024], P(('fsdp', 'ctx'))
- norm_gain_grad: float32 [1024], P('fsdp')
- qkv_grad: float32 [3, 1024, 1024], P(None, 'fsdp', 'tp')
- beta_grad: float32 [1024, 8], P('fsdp', 'tp')
- conv_grad: float32 [3, 4, 8, 128], P(None, None, 'tp', 'fsdp')
- head_gain_grad: float32 [128], P('fsdp')
- out_grad: float32 [1024, 1024], P('tp', 'fsdp')
- mlp_gain_grad: float32 [1024], P('fsdp')
- gate_up_grad: float32 [2, 1024, 2816], P(None, 'fsdp', 'tp')
- down_grad: float32 [2816, 1024], P('tp', 'fsdp')
- rms: float32 [5], replicated
The draws below stay inside these ranges and needn't reach their ends.
Inputs may be any that keep to these rules, and one draw needn't show every extreme that they name: Row g lists the 4 sequence lengths of stream g in order; they sum to at most 1024, the remaining slots at the end are padding. The second sequence of each stream ends at slot 960, so it includes a slot of the first and of the last of its 4 blocks of 256 slots.
All inputs are finite; a program needn't handle non-finite values.
Results may differ from the reference program's by a relative error of at most 0.012.
The reference program's roundings to bfloat16 on the way count: a program that leaves them out, or rounds other values in their place, can miss the bound.
Values may be sent and summed in bfloat16 or wider, within the bound.
No kernel may reach another device: no remote copies, remote signals or barrier semaphores. Data moves between devices by JAX's collectives and lax.ppermute only.
A program may use at most 128 MiB of HBM per device.

```python
import jax
import jax.numpy as jnp
from jax import lax

D = 1024
H = 8
HD = 128
FF = 2816
C = 64
CONV = 4
TOK_DEV = 256
HK = 1024
STREAM = 1024
TOKENS = 4096
N_FSDP = 4
N_CTX = 4


def draw_lengths(key, part):
    stream = TOK_DEV * N_CTX
    key_first, key_pick, key_pad, key_third = jax.random.split(key, 4)
    long_end = 15 * stream // 16
    chosen = jax.random.randint(key_pick, (), 0, N_FSDP)
    forced = jnp.arange(N_FSDP, dtype=jnp.int32) == chosen
    first_len = jnp.where(forced, 1, jax.random.randint(key_first, (N_FSDP,), 1, stream // 16))
    padding = jax.random.randint(key_pad, (N_FSDP,), 0, stream // 32 + 1)
    remainder = stream - long_end - padding
    third_len = jnp.where(forced, 1, jax.random.randint(key_third, (N_FSDP,), jnp.ones((N_FSDP,), jnp.int32), remainder))
    fourth_len = remainder - third_len
    return jnp.stack([first_len, long_end - first_len, third_len, fourth_len], -1).astype(jnp.int32)


def shard_levels(own_key, extent, cuts, low, top_value):
    def one(axis_at, parts):
        steps = jax.random.uniform(jax.random.fold_in(jax.random.fold_in(own_key, 6), axis_at), (parts,), jnp.float32, low / len(cuts), top_value / len(cuts))
        return jnp.repeat(jnp.exp(steps), extent[axis_at] // parts).reshape((-1,) + (1,) * (len(extent) - axis_at - 1))

    loudness = one(*cuts[0])
    for cut in cuts[1:]:
        loudness = loudness * one(*cut)
    return loudness


def noise(own_key, shape, deviation, reach, cuts=(), held_as=jnp.bfloat16):
    values = deviation * jax.random.normal(own_key, shape, jnp.float32)
    if cuts:
        values = values * shard_levels(own_key, shape, cuts, -0.22, 0.18)
    return jnp.clip(values, -reach, reach).astype(held_as)


def setup_inputs(seed: int = 0) -> dict:
    streams_of = jax.random.split(jax.random.key(seed), 13)
    tokens = noise(streams_of[0], (TOKENS, D), 1.0, 6.0, ((0, 16),))
    lengths = draw_lengths(jax.random.fold_in(streams_of[12], 71), 0)
    norm_gain = jnp.clip(1.0 + 0.1 * jax.random.normal(streams_of[2], (D,), jnp.float32), 0.5, 1.5).astype(jnp.bfloat16)
    qkv_weight = noise(streams_of[3], (3, D, HK), D ** -0.5, 0.1875, ((1, 4), (2, 2)))
    beta_weight = noise(streams_of[4], (D, H), D ** -0.5, 0.1875, ((0, 4), (1, 2)))
    conv_weight = noise(streams_of[5], (3, CONV, H, HD), CONV ** -0.5, 3.0, ((2, 2), (3, 4)))
    head_gain = jnp.clip(1.0 + 0.1 * jax.random.normal(streams_of[6], (HD,), jnp.float32), 0.5, 1.5).astype(jnp.bfloat16)
    out_weight = noise(streams_of[7], (HK, D), HK ** -0.5, 0.1875, ((0, 2), (1, 4)))
    mlp_gain = jnp.clip(1.0 + 0.1 * jax.random.normal(streams_of[8], (D,), jnp.float32), 0.5, 1.5).astype(jnp.bfloat16)
    gate_up_weight = noise(streams_of[9], (2, D, FF), D ** -0.5, 0.1875, ((1, 4), (2, 2)))
    down_weight = noise(streams_of[10], (FF, D), (FF // 2) ** -0.5, 0.15625, ((0, 2), (1, 4)))
    cotangent = noise(streams_of[11], (TOKENS, D), 1.0, 6.0, ((0, 16),))
    return {"tokens": tokens, "lengths": lengths, "norm_gain": norm_gain, "qkv_weight": qkv_weight, "beta_weight": beta_weight, "conv_weight": conv_weight, "head_gain": head_gain, "out_weight": out_weight, "mlp_gain": mlp_gain, "gate_up_weight": gate_up_weight, "down_weight": down_weight, "cotangent": cotangent}


PRECISE = lax.Precision.HIGHEST
NORM_EPS = 1e-06

@jax.custom_vjp
def low(v):
    return lax.optimization_barrier(v.astype(jnp.bfloat16)).astype(jnp.float32)

@jax.custom_vjp
def low_back(v):
    return v

def low_keep(v):
    return (low(v), None)

def low_pass(kept, grad):
    return (grad,)

def back_keep(v):
    return (v, None)

def back_low(kept, grad):
    return (low(grad),)
low.defvjp(low_keep, low_pass)
low_back.defvjp(back_keep, back_low)

def product(form, left, right):
    return jnp.einsum(form, left, right, precision=PRECISE)

def rms_norm(values, gain):
    return values * lax.rsqrt(lax.optimization_barrier(jnp.mean(values * values, -1, keepdims=True)) + NORM_EPS) * gain

def l2_norm(values):
    return values * lax.rsqrt(lax.optimization_barrier(jnp.sum(values * values, -1, keepdims=True)) + NORM_EPS)

def seq_layout(lengths_row, first, row_count):
    ends = jnp.cumsum(lengths_row).astype(jnp.int32)
    places = first + jnp.arange(row_count, dtype=jnp.int32)
    passed = ends[None, :] <= places[:, None]
    begins = lax.optimization_barrier(jnp.max(jnp.where(passed, ends[None, :], 0), -1)).astype(jnp.int32)
    seg_ids = lax.optimization_barrier(jnp.sum(passed.astype(jnp.int32), -1))
    valid = (places < ends[-1]).astype(jnp.float32)
    resets = places == begins
    offsets = places[:, None] - (CONV - 1) + jnp.arange(CONV, dtype=jnp.int32)[None, :]
    taps = (offsets >= begins[:, None]).astype(jnp.float32)
    return (seg_ids, resets, valid, taps)

def block_masks(seg_ids, resets):
    seg_blocks = seg_ids.reshape(-1, C)
    same_seq = (seg_blocks[:, :, None] == seg_blocks[:, None, :]).astype(jnp.float32)
    reset_count = jnp.cumsum(resets.reshape(-1, C).astype(jnp.int32), -1)
    carried = (reset_count == 0).astype(jnp.float32)
    return (same_seq, carried)

def conv_heads(extended, conv_taps, taps):
    row_count = taps.shape[0]
    total = jnp.zeros((row_count,) + extended.shape[1:], jnp.float32)
    for offset in range(CONV):
        total = total + extended[offset:offset + row_count] * conv_taps[:, offset][None] * taps[:, offset][:, None, None]
    activated = jax.nn.silu(total)
    head_count = extended.shape[2] // HD
    split_rows = activated.reshape(row_count, 3, head_count, HD)
    return (l2_norm(split_rows[:, 0]), l2_norm(split_rows[:, 1]), split_rows[:, 2])

def to_blocks(values):
    return values.reshape(values.shape[0] // C, C, values.shape[1], values.shape[2]).transpose(2, 0, 1, 3)

def beta_blocks(values):
    return values.reshape(values.shape[0] // C, C, values.shape[1]).transpose(2, 0, 1)

def from_blocks(values):
    return values.transpose(1, 2, 0, 3).reshape(-1, values.shape[0], values.shape[3])

def unit_inverse(lower):
    size_now = lower.shape[-1]
    identity = jnp.eye(size_now, dtype=jnp.float32)
    inverse = identity - lower
    power = lower
    span = 2
    while span < size_now:
        power = product('...ij,...jk->...ik', power, power)
        inverse = product('...ij,...jk->...ik', inverse, identity + power)
        span = span * 2
    return inverse

def block_terms(queries, key_rows, value_rows, beta_rows, same_seq, carried):
    wide = key_rows.shape[-1]
    last_seg = same_seq[:, -1, :]
    key_gram = product('hncd,hnmd->hncm', key_rows, key_rows)
    lower = jnp.tril(beta_rows[..., :, None] * key_gram * same_seq, -1)
    inverse = unit_inverse(lower)
    stacked = beta_rows[..., None] * jnp.concatenate([key_rows, value_rows], -1)
    solved = product('hncm,hnmd->hncd', inverse, stacked)
    w_part = solved[..., :wide]
    u_part = solved[..., wide:]
    query_key = jnp.tril(product('hncd,hnmd->hncm', queries, key_rows) * same_seq)
    keep_all = carried[:, -1]
    trans = keep_all[:, None, None] * jnp.eye(wide, dtype=jnp.float32) - product('hnci,hncj->hnij', w_part * (carried * last_seg)[..., None], key_rows)
    push = product('hnci,hncj->hnij', u_part * last_seg[..., None], key_rows)
    return (w_part, u_part, query_key, queries, trans, push)

def run_blocks(terms, carried, start_state):
    sequenced = tuple((jnp.moveaxis(piece, 1, 0) for piece in terms)) + (carried,)

    def advance(state, pieces):
        w_now, u_now, qk_now, q_now, trans_now, push_now, carry_now = pieces
        carry_col = carry_now[None, :, None]
        from_state = product('hcd,hvd->hcv', w_now, state)
        fresh = u_now - carry_col * from_state
        output = carry_col * product('hcd,hvd->hcv', q_now, state) + product('hcm,hmv->hcv', qk_now, fresh)
        following = product('hvk,hkj->hvj', state, trans_now) + push_now
        return (following, output)
    final_state, outputs = lax.scan(advance, start_state, sequenced)
    return (jnp.moveaxis(outputs, 0, 1), final_state)

def row_total(values, valid):
    return jnp.sum(valid * lax.optimization_barrier(jnp.sum(values * values, -1)))

def layer(weights, x_wide, seg_ids, resets, valid, taps):
    first_gain, qkv_full, beta_full, conv_full, head_full, out_full, second_gain, gate_up_full, down_full = weights
    row_count = x_wide.shape[0]
    normed_in = low(rms_norm(x_wide, first_gain))
    projected = low_back(low(product('td,idk->tik', normed_in, qkv_full)))
    beta_rows = jax.nn.sigmoid(low_back(jnp.dot(normed_in, beta_full, precision=PRECISE)))
    extended = jnp.concatenate([jnp.zeros((CONV - 1, 3, HK), jnp.float32), projected], 0)
    query_raw, key_raw, value_raw = conv_heads(extended, conv_full.reshape(3, CONV, HK), taps)
    same_seq, carried = block_masks(seg_ids, resets)
    terms = block_terms(to_blocks(low(query_raw)) * HD ** (-0.5), to_blocks(low(key_raw)), to_blocks(low(value_raw)), beta_blocks(beta_rows), same_seq, carried)
    out_blocks, final_state = run_blocks(terms, carried, jnp.zeros((H, HD, HD), jnp.float32))
    mixed_out = from_blocks(out_blocks)
    head_normed = low(rms_norm(mixed_out, head_full).reshape(row_count, HK))
    attn_rows = low_back(jnp.dot(head_normed, out_full, precision=PRECISE)) * valid[:, None]
    middle = x_wide + attn_rows
    normed_mid = low(rms_norm(middle, second_gain))
    gate_up = low_back(product('td,idf->tif', normed_mid, gate_up_full))
    activated = low(jax.nn.silu(gate_up[:, 0]) * gate_up[:, 1])
    ffn_rows = low_back(jnp.dot(activated, down_full, precision=PRECISE)) * valid[:, None]
    result = middle + ffn_rows
    stat_sums = jnp.stack([row_total(x_wide, valid), row_total(attn_rows, valid), row_total(middle, valid), row_total(ffn_rows, valid), row_total(result, valid)])
    return (result, (stat_sums, jnp.sum(valid)))

def reference(tokens, lengths, norm_gain, qkv_weight, beta_weight, conv_weight, head_gain, out_weight, mlp_gain, gate_up_weight, down_weight, cotangent):
    weights = tuple((piece.astype(jnp.float32) for piece in (norm_gain, qkv_weight, beta_weight, conv_weight, head_gain, out_weight, mlp_gain, gate_up_weight, down_weight)))
    streams = tokens.reshape(N_FSDP, STREAM, D)
    cot_streams = cotangent.reshape(N_FSDP, STREAM, D)

    def one_stream(totals, pieces):
        stream_rows, stream_cot, stream_lengths = pieces
        seg_ids, resets, valid, taps = seq_layout(stream_lengths, 0, STREAM)

        def forward(weight_in, x_in):
            return layer(weight_in, x_in, seg_ids, resets, valid, taps)
        result, pull_back, extras = jax.vjp(forward, weights, stream_rows.astype(jnp.float32), has_aux=True)
        weight_grads, x_grad = pull_back(stream_cot.astype(jnp.float32))
        grad_total, stat_total, count_total = totals
        grad_total = jax.tree.map(jnp.add, grad_total, weight_grads)
        return ((grad_total, stat_total + extras[0], count_total + extras[1]), (result.astype(jnp.bfloat16), x_grad))
    start = (jax.tree.map(jnp.zeros_like, weights), jnp.zeros((5,), jnp.float32), jnp.zeros((), jnp.float32))
    (grads, stat_total, count_total), (results, x_grads) = lax.scan(one_stream, start, (streams, cot_streams, lengths))
    rms = jnp.sqrt(stat_total / (count_total * D))
    return (results.reshape(TOKENS, D), x_grads.reshape(TOKENS, D), grads[0], grads[1], grads[2], grads[3], grads[4], grads[5], grads[6], grads[7], grads[8], rms)
```

```python
import functools

import jax
import jax.numpy as jnp
from jax import lax
from jax.experimental import pallas as pl
from jax.experimental.pallas import tpu as pltpu
from jax.sharding import PartitionSpec as P

HD = 128
CONV = 4
PAD = 8
EPS = 1e-06
F32 = jnp.float32
BF16 = jnp.bfloat16
NN = (((1,), (0,)), ((), ()))
NT = (((1,), (1,)), ((), ()))
TN = (((0,), (0,)), ((), ()))
SCALE = HD ** (-0.5)


def parts_of(value, count):
    if value.dtype == BF16:
        return [value]
    pieces = []
    for left in range(count):
        piece = value.astype(BF16)
        pieces.append(piece)
        if left + 1 < count:
            value = value - piece.astype(F32)
    return pieces


def mm(left, right, dims=NN, split=2):
    lefts, rights = parts_of(left, split), parts_of(right, split)
    total = None
    for i, a in enumerate(lefts):
        for j, b in enumerate(rights):
            if i + j < max(len(lefts), len(rights)):
                term = lax.dot_general(a, b, dims, preferred_element_type=F32)
                total = term if total is None else total + term
    return total


def sigmoid(v):
    return 1.0 / (1.0 + jnp.exp(-v))


def unit_lower_inverse(lower):
    n = lower.shape[0]
    row = lax.broadcasted_iota(jnp.int32, (n, n), 0)
    col = lax.broadcasted_iota(jnp.int32, (n, n), 1)
    inverse = jnp.where(row == col, 1.0, 0.0) - jnp.where(row // 2 == col // 2, lower, 0.0)
    size = 2
    while size < n:
        inside = (row // (2 * size) == col // (2 * size)) & (row // size != col // size)
        step = jnp.where(inside, lower, 0.0)
        inverse = inverse - mm(inverse, mm(step, inverse))
        size *= 2
    return inverse


def conv_forward(ext_ref, taps, age, rows):
    total = jnp.zeros((rows, HD), F32)
    for k in range(CONV):
        reach = CONV - 1 - k
        rows_k = ext_ref[pl.ds(PAD - reach, rows), :]
        total = total + jnp.where(age >= reach, rows_k, 0.0) * taps[k : k + 1]
    return total


def l2_ratio(values):
    return lax.rsqrt(jnp.sum(values * values, -1, keepdims=True) + EPS)


def terms_kernel(x_ref, w_ref, taps_ref, beta_ref, lb_ref, pre_ref, qkv_ref, tt_ref, y_ref, ms_ref, ext):
    rows = lb_ref.shape[0]
    lb = lb_ref[...]
    place = lax.broadcasted_iota(jnp.int32, (rows, 1), 0)
    age = place - lb
    row = lax.broadcasted_iota(jnp.int32, (rows, rows), 0)
    col = lax.broadcasted_iota(jnp.int32, (rows, rows), 1)
    same = col >= lb
    lb_last = lb_ref[pl.ds(rows - 1, 1), :]
    last = jnp.where(place >= lb_last, 1.0, 0.0)
    keep = jnp.where(lb_last < 0, 1.0, 0.0)
    eye = jnp.where(lax.broadcasted_iota(jnp.int32, (HD, HD), 0) == lax.broadcasted_iota(jnp.int32, (HD, HD), 1), 1.0, 0.0)
    out = []
    for i in range(3):
        pre = lax.dot_general(x_ref[...], w_ref[0, i], NN, preferred_element_type=F32).astype(BF16)
        pre_ref[0, i] = pre
        ext[...] = pre.astype(F32)
        total = conv_forward(ext, taps_ref[0, i], age, rows)
        act = total * sigmoid(total)
        if i < 2:
            act = act * l2_ratio(act)
        act = act.astype(BF16)
        qkv_ref[0, i] = act
        out.append(act)
    _, key, value = out
    beta = beta_ref[0]
    gram = lax.dot_general(key, key, NT, preferred_element_type=F32)
    lower = jnp.where(same & (col < row), beta * gram, 0.0)
    inverse = unit_lower_inverse(lower)
    tt_ref[0] = inverse.T
    scaled = beta * jnp.concatenate([key, value], -1).astype(F32)
    solved = mm(inverse, scaled)
    y_ref[0] = solved
    w_part, u_part = solved[:, :HD], solved[:, HD:]
    ms_ref[0, 0] = keep * (eye - mm(w_part, key, TN))
    ms_ref[0, 1] = mm(last * u_part, key, TN)


def output_kernel(*refs, sources):
    arrived, (y_ref, qkv_ref, lb_ref, gain_ref, o_ref, r_ref, s_ref, n_ref) = refs[:sources], refs[sources:]
    rows = lb_ref.shape[0]
    lb = lb_ref[...]
    row = lax.broadcasted_iota(jnp.int32, (rows, rows), 0)
    col = lax.broadcasted_iota(jnp.int32, (rows, rows), 1)
    carried = jnp.where(lb < 0, 1.0, 0.0)
    state = arrived[-1][0, 1]
    for ref in reversed(arrived[:-1]):
        state = mm(state, ref[0, 0]) + ref[0, 1]
    query, key = qkv_ref[0, 0], qkv_ref[0, 1]
    w_part, u_part = y_ref[0, :, :HD], y_ref[0, :, HD:]
    scores = lax.dot_general(query, key, NT, preferred_element_type=F32)
    scores = jnp.where((col >= lb) & (col <= row), scores * SCALE, 0.0)
    fresh = u_part - carried * mm(w_part, state, NT)
    mixed = carried * (SCALE * mm(query, state, NT)) + mm(scores, fresh)
    o_ref[0] = mixed
    r_ref[0] = fresh
    s_ref[0] = state
    ratio = lax.rsqrt(jnp.mean(mixed * mixed, -1, keepdims=True) + EPS)
    n_ref[...] = (mixed * ratio * gain_ref[...]).astype(BF16)


def mixed_back_kernel(g_ref, o_ref, qkv_ref, y_ref, lb_ref, lbr_ref, gain_ref, do_ref, dr_ref, ds_ref, hg_ref):
    rows = lb_ref.shape[0]
    row = lax.broadcasted_iota(jnp.int32, (rows, rows), 0)
    col = lax.broadcasted_iota(jnp.int32, (rows, rows), 1)
    carried = jnp.where(lb_ref[...] < 0, 1.0, 0.0)
    mixed, grad = o_ref[0], g_ref[...]
    ratio = lax.rsqrt(jnp.mean(mixed * mixed, -1, keepdims=True) + EPS)
    scaled = mixed * ratio
    weighted = grad * gain_ref[...]
    d_mixed = ratio * (weighted - scaled * jnp.mean(weighted * scaled, -1, keepdims=True))
    hg_ref[0] = jnp.broadcast_to(jnp.sum(grad * scaled, 0, keepdims=True), (8, HD))
    query, key = qkv_ref[0, 0], qkv_ref[0, 1]
    turned = lax.dot_general(key, query, NT, preferred_element_type=F32)
    turned = jnp.where((row >= lbr_ref[...]) & (row <= col), turned * SCALE, 0.0)
    d_fresh = mm(turned, d_mixed)
    do_ref[0] = d_mixed
    dr_ref[0] = d_fresh
    ds_ref[0] = SCALE * mm(carried * d_mixed, query, TN) - mm(carried * d_fresh, y_ref[0, :, :HD], TN)


def terms_back_kernel(*refs, sources):
    grads, maps = refs[:sources], refs[sources : 2 * sources - 1]
    (pre_ref, qkv_ref, tt_ref, y_ref, r_ref, s_ref, do_ref, dr_ref, beta_ref, taps_ref, lb_ref, lbr_ref,
     g_ref, gb_ref, cg_ref, ext, acc) = refs[2 * sources - 1 :]
    rows = lb_ref.shape[0]
    lb = lb_ref[...]
    place = lax.broadcasted_iota(jnp.int32, (rows, 1), 0)
    age = place - lb
    row = lax.broadcasted_iota(jnp.int32, (rows, rows), 0)
    col = lax.broadcasted_iota(jnp.int32, (rows, rows), 1)
    lb_last = lb_ref[pl.ds(rows - 1, 1), :]
    last = jnp.where(place >= lb_last, 1.0, 0.0)
    carried = jnp.where(lb < 0, 1.0, 0.0)
    same = col >= lb
    d_state = grads[-1][0]
    for grad, turn in zip(reversed(grads[:-1]), reversed(maps), strict=True):
        d_state = mm(d_state, turn[0, 0], NT) + grad[0]
    query, key, value = qkv_ref[0, 0], qkv_ref[0, 1], qkv_ref[0, 2]
    solved = y_ref[0]
    fresh, state, d_mixed = r_ref[0], s_ref[0], do_ref[0]
    beta = beta_ref[0]
    d_fresh = dr_ref[0] + last * mm(key, d_state, NT)
    lower_eq = same & (col <= row)
    d_scores = jnp.where(lower_eq, SCALE * mm(d_mixed, fresh, NT), 0.0)
    turned = jnp.where((row >= lbr_ref[...]) & (row <= col), SCALE * mm(fresh, d_mixed, NT), 0.0)
    d_query = mm(d_scores, key) + carried * (SCALE * mm(d_mixed, state))
    d_key = mm(turned, query) + mm(last * fresh, d_state)
    d_solved = jnp.concatenate([-carried * mm(d_fresh, state), d_fresh], -1)
    d_scaled = mm(tt_ref[0], d_solved)
    d_value = beta * d_scaled[:, HD:]
    d_key = d_key + beta * d_scaled[:, :HD]
    d_beta = jnp.sum(d_scaled[:, :HD] * key.astype(F32) + d_scaled[:, HD:] * value.astype(F32), -1, keepdims=True)
    gram = lax.dot_general(key, key, NT, preferred_element_type=F32)
    d_lower = jnp.where(same & (col < row), -mm(d_scaled, solved, NT), 0.0)
    d_beta = d_beta + jnp.sum(d_lower * gram, -1, keepdims=True)
    d_gram = beta * d_lower
    d_key = d_key + mm(d_gram, key) + mm(d_gram, key, TN)
    gb_ref[0] = d_beta * beta * (1.0 - beta)
    acc[...] = jnp.zeros_like(acc)
    for i, grad in enumerate((d_query, d_key, d_value)):
        taps = taps_ref[0, i]
        ext[...] = pre_ref[0, i].astype(F32)
        total = conv_forward(ext, taps, age, rows)
        sig = sigmoid(total)
        if i < 2:
            act = total * sig
            ratio = l2_ratio(act)
            unit = act * ratio
            grad = ratio * (grad - unit * jnp.sum(grad * unit, -1, keepdims=True))
        grad = grad * sig * (1.0 + total * (1.0 - sig))
        back = jnp.zeros((rows + PAD, HD), F32)
        for k in range(CONV):
            reach = CONV - 1 - k
            grad_k = jnp.where(age >= reach, grad, 0.0)
            rows_k = ext[pl.ds(PAD - reach, rows), :]
            cg_ref[0, pl.ds(i * CONV + k, 1), :] = jnp.sum(grad_k * rows_k, 0, keepdims=True)
            acc[pl.ds(PAD, rows), :] = grad_k
            back = back + acc[pl.ds(reach, rows + PAD), :] * taps[k : k + 1]
        g_ref[0, i] = back


def head_spec(*shape):
    return pl.BlockSpec((1,) + shape, lambda h: (h,) + (0,) * len(shape))


def whole_spec(*shape):
    return pl.BlockSpec(shape, lambda h: (0,) * len(shape))


def params():
    return pltpu.CompilerParams(vmem_limit_bytes=56 * 1024 * 1024, dimension_semantics=("arbitrary",))


def sds(*shape, dtype=F32):
    return jax.ShapeDtypeStruct(shape, dtype)


def delta_terms(x_ext, weights, taps, beta, lb):
    heads, rows = beta.shape[0], lb.shape[0]
    width = x_ext.shape[1]
    ext = rows + PAD
    return pl.pallas_call(
        terms_kernel,
        name="delta_terms",
        grid=(heads,),
        in_specs=[whole_spec(ext, width), head_spec(3, width, HD), head_spec(3, CONV, HD), head_spec(rows, 1), whole_spec(rows, 1)],
        out_specs=[head_spec(3, ext, HD), head_spec(3, rows, HD), head_spec(rows, rows), head_spec(rows, 2 * HD), head_spec(2, HD, HD)],
        out_shape=[
            sds(heads, 3, ext, HD, dtype=BF16),
            sds(heads, 3, rows, HD, dtype=BF16),
            sds(heads, rows, rows),
            sds(heads, rows, 2 * HD),
            sds(heads, 2, HD, HD),
        ],
        scratch_shapes=[pltpu.VMEM((ext, HD), F32)],
        compiler_params=params(),
        cost_estimate=pl.CostEstimate(flops=heads * 4_000_000_000, bytes_accessed=8_000_000, transcendentals=0),
    )(x_ext, weights, taps, beta, lb)


def delta_outputs(arrived, solved, qkv, lb, gain):
    heads, rows = solved.shape[0], lb.shape[0]
    return pl.pallas_call(
        functools.partial(output_kernel, sources=len(arrived)),
        name="delta_outputs",
        grid=(heads,),
        in_specs=[head_spec(2, HD, HD)] * len(arrived)
        + [head_spec(rows, 2 * HD), head_spec(3, rows, HD), whole_spec(rows, 1), whole_spec(1, HD)],
        out_specs=[head_spec(rows, HD), head_spec(rows, HD), head_spec(HD, HD), pl.BlockSpec((rows, HD), lambda h: (0, h))],
        out_shape=[sds(heads, rows, HD), sds(heads, rows, HD), sds(heads, HD, HD), sds(rows, heads * HD, dtype=BF16)],
        compiler_params=params(),
        cost_estimate=pl.CostEstimate(flops=heads * 1_000_000_000, bytes_accessed=5_000_000, transcendentals=0),
    )(*arrived, solved, qkv, lb, gain)


def mixed_back(head_grad, mixed, qkv, solved, lb, lb_row, gain):
    heads, rows = solved.shape[0], lb.shape[0]
    return pl.pallas_call(
        mixed_back_kernel,
        name="mixed_back",
        grid=(heads,),
        in_specs=[
            pl.BlockSpec((rows, HD), lambda h: (0, h)),
            head_spec(rows, HD),
            head_spec(3, rows, HD),
            head_spec(rows, 2 * HD),
            whole_spec(rows, 1),
            whole_spec(1, rows),
            whole_spec(1, HD),
        ],
        out_specs=[head_spec(rows, HD), head_spec(rows, HD), head_spec(HD, HD), head_spec(8, HD)],
        out_shape=[sds(heads, rows, HD), sds(heads, rows, HD), sds(heads, HD, HD), sds(heads, 8, HD)],
        compiler_params=params(),
        cost_estimate=pl.CostEstimate(flops=heads * 1_000_000_000, bytes_accessed=5_000_000, transcendentals=0),
    )(head_grad, mixed, qkv, solved, lb, lb_row, gain)


def terms_back(grads, maps, pre, qkv, turned, solved, fresh, state, d_mixed, d_fresh, beta, taps, lb, lb_row):
    heads, rows = solved.shape[0], lb.shape[0]
    ext = rows + PAD
    return pl.pallas_call(
        functools.partial(terms_back_kernel, sources=len(grads)),
        name="terms_back",
        grid=(heads,),
        in_specs=[head_spec(HD, HD)] * len(grads)
        + [head_spec(1, HD, HD)] * len(maps)
        + [
            head_spec(3, ext, HD),
            head_spec(3, rows, HD),
            head_spec(rows, rows),
            head_spec(rows, 2 * HD),
            head_spec(rows, HD),
            head_spec(HD, HD),
            head_spec(rows, HD),
            head_spec(rows, HD),
            head_spec(rows, 1),
            head_spec(3, CONV, HD),
            whole_spec(rows, 1),
            whole_spec(1, rows),
        ],
        out_specs=[head_spec(3, ext, HD), head_spec(rows, 1), head_spec(16, HD)],
        out_shape=[sds(heads, 3, ext, HD), sds(heads, rows, 1), sds(heads, 16, HD)],
        scratch_shapes=[pltpu.VMEM((ext, HD), F32), pltpu.VMEM((ext + PAD, HD), F32)],
        compiler_params=params(),
        cost_estimate=pl.CostEstimate(flops=heads * 3_000_000_000, bytes_accessed=8_000_000, transcendentals=0),
    )(*grads, *maps, pre, qkv, turned, solved, fresh, state, d_mixed, d_fresh, beta, taps, lb, lb_row)


def shifted(value, axis, steps):
    count = lax.axis_size(axis)
    first, end = max(0, -steps), min(count, count - steps)
    return lax.ppermute(value, axis, [(s, s + steps) for s in range(first, end)])


def swapped(value, axis, mask):
    return lax.ppermute(value, axis, [(s, s ^ mask) for s in range(lax.axis_size(axis))])


def tp_sum(value):
    return value + swapped(value, "tp", 1)


def plane_gather(value):
    half = value.shape[0] // 2
    one, two = swapped(value, "ctx", 1), swapped(value, "ctx", 2)
    three = jnp.concatenate([swapped(one[:half], "ctx", 2), swapped(two[half:], "ctx", 1)])
    return [value, one, two, three]


def in_order(pieces):
    here = lax.axis_index("ctx")
    stacked = jnp.stack(pieces)
    return [lax.dynamic_index_in_dim(stacked, here ^ k, 0, False) for k in range(len(pieces))]


def plane_reduce(own, first_one, first_two, second_one, second_two):
    from_one = [swapped(v.astype(BF16), "ctx", 1) for v in first_one]
    from_two = [swapped(v.astype(BF16), "ctx", 2) for v in first_two]
    late_two = swapped((second_two + from_one[1].astype(F32)).astype(BF16), "ctx", 2)
    late_one = swapped((second_one + from_two[1].astype(F32)).astype(BF16), "ctx", 1)
    half_a = own[0] + from_one[0].astype(F32) + late_two.astype(F32)
    half_b = own[1] + from_two[0].astype(F32) + late_one.astype(F32)
    return half_a.astype(BF16), half_b.astype(BF16)


def butterfly(value):
    for axis in ("ctx", "fsdp"):
        mask = 1
        while mask < lax.axis_size(axis):
            value = value + swapped(value, axis, mask)
            mask *= 2
    return value


def rms_norm(values, gain):
    return values * lax.rsqrt(jnp.mean(values * values, -1, keepdims=True) + EPS) * gain


def norm_back(values, gain, grad):
    ratio = lax.rsqrt(jnp.mean(values * values, -1, keepdims=True) + EPS)
    scaled = values * ratio
    weighted = grad * gain
    value_grad = ratio * (weighted - scaled * jnp.mean(weighted * scaled, -1, keepdims=True))
    return value_grad, jnp.sum(grad * scaled, 0)


def row_total(values, valid):
    return jnp.sum(valid * jnp.sum(values * values, -1))


def bdot(left, right, dims=NN):
    return lax.dot_general(left, right, dims, preferred_element_type=F32)


def local(
    tokens, lengths, norm_gain, qkv_weight, beta_weight, conv_weight, head_gain, out_weight, mlp_gain, gate_up_weight, down_weight, cotangent
):
    rows, width = tokens.shape
    n_ctx, n_fsdp = lax.axis_size("ctx"), lax.axis_size("fsdp")
    ctx, fsdp = lax.axis_index("ctx"), lax.axis_index("fsdp")
    d_loc = qkv_weight.shape[1]
    heads = beta_weight.shape[1]
    units = down_weight.shape[0]
    hk = heads * HD
    hd_loc = head_gain.shape[0]

    first = ctx * rows
    ends, total = [], 0
    for i in range(lengths.shape[1]):
        total = total + lengths[0, i]
        ends.append(total)
    place = first + lax.broadcasted_iota(jnp.int32, (rows, 1), 0)
    begins = jnp.zeros((rows, 1), jnp.int32)
    for end in ends:
        begins = jnp.where(end <= place, jnp.maximum(begins, end), begins)
    lb = begins - first
    lb_row = lb.reshape(1, rows)
    valid = (place < ends[-1]).astype(F32)
    valid_row = valid[:, 0]

    small = jnp.concatenate([norm_gain, mlp_gain, head_gain, beta_weight.reshape(-1), conv_weight.reshape(-1)])
    small_rows = -(-small.shape[0] // (HD * 16)) * 16
    small = jnp.pad(small, (0, small_rows * HD - small.shape[0])).reshape(small_rows, HD)
    qkv_part = lax.dynamic_slice_in_dim(qkv_weight, ctx * HD, HD, 2).reshape(3 * d_loc, HD)
    pack = lax.all_gather(jnp.concatenate([qkv_part, small]), "fsdp", axis=0)
    out_part = lax.dynamic_slice_in_dim(out_weight, ctx * HD, HD, 0)
    down_part = lax.dynamic_slice_in_dim(down_weight, ctx * (units // n_ctx), units // n_ctx, 0)
    od_all = lax.all_gather(jnp.concatenate([out_part, down_part]), "fsdp", axis=0)
    gu_rows = d_loc // n_ctx
    gu_part = lax.dynamic_slice_in_dim(gate_up_weight, ctx * gu_rows, gu_rows, 1)
    gu_all = lax.all_gather(gu_part, "fsdp", axis=0)

    qkv_heads = in_order(plane_gather(pack[:, : 3 * d_loc]))
    qkv_heads = jnp.stack([p.reshape(n_fsdp, 3, d_loc, HD).transpose(1, 0, 2, 3).reshape(3, width, HD) for p in qkv_heads])
    od = in_order(plane_gather(od_all))
    od = [p.transpose(1, 0, 2).reshape(-1, width) for p in od]
    out_full = jnp.concatenate([p[:HD] for p in od])
    down_full = jnp.concatenate([p[HD:] for p in od])
    gu = jnp.stack(in_order(plane_gather(gu_all)))
    gate_up_full = gu.transpose(2, 1, 0, 3, 4).reshape(2, width, units)

    flat = pack[:, 3 * d_loc :].reshape(n_fsdp, -1).astype(F32)
    at = 0
    first_gain = flat[:, at : at + d_loc].reshape(1, width)
    at += d_loc
    second_gain = flat[:, at : at + d_loc].reshape(1, width)
    at += d_loc
    head_full = flat[:, at : at + hd_loc].reshape(1, HD)
    at += hd_loc
    beta_full = flat[:, at : at + d_loc * heads].reshape(width, heads).astype(BF16)
    at += d_loc * heads
    conv_full = flat[:, at : at + 3 * CONV * heads * hd_loc].reshape(n_fsdp, 3, CONV, heads, hd_loc)
    conv_full = conv_full.transpose(3, 1, 2, 0, 4).reshape(heads, 3, CONV, HD)

    x_ext = jnp.concatenate([shifted(tokens[rows - PAD :], "ctx", 1), tokens])
    normed_ext = rms_norm(x_ext.astype(F32), first_gain).astype(BF16)
    normed_in = normed_ext[PAD:]
    x_wide = tokens.astype(F32)
    beta = jax.nn.sigmoid(bdot(normed_in, beta_full)).T.reshape(heads, rows, 1)
    pre, qkv, turned, solved, ends_map = delta_terms(normed_ext, qkv_heads, conv_full, beta, lb)

    arrived = [shifted(ends_map, "ctx", r) for r in range(1, n_ctx)]
    ahead = [shifted(ends_map[:, :1], "ctx", -r) for r in range(1, n_ctx - 1)]
    mixed, fresh, state, head_out = delta_outputs(arrived, solved, qkv, lb, head_full)

    attn = tp_sum(bdot(head_out, out_full)) * valid
    middle = x_wide + attn
    normed_mid = rms_norm(middle, second_gain).astype(BF16)
    gate = bdot(normed_mid, gate_up_full[0])
    up = bdot(normed_mid, gate_up_full[1])
    sig = jax.nn.sigmoid(gate)
    act = (gate * sig * up).astype(BF16)
    ffn = tp_sum(bdot(act, down_full)) * valid
    result = middle + ffn

    cot = cotangent.astype(F32)
    g_ffn = (cot * valid).astype(BF16)
    g_act = bdot(g_ffn, down_full, NT)
    g_up = (g_act * gate * sig).astype(BF16)
    g_gate = (g_act * up * sig * (1.0 + gate * (1.0 - sig))).astype(BF16)
    mid_part = bdot(g_gate, gate_up_full[0], NT) + bdot(g_up, gate_up_full[1], NT)

    def by_ctx(value, axis):
        return [lax.dynamic_index_in_dim(value, ctx ^ j, axis, False) for j in range(n_ctx)]

    act_t = act.T.reshape(n_ctx, 2, units // n_ctx // 2, rows)
    act_p = by_ctx(act_t, 0)
    down_g = [[bdot(p[h], g_ffn) for h in range(2)] for p in act_p]
    down_sum = plane_reduce(
        down_g[0], [down_g[1][0], down_g[3][0]], [down_g[2][1], down_g[3][1]], down_g[1][1], down_g[2][0]
    )
    down_sum = jnp.concatenate(down_sum).reshape(-1, n_fsdp, d_loc)
    down_sh = lax.psum_scatter(down_sum, "fsdp", scatter_dimension=1)

    g_gu = jnp.concatenate([g_gate, g_up], -1)
    mid_t = normed_mid.T.reshape(n_fsdp, n_ctx, 2, gu_rows // 2, rows).transpose(1, 2, 0, 3, 4)
    mid_p = by_ctx(mid_t, 0)
    gu_g = [[bdot(p[h].reshape(-1, rows), g_gu) for h in range(2)] for p in mid_p]
    gu_sum = plane_reduce(gu_g[0], [gu_g[1][0], gu_g[3][0]], [gu_g[2][1], gu_g[3][1]], gu_g[1][1], gu_g[2][0])
    gu_sum = jnp.stack(gu_sum).reshape(2, n_fsdp, gu_rows // 2, 2 * units)
    gu_sh = lax.psum_scatter(gu_sum, "fsdp", scatter_dimension=1)

    mid_grad = tp_sum(mid_part)
    mid_norm_grad, second_gain_grad = norm_back(middle, second_gain, mid_grad)
    g_middle = cot + mid_norm_grad
    g_attn = (g_middle * valid).astype(BF16)
    g_head = bdot(g_attn, out_full, NT)

    head_t = head_out.T.reshape(n_ctx, 2, HD // 2, rows)
    head_p = by_ctx(head_t, 0)
    out_g = [[bdot(p[h], g_attn) for h in range(2)] for p in head_p]
    out_sum = plane_reduce(out_g[0], [out_g[1][0], out_g[3][0]], [out_g[2][1], out_g[3][1]], out_g[1][1], out_g[2][0])
    out_sum = jnp.concatenate(out_sum).reshape(-1, n_fsdp, d_loc)
    out_sh = lax.psum_scatter(out_sum, "fsdp", scatter_dimension=1)

    d_mixed, d_fresh, d_state, head_gain_part = mixed_back(g_head, mixed, qkv, solved, lb, lb_row, head_full)
    behind = [shifted(d_state, "ctx", -r) for r in range(1, n_ctx)]
    g_ext, g_logit, conv_grad = terms_back(
        behind, ahead, pre, qkv, turned, solved, fresh, state, d_mixed, d_fresh, beta, conv_full, lb, lb_row
    )
    rim = shifted(g_ext[:, :, PAD - (CONV - 1) : PAD], "ctx", -1)
    g_pre = jnp.concatenate([g_ext[:, :, PAD : PAD + rows - (CONV - 1)], g_ext[:, :, PAD + rows - (CONV - 1) :] + rim], 2).astype(BF16)
    g_logit = g_logit[:, :, 0].astype(BF16)

    in_t = normed_in.T.reshape(n_fsdp, 2, d_loc // 2, rows).transpose(1, 0, 2, 3).reshape(2, width // 2, rows)
    g_p = [p.transpose(1, 0, 2).reshape(rows, 3 * HD) for p in by_ctx(g_pre, 0)]
    qkv_g = [[bdot(in_t[h], p) for h in range(2)] for p in g_p]
    qkv_sum = plane_reduce(qkv_g[0], [qkv_g[1][0], qkv_g[3][0]], [qkv_g[2][1], qkv_g[3][1]], qkv_g[1][1], qkv_g[2][0])
    qkv_sum = jnp.stack(qkv_sum).reshape(2, n_fsdp, d_loc // 2, 3 * HD)
    qkv_sh = lax.psum_scatter(qkv_sum, "fsdp", scatter_dimension=1)

    in_part = bdot(g_logit, beta_full, (((0,), (1,)), ((), ())))
    g_rows = g_pre.transpose(2, 1, 0, 3).reshape(rows, 3, hk)
    qkv_wide = qkv_heads.transpose(1, 2, 0, 3).reshape(3, width, hk)
    for i in range(3):
        in_part = in_part + bdot(g_rows[:, i], qkv_wide[i], NT)
    head_gain_row = jnp.pad(jnp.sum(head_gain_part[:, 0], 0), (0, width - HD))
    in_all = tp_sum(jnp.concatenate([in_part, jnp.broadcast_to(head_gain_row[None], (8, width))]))
    x_norm_grad, first_gain_grad = norm_back(x_wide, first_gain, in_all[:rows])
    input_grad = g_middle + x_norm_grad
    beta_grad = bdot(normed_in, g_logit, (((0,), (1,)), ((), ())))

    stats = jnp.stack([row_total(v, valid_row) for v in (x_wide, attn, middle, ffn, result)] + [jnp.sum(valid_row)])
    sums = butterfly(
        jnp.concatenate(
            [first_gain_grad, second_gain_grad, in_all[rows, :HD], beta_grad.reshape(-1), conv_grad[:, : 3 * CONV].reshape(-1), stats]
        )
    )
    at = 0
    first_out = lax.dynamic_slice_in_dim(sums[at : at + width], fsdp * d_loc, d_loc)
    at += width
    second_out = lax.dynamic_slice_in_dim(sums[at : at + width], fsdp * d_loc, d_loc)
    at += width
    head_out_grad = lax.dynamic_slice_in_dim(sums[at : at + HD], fsdp * hd_loc, hd_loc)
    at += HD
    beta_out = lax.dynamic_slice_in_dim(sums[at : at + width * heads].reshape(width, heads), fsdp * d_loc, d_loc)
    at += width * heads
    conv_out = sums[at : at + heads * 3 * CONV * HD].reshape(heads, 3, CONV, HD).transpose(1, 2, 0, 3)
    conv_out = lax.dynamic_slice_in_dim(conv_out, fsdp * hd_loc, hd_loc, 3)
    at += heads * 3 * CONV * HD
    stat = sums[at : at + 6]
    rms = jnp.sqrt(stat[:5] / (stat[5] * width))

    def whole(part):
        pieces = [part] + [swapped(part, "ctx", j) for j in range(1, n_ctx)]
        return jnp.stack(in_order(pieces)).astype(F32)

    down_out = whole(down_sh).reshape(units, d_loc)
    gu_out = whole(gu_sh).reshape(d_loc, 2, units).transpose(1, 0, 2)
    out_out = whole(out_sh).reshape(hk, d_loc)
    qkv_out = whole(qkv_sh).reshape(n_ctx, d_loc, 3, HD).transpose(2, 1, 0, 3).reshape(3, d_loc, hk)
    return (
        result.astype(BF16),
        input_grad,
        first_out,
        qkv_out,
        beta_out,
        conv_out,
        head_out_grad,
        out_out,
        second_out,
        gu_out,
        down_out,
        rms,
    )


def solution(mesh):
    return jax.shard_map(
        local,
        mesh=mesh,
        in_specs=(
            P(("fsdp", "ctx"), None),
            P("fsdp", None),
            P("fsdp"),
            P(None, "fsdp", "tp"),
            P("fsdp", "tp"),
            P(None, None, "tp", "fsdp"),
            P("fsdp"),
            P("tp", "fsdp"),
            P("fsdp"),
            P(None, "fsdp", "tp"),
            P("tp", "fsdp"),
            P(("fsdp", "ctx"), None),
        ),
        out_specs=(
            P(("fsdp", "ctx"), None),
            P(("fsdp", "ctx"), None),
            P("fsdp"),
            P(None, "fsdp", "tp"),
            P("fsdp", "tp"),
            P(None, None, "tp", "fsdp"),
            P("fsdp"),
            P("tp", "fsdp"),
            P("fsdp"),
            P(None, "fsdp", "tp"),
            P("tp", "fsdp"),
            P(),
        ),
        check_vma=False,
    )
```

```python
import functools

import jax
import jax.numpy as jnp
from jax import lax
from jax.experimental import pallas as pl
from jax.experimental.pallas import tpu as pltpu
from jax.sharding import PartitionSpec as P

HD = 128
CONV = 4
PAD = 8
EPS = 1e-06
F32 = jnp.float32
BF16 = jnp.bfloat16
NN = (((1,), (0,)), ((), ()))
NT = (((1,), (1,)), ((), ()))
TN = (((0,), (0,)), ((), ()))
SCALE = HD ** (-0.5)
GU_BLOCKS = 6
SMALL_ROWS = 24

ANY = pl.BlockSpec(memory_space=pl.ANY)
SMEM = pl.BlockSpec(memory_space=pltpu.SMEM)
VMEM = pl.BlockSpec(memory_space=pltpu.VMEM)


def parts_of(value, count):
    if value.dtype == BF16:
        return [value]
    pieces = []
    for left in range(count):
        piece = value.astype(BF16)
        pieces.append(piece)
        if left + 1 < count:
            value = value - piece.astype(F32)
    return pieces


def pdot(left, right, dims=NN):
    return lax.dot_general(left, right, dims, preferred_element_type=F32)


def mm_parts(lefts, rights, dims=NN):
    total = None
    for i, a in enumerate(lefts):
        for j, b in enumerate(rights):
            if i + j < max(len(lefts), len(rights)):
                term = pdot(a, b, dims)
                total = term if total is None else total + term
    return total


def mm(left, right, dims=NN, split=2):
    return mm_parts(parts_of(left, split), parts_of(right, split), dims)


def sigmoid(v):
    return 1.0 / (1.0 + jnp.exp(-v))


def iota(shape, axis):
    return lax.broadcasted_iota(jnp.int32, shape, axis)


def slots(meta, rows, axis, lengths):
    first = meta[0] * rows
    place = iota((rows, 1) if axis == 0 else (1, rows), axis) + first
    begins, end = jnp.zeros_like(place), 0
    for i in range(lengths):
        end = end + meta[2 + i]
        begins = jnp.where(end <= place, jnp.maximum(begins, end), begins)
    return begins - first, place < end


def unit_lower_inverses(lowers):
    n = lowers[0].shape[0]
    half = n // 2
    row, col = iota((half, half), 0), iota((half, half), 1)
    blocks = [low[at : at + half, at : at + half] for low in lowers for at in (0, half)]
    inverses = [jnp.where(row == col, 1.0, 0.0) - jnp.where(row // 2 == col // 2, b, 0.0) for b in blocks]
    split = [parts_of(b, 2) for b in blocks]
    zero = jnp.zeros((half, half), BF16)
    size = 2
    while size < half:
        inside = (row // (2 * size) == col // (2 * size)) & (row // size != col // size)
        pieces = [parts_of(inv, 2) for inv in inverses]
        steps = [mm_parts([jnp.where(inside, s, zero) for s in sp], pc) for sp, pc in zip(split, pieces, strict=True)]
        inverses = [inv - mm_parts(pc, parts_of(st, 2)) for inv, pc, st in zip(inverses, pieces, steps, strict=True)]
        size *= 2
    out = []
    for i, low in enumerate(lowers):
        top, bottom = inverses[2 * i], inverses[2 * i + 1]
        corner = -mm(bottom, mm(low[half:, :half], top))
        out.append((top, corner, bottom))
    return out


def conv_rows(pre, reach):
    return (pltpu.roll(pre, reach, 0) if reach else pre)[PAD:]


def conv_forward(pre, taps, age):
    total = jnp.zeros((pre.shape[0] - PAD, pre.shape[1]), F32)
    for k in range(CONV):
        reach = CONV - 1 - k
        total = total + jnp.where(age >= reach, conv_rows(pre, reach), 0.0) * taps[k : k + 1]
    return total


def pick(refs, j, *index):
    value = refs[-1][index]
    for k in range(len(refs) - 1, 0, -1):
        value = jnp.where(j == k, refs[k - 1][index], value)
    return value


def l2_ratio(values):
    return lax.rsqrt(jnp.sum(values * values, -1, keepdims=True) + EPS)


def rms_ratio(values):
    return lax.rsqrt(jnp.mean(values * values, -1, keepdims=True) + EPS)


def norm_back(values, gain, grad):
    ratio = rms_ratio(values)
    scaled = values * ratio
    weighted = grad * gain
    value_grad = ratio * (weighted - scaled * jnp.mean(weighted * scaled, -1, keepdims=True))
    return value_grad, jnp.sum(grad * scaled, 0, keepdims=True)


def terms_kernel(*refs, lengths, n_fsdp, cut):
    (meta, x_ref, gain_ref, bw_ref, taps_ref, local_ref, own_ref, a1, b1, a2, b2, a3, b3,
     w_ref, pre_ref, act_ref, tt_ref, y_ref, ms_ref, xt_ref, xh_ref, beta_ref, sem) = refs
    heads = w_ref.shape[0]
    d_loc = local_ref.shape[1]
    rows = x_ref.shape[0] - PAD
    ctx, fsdp = meta[0], meta[1]

    def fill(source, head, i, shard):
        at = pl.multiple_of(shard * d_loc, d_loc)
        pltpu.make_async_copy(source, w_ref.at[head, i, pl.ds(at, d_loc), :], sem).start()

    for i in range(3):
        for f in range(n_fsdp):
            fill(own_ref.at[f, pl.ds(i * d_loc, d_loc), :], ctx, i, f)
    for j, (a, b) in enumerate(((a1, b1), (a2, b2), (a3, b3))):
        head = ctx ^ (j + 1)
        for i in range(3):
            fill(local_ref.at[i, :, pl.ds(pl.multiple_of(head * HD, HD), HD)], head, i, fsdp)
            for r in range(n_fsdp - 1):
                block = r * 3 + i
                source = a.at[block] if block < cut else b.at[block - cut]
                fill(source, head, i, lax.rem(fsdp + r + 1, n_fsdp))

    x_wide = x_ref[...].astype(F32)
    normed = (x_wide * rms_ratio(x_wide) * gain_ref[...]).astype(BF16)
    xt_ref[...] = normed[PAD:].T
    xh_ref[...] = normed[:PAD].T
    beta = sigmoid(pdot(normed[PAD:], bw_ref[...]))
    beta_ref[...] = beta
    lb, _ = slots(meta, rows, 0, lengths)
    place = iota((rows, 1), 0)
    age = place - lb
    row, col = iota((rows, rows), 0), iota((rows, rows), 1)
    below = (col >= lb) & (col < row)
    lb_last = lb[rows - 1 :]
    last = jnp.where(place >= lb_last, 1.0, 0.0)
    keep = jnp.where(lb_last < 0, 1.0, 0.0)
    eye = jnp.where(iota((HD, HD), 0) == iota((HD, HD), 1), 1.0, 0.0)
    pltpu.make_async_copy(w_ref, w_ref, sem).wait()

    lowers, keys, scaled = [], [], []
    for h in range(heads):
        acts = []
        for i in range(3):
            pre = pdot(normed, w_ref[h, i]).astype(BF16)
            pre_ref[h, i] = pre
            total = conv_forward(pre.astype(F32), taps_ref[h, i], age)
            act = total * sigmoid(total)
            if i < 2:
                act = act * l2_ratio(act)
            acts.append(act.astype(BF16))
            act_ref[h, i] = acts[i]
        key, value = acts[1], acts[2]
        beta_h = beta[:, h : h + 1]
        lowers.append(jnp.where(below, beta_h * pdot(key, key, NT), 0.0))
        keys.append(key)
        scaled.append(beta_h * jnp.concatenate([key, value], -1).astype(F32))
    half = rows // 2
    for h, (top, corner, bottom) in enumerate(unit_lower_inverses(lowers)):
        tt_ref[h, :half, :half] = top.T
        tt_ref[h, :half, half:] = corner.T
        tt_ref[h, half:, :half] = jnp.zeros((half, half), F32)
        tt_ref[h, half:, half:] = bottom.T
        upper = mm(top, scaled[h][:half])
        lower = mm(jnp.concatenate([corner, bottom], -1), scaled[h])
        solved = jnp.concatenate([upper, lower])
        y_ref[h] = solved
        ms_ref[h, 0] = (keep * (eye - mm(solved[:, :HD], keys[h], TN))).astype(BF16)
        ms_ref[h, 1] = mm(last * solved[:, HD:], keys[h], TN).astype(BF16)


def output_kernel(*refs, lengths, sources):
    (meta, y_ref, act_ref, gain_ref, o0, o1, o2, o3), refs = refs[:8], refs[8:]
    arrived, (ow_ref, mixed_ref, r_ref, s_ref, n_ref, attn_ref, sem) = refs[:sources], refs[sources:]
    heads, rows = y_ref.shape[:2]
    ctx = meta[0]
    for j, piece in enumerate((o0, o1, o2, o3)):
        pltpu.make_async_copy(piece, ow_ref.at[ctx ^ j], sem).start()
    lb, _ = slots(meta, rows, 0, lengths)
    row, col = iota((rows, rows), 0), iota((rows, rows), 1)
    upto = (col >= lb) & (col <= row)
    carried = jnp.where(lb < 0, 1.0, 0.0)
    normed = []
    for h in range(heads):
        state = jnp.zeros((HD, HD), F32)
        for c in range(sources):
            after = pick(arrived, ctx ^ c, h, 1).astype(F32)
            if c:
                after = after + mm(state, pick(arrived, ctx ^ c, h, 0))
            state = jnp.where(c < ctx, after, state)
        query, key = act_ref[h, 0], act_ref[h, 1]
        w_part, u_part = y_ref[h, :, :HD], y_ref[h, :, HD:]
        scores = jnp.where(upto, pdot(query, key, NT) * SCALE, 0.0)
        fresh = u_part - carried * mm(w_part, state, NT)
        mixed = carried * (SCALE * mm(query, state, NT)) + mm(scores, fresh)
        mixed_ref[h] = mixed
        r_ref[h] = fresh
        s_ref[h] = state
        out = (mixed * rms_ratio(mixed) * gain_ref[...]).astype(BF16)
        n_ref[:, h * HD : (h + 1) * HD] = out
        normed.append(out)
    pltpu.make_async_copy(ow_ref, ow_ref, sem).wait()
    total = pdot(normed[0], ow_ref[0], NT)
    for h in range(1, heads):
        total = total + pdot(normed[h], ow_ref[h], NT)
    attn_ref[...] = total


def mlp_kernel(*refs, lengths, n_fsdp):
    (meta, x_ref, attn_ref, other_ref, gain_ref, cot_ref, local_ref, own_ref, a1, b1, a2, b2, a3, b3, down_ref,
     mid_ref, nt_ref, at_ref, g_ref, gf_ref, ffn_ref, part_ref, st_ref, w, gu, sem) = refs
    rows, width = x_ref.shape
    units = down_ref.shape[0]
    d_loc = local_ref.shape[0]
    step = GU_BLOCKS * HD
    half = step // 2
    quarters = w.shape[0]
    ctx, fsdp = meta[0], meta[1]

    def fill(source, quarter, shard, at, size):
        start = pl.multiple_of(shard * d_loc, d_loc)
        pltpu.make_async_copy(source, w.at[quarter, pl.ds(start, d_loc), pl.ds(at, size)], sem).start()

    for f in range(n_fsdp):
        fill(own_ref.at[f], ctx, f, 0, step)
    for j, (a, b) in enumerate(((a1, b1), (a2, b2), (a3, b3))):
        quarter = ctx ^ (j + 1)
        fill(local_ref.at[:, pl.ds(pl.multiple_of(quarter * step, HD), step)], quarter, fsdp, 0, step)
        for r in range(n_fsdp - 1):
            shard = lax.rem(fsdp + r + 1, n_fsdp)
            fill(a.at[r], quarter, shard, 0, half)
            fill(b.at[r], quarter, shard, half, half)

    _, inside = slots(meta, rows, 0, lengths)
    valid = jnp.where(inside, 1.0, 0.0)
    x_wide = x_ref[...].astype(F32)
    attn = (attn_ref[...] + other_ref[...]) * valid
    middle = x_wide + attn
    mid_ref[...] = middle
    for i, v in enumerate((x_wide, attn, middle)):
        st_ref[i : i + 1] = jnp.sum(valid * v * v, 0, keepdims=True)
    normed = (middle * rms_ratio(middle) * gain_ref[...]).astype(BF16)
    nt_ref[...] = normed.T
    g_ffn = (cot_ref[...].astype(F32) * valid).astype(BF16)
    gf_ref[...] = g_ffn
    g_act = pdot(g_ffn, down_ref[...], NT)
    pltpu.make_async_copy(w, w, sem).wait()
    for q in range(quarters):
        gu[:, q * step : (q + 1) * step] = pdot(normed, w[q])
    gate, up = gu[:, :units], gu[:, units : 2 * units]
    sig = sigmoid(gate)
    act = (gate * sig * up).astype(BF16)
    at_ref[...] = act.T
    g_up = g_act * gate * sig
    g_gate = g_act * up * sig * (1.0 + gate * (1.0 - sig))
    gu[:, :units] = g_gate
    gu[:, units : 2 * units] = g_up
    part = None
    for q in range(quarters):
        real = min(step, 2 * units - q * step)
        grad = gu[:, q * step : q * step + real].astype(BF16)
        if real < step:
            grad = jnp.concatenate([grad, jnp.zeros((rows, step - real), BF16)], -1)
        g_ref[ctx ^ q] = grad
        term = pdot(grad, w[q], NT)
        part = term if part is None else part + term
    part_ref[...] = part
    ffn_ref[...] = pdot(act, down_ref[...])


def mlp_grads_kernel(nt_ref, g_ref, x3_ref, y3_ref, x1_ref, y2_ref, late_x_ref, late_y_ref, own_ref):
    half = g_ref.shape[2] // 2
    nt = nt_ref[...]

    def put(ref, j, side):
        ref[...] = pdot(nt, g_ref[j, :, side * half : (side + 1) * half]).astype(BF16)

    put(x3_ref, 3, 0)
    put(y3_ref, 3, 1)
    put(x1_ref, 1, 0)
    put(y2_ref, 2, 1)
    put(late_x_ref, 1, 1)
    put(late_y_ref, 2, 0)
    put(own_ref.at[0], 0, 0)
    put(own_ref.at[1], 0, 1)


def middle_kernel(
    meta, part_ref, part2_ref, ffn_ref, ffn2_ref, mid_ref, cot_ref, gain_ref, hgain_ref, ow_ref, n_ref, mixed_ref, act_ref, y_ref,
    out_ref, gm_ref, og_ref, do_ref, dr_ref, ds_ref, sm_ref, *, lengths
):
    heads, rows = mixed_ref.shape[:2]
    ctx = meta[0]
    lb, inside = slots(meta, rows, 0, lengths)
    lb_row, _ = slots(meta, rows, 1, lengths)
    valid = jnp.where(inside, 1.0, 0.0)
    row, col = iota((rows, rows), 0), iota((rows, rows), 1)
    upto = (row >= lb_row) & (row <= col)
    carried = jnp.where(lb < 0, 1.0, 0.0)
    middle = mid_ref[...]
    value_grad, gain_grad = norm_back(middle, gain_ref[...], part_ref[...] + part2_ref[...])
    g_middle = cot_ref[...].astype(F32) + value_grad
    gm_ref[...] = g_middle
    g_attn = (g_middle * valid).astype(BF16)
    turned_grad = g_attn.T
    total = jnp.zeros((1, HD), F32)
    for h in range(heads):
        key = act_ref[h, 1]
        g_head = pdot(g_attn, ow_ref[h])
        d_mixed, part = norm_back(mixed_ref[h], hgain_ref[...], g_head)
        total = total + part
        turned = jnp.where(upto, pdot(key, act_ref[h, 0], NT) * SCALE, 0.0)
        d_fresh = mm(turned, d_mixed)
        do_ref[h] = d_mixed
        dr_ref[h] = d_fresh
        d_state = SCALE * mm(carried * d_mixed, act_ref[h, 0], TN) - mm(carried * d_fresh, y_ref[h, :, :HD], TN)
        ds_ref[h] = d_state.astype(BF16)
        og_ref[ctx ^ h] = pdot(turned_grad, n_ref[:, h * HD : (h + 1) * HD]).astype(BF16)
    ffn = (ffn_ref[...] + ffn2_ref[...]) * valid
    result = middle + ffn
    out_ref[...] = result.astype(BF16)
    sm_ref[...] = jnp.zeros_like(sm_ref)
    sm_ref[0:1] = gain_grad
    sm_ref[1:2, :HD] = total
    sm_ref[2:3] = jnp.sum(valid * ffn * ffn, 0, keepdims=True)
    sm_ref[3:4] = jnp.sum(valid * result * result, 0, keepdims=True)
    sm_ref[4:5] = jnp.broadcast_to(jnp.sum(valid, 0, keepdims=True), gain_grad.shape) / gain_grad.shape[1]


def delta_back_kernel(*refs, lengths, sources):
    meta, grads, maps = refs[0], refs[1 : 1 + sources], refs[1 + sources : 1 + 2 * sources]
    (pre_ref, act_ref, tt_ref, y_ref, r_ref, s_ref, do_ref, dr_ref, beta_ref, taps_ref, w_ref, bw_ref, xt_ref, xh_ref, sm_ref, og_ref,
     a0, a1, a2, a3, b0, b1, b2, b3, part_ref, bg_ref, cg_ref) = refs[1 + 2 * sources :]
    heads, rows = r_ref.shape[:2]
    width = w_ref.shape[2]
    ext = rows + PAD
    ctx = meta[0]
    lb, _ = slots(meta, rows, 0, lengths)
    lb_row, _ = slots(meta, rows, 1, lengths)
    place = iota((rows, 1), 0)
    age = place - lb
    row, col = iota((rows, rows), 0), iota((rows, rows), 1)
    last = jnp.where(place >= lb[rows - 1 :], 1.0, 0.0)
    carried = jnp.where(lb < 0, 1.0, 0.0)
    upto = (col >= lb) & (col <= row)
    below = (col >= lb) & (col < row)
    turned_upto = (row >= lb_row) & (row <= col)
    lane = iota((rows, HD), 1)
    logits = jnp.zeros((rows, HD), F32)
    top = jnp.zeros((PAD, HD), F32)
    xt, xh = xt_ref[...], xh_ref[...]
    part = jnp.zeros((rows, width), F32)
    ahead = jnp.zeros((PAD, width), F32)
    for h in range(heads):
        d_state = jnp.zeros((HD, HD), F32)
        for c in range(sources, 0, -1):
            before = pick(grads, ctx ^ c, h).astype(F32)
            if c < sources:
                before = before + mm(d_state, pick(maps, ctx ^ c, h, 0), NT)
            d_state = jnp.where(c > ctx, before, d_state)
        query, key, value = act_ref[h, 0], act_ref[h, 1], act_ref[h, 2]
        solved = y_ref[h]
        fresh, state, d_mixed = r_ref[h], s_ref[h], do_ref[h]
        beta = beta_ref[:, h : h + 1]
        d_fresh = dr_ref[h] + last * mm(key, d_state, NT)
        d_scores = jnp.where(upto, SCALE * mm(d_mixed, fresh, NT), 0.0)
        turned = jnp.where(turned_upto, SCALE * mm(fresh, d_mixed, NT), 0.0)
        d_query = mm(d_scores, key) + carried * (SCALE * mm(d_mixed, state))
        d_key = mm(turned, query) + mm(last * fresh, d_state)
        d_solved = jnp.concatenate([-carried * mm(d_fresh, state), d_fresh], -1)
        d_scaled = mm(tt_ref[h], d_solved)
        d_value = beta * d_scaled[:, HD:]
        d_key = d_key + beta * d_scaled[:, :HD]
        d_beta = jnp.sum(d_scaled[:, :HD] * key.astype(F32) + d_scaled[:, HD:] * value.astype(F32), -1, keepdims=True)
        d_lower = jnp.where(below, -mm(d_scaled, solved, NT), 0.0)
        d_beta = d_beta + jnp.sum(d_lower * pdot(key, key, NT), -1, keepdims=True)
        d_gram = beta * d_lower
        d_key = d_key + mm(d_gram, key) + mm(d_gram, key, TN)
        logits = jnp.where(lane == h, d_beta * beta * (1.0 - beta), logits)
        g_main, g_head = [], []
        for i, grad in enumerate((d_query, d_key, d_value)):
            taps = taps_ref[h, i]
            pre = pre_ref[h, i].astype(F32)
            total = conv_forward(pre, taps, age)
            sig = sigmoid(total)
            if i < 2:
                act = total * sig
                ratio = l2_ratio(act)
                unit = act * ratio
                grad = ratio * (grad - unit * jnp.sum(grad * unit, -1, keepdims=True))
            grad = grad * sig * (1.0 + total * (1.0 - sig))
            back = jnp.zeros((ext, HD), F32)
            for k in range(CONV):
                reach = CONV - 1 - k
                grad_k = jnp.where(age >= reach, grad, 0.0)
                cg_ref[h, i * CONV + k : i * CONV + k + 1, :] = jnp.sum(grad_k * conv_rows(pre, reach), 0, keepdims=True)
                padded = jnp.concatenate([top, grad_k])
                back = back + (pltpu.roll(padded, ext - reach, 0) if reach else padded) * taps[k : k + 1]
            g_main.append(back[PAD:].astype(BF16))
            g_head.append(back[:PAD].astype(BF16))
            part = part + pdot(g_main[i], w_ref[h, i], NT)
            ahead = ahead + pdot(g_head[i], w_ref[h, i], NT)
        piece = pdot(xt, jnp.concatenate(g_main, -1)) + pdot(xh, jnp.concatenate(g_head, -1))
        piece = piece.astype(BF16)
        for j, (a, b) in enumerate(((a0, b0), (a1, b1), (a2, b2), (a3, b3))):

            @pl.when(ctx ^ j == h)
            def _(a=a, b=b, j=j, piece=piece):
                a[...] = piece[:, : 2 * HD]
                b[:, :HD] = piece[:, 2 * HD :]
                b[:, HD:] = og_ref[j]

    logits = logits.astype(BF16)
    part_ref[:rows] = part + pdot(logits, bw_ref[...], NT)
    part_ref[rows:ext] = ahead
    part_ref[ext:] = jnp.zeros((PAD, width), F32)
    part_ref[ext : ext + 1, :HD] = sm_ref[1:2, :HD]
    bg_ref[...] = lax.dot_general(logits, xt, (((0,), (1,)), ((), ())), preferred_element_type=F32)[:PAD]


def last_kernel(x_ref, gain_ref, part_ref, other_ref, rim_ref, gm_ref, sm_ref, st_ref, bg_ref, cg_ref, grad_ref, small_ref):
    rows, width = x_ref.shape
    heads = cg_ref.shape[0]
    total = part_ref[...] + other_ref[...]
    grad = jnp.concatenate([total[: rows - PAD], total[rows - PAD : rows] + rim_ref[...]])
    value_grad, gain_grad = norm_back(x_ref[...].astype(F32), gain_ref[...], grad)
    grad_ref[...] = gm_ref[...] + value_grad
    small_ref[...] = jnp.zeros_like(small_ref)
    small_ref[0:1] = gain_grad
    small_ref[1:2] = sm_ref[0:1]
    small_ref[2 : 2 + heads] = bg_ref[:heads]
    small_ref[6:9] = st_ref[0:3]
    small_ref[9:11] = sm_ref[2:4]
    small_ref[11:12] = sm_ref[4:5]
    small_ref[12:13, :HD] = total[rows + PAD : rows + PAD + 1, :HD]
    per = width // HD
    for h in range(heads):
        for k in range(3 * CONV):
            at = h * 3 * CONV + k
            small_ref[13 + at // per : 14 + at // per, (at % per) * HD : (at % per + 1) * HD] = cg_ref[h, k : k + 1]


def gate_up_whole_kernel(meta, p0, p1, p2, p3, gu_ref):
    ctx = meta[0]
    units = gu_ref.shape[2]
    for q in range(4):
        for j, ref in enumerate((p0, p1, p2, p3)):

            @pl.when(ctx ^ j == q)
            def _(ref=ref, q=q):
                for b in range(GU_BLOCKS):
                    at = (q * GU_BLOCKS + b) * HD
                    if at < 2 * units:
                        gu_ref[at // units, :, at % units : at % units + HD] = ref[:, b * HD : (b + 1) * HD].astype(F32)


def mixer_whole_kernel(meta, p0, p1, p2, p3, qkv_ref, out_ref):
    ctx = meta[0]
    for q in range(4):
        for j, ref in enumerate((p0, p1, p2, p3)):

            @pl.when(ctx ^ j == q)
            def _(ref=ref, q=q):
                for i in range(3):
                    qkv_ref[i, :, q * HD : (q + 1) * HD] = ref[:, i * HD : (i + 1) * HD].astype(F32)
                out_ref[q * HD : (q + 1) * HD, :] = ref[:, 3 * HD :].T.astype(F32)


def sds(*shape, dtype=F32):
    return jax.ShapeDtypeStruct(shape, dtype)


def call(body, name, out_shape, in_specs, args, scratch=(), gflops=1, mbytes=4):
    return pl.pallas_call(
        body,
        name=name,
        in_specs=in_specs,
        out_specs=jax.tree.map(lambda _: VMEM, out_shape),
        out_shape=out_shape,
        scratch_shapes=list(scratch),
        compiler_params=pltpu.CompilerParams(vmem_limit_bytes=56 * 1024 * 1024),
        cost_estimate=pl.CostEstimate(flops=gflops * 10**9, bytes_accessed=mbytes * 10**6, transcendentals=0),
    )(*args)


def shifted(value, axis, steps):
    count = lax.axis_size(axis)
    first, end = max(0, -steps), min(count, count - steps)
    return lax.ppermute(value, axis, [(s, s + steps) for s in range(first, end)])


def swapped(value, axis, mask):
    return lax.ppermute(value, axis, [(s, s ^ mask) for s in range(lax.axis_size(axis))])


def others(value):
    count, here = lax.axis_size("fsdp"), lax.axis_index("fsdp")
    return [lax.dynamic_index_in_dim(value, (here + r) % count, 0) for r in range(1, count)]


def plane_gather(a, b):
    a1, b2 = swapped(a, "ctx", 1), swapped(b, "ctx", 2)
    b1, a2 = swapped(b, "ctx", 1), swapped(a, "ctx", 2)
    return [(a1, b1), (a2, b2), (swapped(a1, "ctx", 2), swapped(b2, "ctx", 1))]


def in_order(pieces):
    here = lax.axis_index("ctx")
    stacked = jnp.stack(pieces)
    return [lax.dynamic_index_in_dim(stacked, here ^ k, 0, False) for k in range(len(pieces))]


def plane_sum(pieces):
    return (pieces[0].astype(F32) + pieces[1].astype(F32)) + (pieces[2].astype(F32) + pieces[3].astype(F32))


def butterfly(value):
    for axis in ("ctx", "fsdp"):
        mask = 1
        while mask < lax.axis_size(axis):
            value = value + swapped(value, axis, mask)
            mask *= 2
    return value


def local(
    tokens, lengths, norm_gain, qkv_weight, beta_weight, conv_weight, head_gain, out_weight, mlp_gain, gate_up_weight, down_weight, cotangent
):
    rows, width = tokens.shape
    n_ctx, n_fsdp = lax.axis_size("ctx"), lax.axis_size("fsdp")
    ctx, fsdp = lax.axis_index("ctx"), lax.axis_index("fsdp")
    d_loc = qkv_weight.shape[1]
    heads = beta_weight.shape[1]
    units = down_weight.shape[0]
    hd_loc = head_gain.shape[0]
    n_len = lengths.shape[1]
    step = GU_BLOCKS * HD
    ext = rows + PAD
    meta = jnp.concatenate([jnp.stack([ctx, fsdp]).astype(jnp.int32), lengths[0]])

    small = jnp.concatenate([norm_gain, mlp_gain, head_gain, beta_weight.reshape(-1), conv_weight.reshape(-1)])
    small_rows = -(-small.shape[0] // (HD * 16)) * 16
    small = jnp.pad(small, (0, small_rows * HD - small.shape[0])).reshape(small_rows, HD)
    qkv_part = lax.dynamic_slice_in_dim(qkv_weight, ctx * HD, HD, 2).reshape(3 * d_loc, HD)
    out_part = lax.dynamic_slice_in_dim(out_weight, ctx * HD, HD, 0).T
    pack = lax.all_gather(jnp.concatenate([qkv_part, small]), "fsdp", axis=0)
    gu_local = jnp.concatenate(
        [gate_up_weight[0], gate_up_weight[1], jnp.zeros((d_loc, n_ctx * step - 2 * units), BF16)], -1
    )
    gu_part = lax.dynamic_slice_in_dim(gu_local, ctx * step, step, 1)
    gu_out_own = lax.all_gather(jnp.concatenate([gu_part, out_part], -1), "fsdp", axis=0)
    gu_own = gu_out_own[:, :, :step]
    down_full = lax.all_gather(down_weight, "fsdp", axis=1, tiled=True)
    x_ext = jnp.concatenate([shifted(tokens[rows - PAD :], "ctx", 1), tokens])

    cut = 3 * (n_fsdp - 1) // 2
    blocks = [o.reshape(-1, HD)[: 3 * d_loc].reshape(3, d_loc, HD) for o in others(pack)]
    blocks = jnp.concatenate(blocks)
    qkv_pieces = plane_gather(blocks[:cut], blocks[cut:])
    out_own = gu_out_own[:, :, step:].reshape(width, HD)
    out_pieces = [out_own] + [swapped(out_own, "ctx", j) for j in range(1, n_ctx)]

    flat = pack[:, 3 * d_loc :].reshape(n_fsdp, -1)
    at = 0
    first_gain = flat[:, at : at + d_loc].reshape(1, width).astype(F32)
    at += d_loc
    second_gain = flat[:, at : at + d_loc].reshape(1, width).astype(F32)
    at += d_loc
    head_full = flat[:, at : at + hd_loc].reshape(1, HD).astype(F32)
    at += hd_loc
    beta_full = jnp.pad(flat[:, at : at + d_loc * heads].reshape(width, heads), ((0, 0), (0, HD - heads)))
    at += d_loc * heads
    conv_full = flat[:, at : at + 3 * CONV * heads * hd_loc].reshape(n_fsdp, 3, CONV, heads, hd_loc)
    conv_full = conv_full.transpose(3, 1, 2, 0, 4).reshape(heads, 3, CONV, HD).astype(F32)

    qkv_full, pre, acts, turned, solved, ends_map, normed_t, normed_far, beta = call(
        functools.partial(terms_kernel, lengths=n_len, n_fsdp=n_fsdp, cut=cut),
        "delta_terms",
        (
            sds(heads, 3, width, HD, dtype=BF16),
            sds(heads, 3, ext, HD, dtype=BF16),
            sds(heads, 3, rows, HD, dtype=BF16),
            sds(heads, rows, rows),
            sds(heads, rows, 2 * HD),
            sds(heads, 2, HD, HD, dtype=BF16),
            sds(width, rows, dtype=BF16),
            sds(width, PAD, dtype=BF16),
            sds(rows, HD),
        ),
        [SMEM] + [VMEM] * 4 + [ANY] * 8,
        (meta, x_ext, first_gain, beta_full, conv_full, qkv_weight, pack, *[p for pair in qkv_pieces for p in pair]),
        [pltpu.SemaphoreType.DMA],
        gflops=15,
        mbytes=8,
    )
    arrived = [swapped(ends_map, "ctx", j) for j in range(1, n_ctx)]
    gu_far = jnp.concatenate(others(gu_own))
    gu_a, gu_b, _ = lax.optimization_barrier((gu_far[:, :, : step // 2], gu_far[:, :, step // 2 :], ends_map))
    gu_pieces = plane_gather(gu_a, gu_b)
    out_full, mixed, fresh, state, head_out, attn_part = call(
        functools.partial(output_kernel, lengths=n_len, sources=n_ctx - 1),
        "delta_outputs",
        (
            sds(heads, width, HD, dtype=BF16),
            sds(heads, rows, HD),
            sds(heads, rows, HD),
            sds(heads, HD, HD),
            sds(rows, heads * HD, dtype=BF16),
            sds(rows, width),
        ),
        [SMEM] + [VMEM] * 3 + [ANY] * n_ctx + [VMEM] * len(arrived),
        (meta, solved, acts, head_full, *out_pieces, *arrived),
        [pltpu.SemaphoreType.DMA],
        gflops=6,
        mbytes=6,
    )
    attn_other = swapped(attn_part, "tp", 1)

    middle, normed_mid_t, act_t, g_gu, g_ffn, ffn_part, mid_part, stats = call(
        functools.partial(mlp_kernel, lengths=n_len, n_fsdp=n_fsdp),
        "mlp",
        (
            sds(rows, width),
            sds(width, rows, dtype=BF16),
            sds(units, rows, dtype=BF16),
            sds(n_ctx, rows, step, dtype=BF16),
            sds(rows, width, dtype=BF16),
            sds(rows, width),
            sds(rows, width),
            sds(8, width),
        ),
        [SMEM] + [VMEM] * 5 + [ANY] * 8 + [VMEM],
        (
            meta, tokens, attn_part, attn_other, second_gain, cotangent, gu_local, gu_own,
            *[p for pair in gu_pieces for p in pair], down_full,
        ),
        [pltpu.VMEM((n_ctx, width, step), BF16), pltpu.VMEM((rows, n_ctx * step), F32), pltpu.SemaphoreType.DMA],
        gflops=10,
        mbytes=14,
    )
    mid_other = swapped(mid_part, "tp", 1)
    ffn_other = swapped(ffn_part, "tp", 1)

    down_grad = pdot(act_t, g_ffn).astype(BF16)
    down_sh = lax.psum_scatter(down_grad, "fsdp", scatter_dimension=1, tiled=True)
    quarter = sds(width, step // 2, dtype=BF16)
    gu_grads = call(
        mlp_grads_kernel,
        "mlp_grads",
        (quarter,) * 6 + (sds(2, width, step // 2, dtype=BF16),),
        [VMEM] * 2,
        (normed_mid_t, g_gu),
        gflops=3,
        mbytes=8,
    )
    mid_other, gu_grads, down_grad = lax.optimization_barrier((mid_other, gu_grads, down_grad))

    result, g_middle, out_grads, d_mixed, d_fresh, d_state, sums = call(
        functools.partial(middle_kernel, lengths=n_len),
        "middle_back",
        (
            sds(rows, width, dtype=BF16),
            sds(rows, width),
            sds(n_ctx, width, HD, dtype=BF16),
            sds(heads, rows, HD),
            sds(heads, rows, HD),
            sds(heads, HD, HD, dtype=BF16),
            sds(8, width),
        ),
        [SMEM] + [VMEM] * 13,
        (
            meta, mid_part, mid_other, ffn_part, ffn_other, middle, cotangent, second_gain, head_full, out_full, head_out, mixed, acts,
            solved,
        ),
        gflops=6,
        mbytes=12,
    )
    behind = [swapped(d_state, "ctx", j) for j in range(1, n_ctx)]

    gu_grads, _ = lax.optimization_barrier((gu_grads, d_state))
    gu_x3, gu_y3, gu_x1, gu_y2, gu_late_x, gu_late_y, gu_keep = gu_grads
    from_x3, from_y3 = swapped(gu_x3, "ctx", 1), swapped(gu_y3, "ctx", 2)
    from_x1, from_y2 = swapped(gu_x1, "ctx", 1), swapped(gu_y2, "ctx", 2)

    half = sds(width, 2 * HD, dtype=BF16)
    back = call(
        functools.partial(delta_back_kernel, lengths=n_len, sources=n_ctx - 1),
        "delta_back",
        (half,) * 8 + (sds(ext + PAD, width), sds(PAD, width), sds(heads, 16, HD)),
        [SMEM] + [VMEM] * (2 * n_ctx - 2 + 16),
        (
            meta, *behind, *arrived, pre, acts, turned, solved, fresh, state, d_mixed, d_fresh, beta, conv_full, qkv_full, beta_full,
            normed_t, normed_far, sums, out_grads,
        ),
        gflops=16,
        mbytes=16,
    )
    late_y = (gu_late_y.astype(F32) + from_x3.astype(F32)).astype(BF16)
    late_x = (gu_late_x.astype(F32) + from_y3.astype(F32)).astype(BF16)
    late_x, late_y, back = lax.optimization_barrier((late_x, late_y, back))
    a0, a1, a2, a3, b0, b1, b2, b3, in_part, beta_grad, conv_grad = back
    late_x, late_y = swapped(late_x, "ctx", 1), swapped(late_y, "ctx", 2)

    from_a3, from_b3 = swapped(a3, "ctx", 1), swapped(b3, "ctx", 2)
    from_a1, from_b2 = swapped(a1, "ctx", 1), swapped(b2, "ctx", 2)

    gu_sum = [
        (gu_keep[0].astype(F32) + from_x1.astype(F32) + late_y.astype(F32)).astype(BF16),
        (gu_keep[1].astype(F32) + from_y2.astype(F32) + late_x.astype(F32)).astype(BF16),
    ]
    gu_sum = jnp.concatenate(gu_sum, -1)
    gu_sh = lax.psum_scatter(gu_sum, "fsdp", scatter_dimension=0, tiled=True)

    late_a = (a2.astype(F32) + from_a3.astype(F32)).astype(BF16)
    late_b = (b1.astype(F32) + from_b3.astype(F32)).astype(BF16)
    late_a, late_b = swapped(late_a, "ctx", 2), swapped(late_b, "ctx", 1)
    mix_sum = [
        (a0.astype(F32) + from_a1.astype(F32) + late_a.astype(F32)).astype(BF16),
        (b0.astype(F32) + from_b2.astype(F32) + late_b.astype(F32)).astype(BF16),
    ]
    mix_sh = lax.psum_scatter(jnp.concatenate(mix_sum, -1), "fsdp", scatter_dimension=0, tiled=True)

    in_other = swapped(in_part, "tp", 1)
    rim = shifted(in_part[rows:ext] + in_other[rows:ext], "ctx", -1)
    input_grad, smalls = call(
        last_kernel,
        "input_back",
        (sds(rows, width), sds(SMALL_ROWS, width)),
        [VMEM] * 10,
        (tokens, first_gain, in_part, in_other, rim, g_middle, sums, stats, beta_grad, conv_grad),
        gflops=1,
        mbytes=6,
    )
    smalls = butterfly(smalls)
    mine = lax.dynamic_slice_in_dim(smalls[:6], fsdp * d_loc, d_loc, 1)
    first_out, second_out, beta_out = mine[0], mine[1], mine[2 : 2 + heads].T
    head_out_grad = lax.dynamic_slice_in_dim(smalls[12], fsdp * hd_loc, hd_loc)
    conv_out = smalls[13 : 13 + heads * 3 * CONV * HD // width].reshape(heads, 3, CONV, HD)
    conv_out = lax.dynamic_slice_in_dim(conv_out, fsdp * hd_loc, hd_loc, 3).transpose(1, 2, 0, 3)
    stat = jnp.sum(smalls[6:12], -1)
    rms = jnp.sqrt(stat[:5] / (stat[5] * width))

    def plane_total(value):
        half = value.shape[0] // 2
        a, b = value[:half], value[half:]
        a = (a.astype(F32) + swapped(a, "ctx", 1).astype(F32)).astype(BF16)
        b = (b.astype(F32) + swapped(b, "ctx", 2).astype(F32)).astype(BF16)
        return a, swapped(a, "ctx", 2), b, swapped(b, "ctx", 1)

    def pieces(part):
        return [part] + [swapped(part, "ctx", j) for j in range(1, n_ctx)]

    a0, a1, b0, b1 = (t.astype(F32) for t in plane_total(down_sh))
    down_out = jnp.concatenate([a0 + a1, b0 + b1])
    gu_out = call(
        gate_up_whole_kernel,
        "gate_up_whole",
        sds(2, d_loc, units),
        [SMEM] + [VMEM] * n_ctx,
        (meta, *pieces(gu_sh)),
        gflops=1,
        mbytes=6,
    )
    qkv_out, out_out = call(
        mixer_whole_kernel,
        "mixer_whole",
        (sds(3, d_loc, heads * HD), sds(heads * HD, d_loc)),
        [SMEM] + [VMEM] * n_ctx,
        (meta, *pieces(mix_sh)),
        gflops=1,
        mbytes=4,
    )
    return (
        result,
        input_grad,
        first_out,
        qkv_out,
        beta_out,
        conv_out,
        head_out_grad,
        out_out,
        second_out,
        gu_out,
        down_out,
        rms,
    )


def solution(mesh):
    return jax.shard_map(
        local,
        mesh=mesh,
        in_specs=(
            P(("fsdp", "ctx"), None),
            P("fsdp", None),
            P("fsdp"),
            P(None, "fsdp", "tp"),
            P("fsdp", "tp"),
            P(None, None, "tp", "fsdp"),
            P("fsdp"),
            P("tp", "fsdp"),
            P("fsdp"),
            P(None, "fsdp", "tp"),
            P("tp", "fsdp"),
            P(("fsdp", "ctx"), None),
        ),
        out_specs=(
            P(("fsdp", "ctx"), None),
            P(("fsdp", "ctx"), None),
            P("fsdp"),
            P(None, "fsdp", "tp"),
            P("fsdp", "tp"),
            P(None, None, "tp", "fsdp"),
            P("fsdp"),
            P("tp", "fsdp"),
            P("fsdp"),
            P(None, "fsdp", "tp"),
            P("tp", "fsdp"),
            P(),
        ),
        check_vma=False,
    )
```

```python
import functools

import jax
import jax.numpy as jnp
from jax import lax
from jax.experimental import pallas as pl
from jax.experimental.pallas import tpu as pltpu
from jax.sharding import PartitionSpec as P

HD = 128
CONV = 4
PAD = 8
EPS = 1e-06
F32 = jnp.float32
BF16 = jnp.bfloat16
NN = (((1,), (0,)), ((), ()))
NT = (((1,), (1,)), ((), ()))
TN = (((0,), (0,)), ((), ()))
SCALE = HD ** (-0.5)
COST = 3.0
US = {'delta_terms': 12, 'delta_outputs': 6.5, 'mlp': 12.2, 'mlp_grads': 6.5, 'middle_back': 9.6, 'delta_back': 22, 'input_back': 3.7, 'mixer_sum': 3.5, 'mixer_total': 2.3, 'gate_up_whole': 3.3, 'mixer_whole': 2.9}
GU_BLOCKS = 6
SMALL_ROWS = 24

ANY = pl.BlockSpec(memory_space=pl.ANY)
SMEM = pl.BlockSpec(memory_space=pltpu.SMEM)
VMEM = pl.BlockSpec(memory_space=pltpu.VMEM)


def parts_of(value, count):
    if value.dtype == BF16:
        return [value]
    pieces = []
    for left in range(count):
        piece = value.astype(BF16)
        pieces.append(piece)
        if left + 1 < count:
            value = value - piece.astype(F32)
    return pieces


def pdot(left, right, dims=NN):
    return lax.dot_general(left, right, dims, preferred_element_type=F32)


def mm_parts(lefts, rights, dims=NN):
    total = None
    for i, a in enumerate(lefts):
        for j, b in enumerate(rights):
            if i + j < max(len(lefts), len(rights)):
                term = pdot(a, b, dims)
                total = term if total is None else total + term
    return total


def mm(left, right, dims=NN, split=2):
    return mm_parts(parts_of(left, split), parts_of(right, split), dims)


def sigmoid(v):
    return 1.0 / (1.0 + jnp.exp(-v))


def iota(shape, axis):
    return lax.broadcasted_iota(jnp.int32, shape, axis)


def slots(meta, rows, axis, lengths):
    first = meta[0] * rows
    place = iota((rows, 1) if axis == 0 else (1, rows), axis) + first
    begins, end = jnp.zeros_like(place), 0
    for i in range(lengths):
        end = end + meta[2 + i]
        begins = jnp.where(end <= place, jnp.maximum(begins, end), begins)
    return begins - first, place < end


def unit_lower_inverses(lowers):
    n = lowers[0].shape[0]
    half = n // 2
    row, col = iota((half, half), 0), iota((half, half), 1)
    blocks = [low[at : at + half, at : at + half] for low in lowers for at in (0, half)]
    inverses = [jnp.where(row == col, 1.0, 0.0) - jnp.where(row // 2 == col // 2, b, 0.0) for b in blocks]
    split = [parts_of(b, 2) for b in blocks]
    zero = jnp.zeros((half, half), BF16)
    size = 2
    while size < half:
        inside = (row // (2 * size) == col // (2 * size)) & (row // size != col // size)
        pieces = [parts_of(inv, 2) for inv in inverses]
        steps = [mm_parts([jnp.where(inside, s, zero) for s in sp], pc) for sp, pc in zip(split, pieces, strict=True)]
        inverses = [inv - mm_parts(pc, parts_of(st, 2)) for inv, pc, st in zip(inverses, pieces, steps, strict=True)]
        size *= 2
    out = []
    for i, low in enumerate(lowers):
        top, bottom = inverses[2 * i], inverses[2 * i + 1]
        corner = -mm(bottom, mm(low[half:, :half], top))
        out.append((top, corner, bottom))
    return out


def conv_rows(pre, reach):
    return (pltpu.roll(pre, reach, 0) if reach else pre)[PAD:]


def conv_forward(pre, taps, age):
    total = jnp.zeros((pre.shape[0] - PAD, pre.shape[1]), F32)
    for k in range(CONV):
        reach = CONV - 1 - k
        total = total + jnp.where(age >= reach, conv_rows(pre, reach), 0.0) * taps[k : k + 1]
    return total


def pick(refs, j, *index):
    value = refs[-1][index]
    for k in range(len(refs) - 1, 0, -1):
        value = jnp.where(j == k, refs[k - 1][index], value)
    return value


def l2_ratio(values):
    return lax.rsqrt(jnp.sum(values * values, -1, keepdims=True) + EPS)


def rms_ratio(values):
    return lax.rsqrt(jnp.mean(values * values, -1, keepdims=True) + EPS)


def norm_back(values, gain, grad):
    ratio = rms_ratio(values)
    scaled = values * ratio
    weighted = grad * gain
    value_grad = ratio * (weighted - scaled * jnp.mean(weighted * scaled, -1, keepdims=True))
    return value_grad, jnp.sum(grad * scaled, 0, keepdims=True)


def terms_kernel(*refs, lengths, n_fsdp, n_blocks):
    (meta, x_ref, gain_ref, bw_ref, taps_ref, local_ref, own_ref), refs = refs[:7], refs[7:]
    pieces = [refs[j * n_blocks : (j + 1) * n_blocks] for j in range(4)]
    (w_ref, pre_ref, act_ref, tt_ref, y_ref, ms_ref, xt_ref, xh_ref, beta_ref, sem) = refs[4 * n_blocks :]
    heads = w_ref.shape[0]
    d_loc = local_ref.shape[1]
    rows = x_ref.shape[0] - PAD
    ctx, fsdp = meta[0], meta[1]

    def fill(source, head, i, shard):
        at = pl.multiple_of(shard * d_loc, d_loc)
        pltpu.make_async_copy(source, w_ref.at[head, i, pl.ds(at, d_loc), :], sem).start()

    for j, blocks in enumerate(pieces):
        head = ctx ^ j
        for i in range(3):
            if j:
                fill(local_ref.at[i, :, pl.ds(pl.multiple_of(head * HD, HD), HD)], head, i, fsdp)
            else:
                fill(own_ref.at[pl.ds(i * d_loc, d_loc), :], head, i, fsdp)
            r = 0
            for block in blocks:
                for k in range(block.shape[0]):
                    r += 1
                    fill(block.at[k, pl.ds(i * d_loc, d_loc), :], head, i, lax.rem(fsdp + n_fsdp - r, n_fsdp))

    x_wide = x_ref[...].astype(F32)
    normed = (x_wide * rms_ratio(x_wide) * gain_ref[...]).astype(BF16)
    xt_ref[...] = normed[PAD:].T
    xh_ref[...] = normed[:PAD].T
    beta = sigmoid(pdot(normed[PAD:], bw_ref[...]))
    beta_ref[...] = beta
    lb, _ = slots(meta, rows, 0, lengths)
    place = iota((rows, 1), 0)
    age = place - lb
    row, col = iota((rows, rows), 0), iota((rows, rows), 1)
    below = (col >= lb) & (col < row)
    lb_last = lb[rows - 1 :]
    last = jnp.where(place >= lb_last, 1.0, 0.0)
    keep = jnp.where(lb_last < 0, 1.0, 0.0)
    eye = jnp.where(iota((HD, HD), 0) == iota((HD, HD), 1), 1.0, 0.0)
    pltpu.make_async_copy(w_ref, w_ref, sem).wait()

    lowers, keys, scaled = [], [], []
    for h in range(heads):
        acts = []
        for i in range(3):
            pre = pdot(normed, w_ref[h, i]).astype(BF16)
            pre_ref[h, i] = pre
            total = conv_forward(pre.astype(F32), taps_ref[h, i], age)
            act = total * sigmoid(total)
            if i < 2:
                act = act * l2_ratio(act)
            acts.append(act.astype(BF16))
            act_ref[h, i] = acts[i]
        key, value = acts[1], acts[2]
        beta_h = beta[:, h : h + 1]
        lowers.append(jnp.where(below, beta_h * pdot(key, key, NT), 0.0))
        keys.append(key)
        scaled.append(beta_h * jnp.concatenate([key, value], -1).astype(F32))
    half = rows // 2
    for h, (top, corner, bottom) in enumerate(unit_lower_inverses(lowers)):
        tt_ref[h, :half, :half] = top.T
        tt_ref[h, :half, half:] = corner.T
        tt_ref[h, half:, :half] = jnp.zeros((half, half), F32)
        tt_ref[h, half:, half:] = bottom.T
        upper = mm(top, scaled[h][:half])
        lower = mm(jnp.concatenate([corner, bottom], -1), scaled[h])
        solved = jnp.concatenate([upper, lower])
        y_ref[h] = solved
        ms_ref[h, 0] = (keep * (eye - mm(solved[:, :HD], keys[h], TN))).astype(BF16)
        ms_ref[h, 1] = mm(last * solved[:, HD:], keys[h], TN).astype(BF16)


def output_kernel(*refs, lengths, sources, n_fsdp):
    (meta, y_ref, act_ref, gain_ref, local_ref, own_ref, o0, o1, o2, o3), refs = refs[:10], refs[10:]
    arrived, (ow_ref, mixed_ref, r_ref, s_ref, n_ref, attn_ref, sem) = refs[:sources], refs[sources:]
    heads, rows = y_ref.shape[:2]
    ctx = meta[0]
    fsdp = meta[1]
    d_loc = own_ref.shape[0]

    def fill(source, head, shard):
        at = pl.multiple_of(shard * d_loc, d_loc)
        pltpu.make_async_copy(source, ow_ref.at[head, pl.ds(at, d_loc), :], sem).start()

    for j, piece in enumerate((o0, o1, o2, o3)):
        head = ctx ^ j
        fill(local_ref.at[:, pl.ds(pl.multiple_of(head * HD, HD), HD)] if j else own_ref, head, fsdp)
        for r in range(1, n_fsdp):
            fill(piece.at[r - 1], head, lax.rem(fsdp + n_fsdp - r, n_fsdp))
    lb, _ = slots(meta, rows, 0, lengths)
    row, col = iota((rows, rows), 0), iota((rows, rows), 1)
    upto = (col >= lb) & (col <= row)
    carried = jnp.where(lb < 0, 1.0, 0.0)
    normed = []
    for h in range(heads):
        state = jnp.zeros((HD, HD), F32)
        for c in range(sources):
            after = pick(arrived, ctx ^ c, h, 1).astype(F32)
            if c:
                after = after + mm(state, pick(arrived, ctx ^ c, h, 0))
            state = jnp.where(c < ctx, after, state)
        query, key = act_ref[h, 0], act_ref[h, 1]
        w_part, u_part = y_ref[h, :, :HD], y_ref[h, :, HD:]
        scores = jnp.where(upto, pdot(query, key, NT) * SCALE, 0.0)
        fresh = u_part - carried * mm(w_part, state, NT)
        mixed = carried * (SCALE * mm(query, state, NT)) + mm(scores, fresh)
        mixed_ref[h] = mixed
        r_ref[h] = fresh
        s_ref[h] = state
        out = (mixed * rms_ratio(mixed) * gain_ref[...]).astype(BF16)
        n_ref[:, h * HD : (h + 1) * HD] = out
        normed.append(out)
    pltpu.make_async_copy(ow_ref, ow_ref, sem).wait()
    total = pdot(normed[0], ow_ref[0], NT)
    for h in range(1, heads):
        total = total + pdot(normed[h], ow_ref[h], NT)
    attn_ref[...] = total


def mlp_kernel(*refs, lengths, n_fsdp):
    (meta, x_ref, attn_ref, other_ref, gain_ref, cot_ref, local_ref, own_ref, f1, f2, a3, b3, down_ref,
     mid_ref, nt_ref, at_ref, g_ref, gf_ref, part_ref, st_ref, w, gu, sem) = refs
    rows, width = x_ref.shape
    units = down_ref.shape[0]
    d_loc = local_ref.shape[0]
    step = GU_BLOCKS * HD
    half = step // 2
    quarters = w.shape[0]
    ctx, fsdp = meta[0], meta[1]

    def fill(source, quarter, shard, at, size):
        start = pl.multiple_of(shard * d_loc, d_loc)
        pltpu.make_async_copy(source, w.at[quarter, pl.ds(start, d_loc), pl.ds(at, size)], sem).start()

    for f in range(n_fsdp):
        fill(own_ref.at[f], ctx, f, 0, step)
    for j in range(1, 4):
        quarter = ctx ^ j
        fill(local_ref.at[:, pl.ds(pl.multiple_of(quarter * step, HD), step)], quarter, fsdp, 0, step)
        for r in range(1, n_fsdp):
            shard = lax.rem(fsdp + n_fsdp - r, n_fsdp)
            if j < 3:
                fill((f1, f2)[j - 1].at[r - 1], quarter, shard, 0, step)
            else:
                fill(a3.at[r - 1], quarter, shard, 0, half)
                fill(b3.at[r - 1], quarter, shard, half, half)

    _, inside = slots(meta, rows, 0, lengths)
    valid = jnp.where(inside, 1.0, 0.0)
    x_wide = x_ref[...].astype(F32)
    attn = (attn_ref[...] + other_ref[...]) * valid
    middle = x_wide + attn
    mid_ref[...] = middle
    for i, v in enumerate((x_wide, attn, middle)):
        st_ref[i : i + 1] = jnp.sum(valid * v * v, 0, keepdims=True)
    normed = (middle * rms_ratio(middle) * gain_ref[...]).astype(BF16)
    nt_ref[...] = normed.T
    g_ffn = (cot_ref[...].astype(F32) * valid).astype(BF16)
    gf_ref[...] = g_ffn
    g_act = pdot(g_ffn, down_ref[...], NT)
    pltpu.make_async_copy(w, w, sem).wait()
    for q in range(quarters):
        gu[:, q * step : (q + 1) * step] = pdot(normed, w[q])
    gate, up = gu[:, :units], gu[:, units : 2 * units]
    sig = sigmoid(gate)
    act = (gate * sig * up).astype(BF16)
    at_ref[...] = act.T
    g_up = g_act * gate * sig
    g_gate = g_act * up * sig * (1.0 + gate * (1.0 - sig))
    gu[:, :units] = g_gate
    gu[:, units : 2 * units] = g_up
    part = None
    for q in range(quarters):
        real = min(step, 2 * units - q * step)
        grad = gu[:, q * step : q * step + real].astype(BF16)
        if real < step:
            grad = jnp.concatenate([grad, jnp.zeros((rows, step - real), BF16)], -1)
        g_ref[ctx ^ q] = grad
        term = pdot(grad, w[q], NT)
        part = term if part is None else part + term
    part_ref[:rows] = part
    part_ref[rows:] = pdot(act, down_ref[...])


def mlp_grads_kernel(nt_ref, g_ref, at_ref, gf_ref, x_ref, y_ref, late_x_ref, late_y_ref, own_ref, down_ref):
    half = g_ref.shape[2] // 2
    nt = nt_ref[...]

    def put(ref, j, side):
        ref[...] = pdot(nt, g_ref[j, :, side * half : (side + 1) * half]).astype(BF16)

    put(x_ref.at[0], 3, 0)
    put(y_ref.at[0], 3, 1)
    put(x_ref.at[1], 1, 0)
    put(y_ref.at[1], 2, 1)
    put(late_x_ref, 1, 1)
    put(late_y_ref, 2, 0)
    put(own_ref.at[0], 0, 0)
    put(own_ref.at[1], 0, 1)
    down_ref[...] = pdot(at_ref[...], gf_ref[...]).astype(BF16)


def middle_kernel(
    meta, part_ref, other_ref, mid_ref, cot_ref, gain_ref, hgain_ref, ow_ref, n_ref, mixed_ref, act_ref, y_ref,
    out_ref, gm_ref, og_ref, do_ref, dr_ref, ds_ref, sm_ref, *, lengths
):
    heads, rows = mixed_ref.shape[:2]
    ctx = meta[0]
    lb, inside = slots(meta, rows, 0, lengths)
    lb_row, _ = slots(meta, rows, 1, lengths)
    valid = jnp.where(inside, 1.0, 0.0)
    row, col = iota((rows, rows), 0), iota((rows, rows), 1)
    upto = (row >= lb_row) & (row <= col)
    carried = jnp.where(lb < 0, 1.0, 0.0)
    middle = mid_ref[...]
    value_grad, gain_grad = norm_back(middle, gain_ref[...], part_ref[:rows] + other_ref[:rows])
    g_middle = cot_ref[...].astype(F32) + value_grad
    gm_ref[...] = g_middle
    g_attn = (g_middle * valid).astype(BF16)
    turned_grad = g_attn.T
    total = jnp.zeros((1, HD), F32)
    for h in range(heads):
        key = act_ref[h, 1]
        g_head = pdot(g_attn, ow_ref[h])
        d_mixed, part = norm_back(mixed_ref[h], hgain_ref[...], g_head)
        total = total + part
        turned = jnp.where(upto, pdot(key, act_ref[h, 0], NT) * SCALE, 0.0)
        d_fresh = mm(turned, d_mixed)
        do_ref[h] = d_mixed
        dr_ref[h] = d_fresh
        d_state = SCALE * mm(carried * d_mixed, act_ref[h, 0], TN) - mm(carried * d_fresh, y_ref[h, :, :HD], TN)
        ds_ref[h] = d_state.astype(BF16)
        og_ref[ctx ^ h] = pdot(turned_grad, n_ref[:, h * HD : (h + 1) * HD]).astype(BF16)
    ffn = (part_ref[rows:] + other_ref[rows:]) * valid
    result = middle + ffn
    out_ref[...] = result.astype(BF16)
    sm_ref[...] = jnp.zeros_like(sm_ref)
    sm_ref[0:1] = gain_grad
    sm_ref[1:2, :HD] = total
    sm_ref[2:3] = jnp.sum(valid * ffn * ffn, 0, keepdims=True)
    sm_ref[3:4] = jnp.sum(valid * result * result, 0, keepdims=True)
    sm_ref[4:5] = jnp.broadcast_to(jnp.sum(valid, 0, keepdims=True), gain_grad.shape) / gain_grad.shape[1]


def delta_back_kernel(*refs, lengths, sources):
    meta, grads, maps = refs[0], refs[1 : 1 + sources], refs[1 + sources : 1 + 2 * sources]
    (pre_ref, act_ref, tt_ref, y_ref, r_ref, s_ref, do_ref, dr_ref, beta_ref, taps_ref, w_ref, bw_ref, xt_ref, xh_ref, sm_ref, og_ref,
     keep_ref, x_ref, y2_ref, late_x_ref, late_y_ref, part_ref, bg_ref, cg_ref) = refs[1 + 2 * sources :]
    heads, rows = r_ref.shape[:2]
    width = w_ref.shape[2]
    ext = rows + PAD
    ctx = meta[0]
    lb, _ = slots(meta, rows, 0, lengths)
    lb_row, _ = slots(meta, rows, 1, lengths)
    place = iota((rows, 1), 0)
    age = place - lb
    row, col = iota((rows, rows), 0), iota((rows, rows), 1)
    last = jnp.where(place >= lb[rows - 1 :], 1.0, 0.0)
    carried = jnp.where(lb < 0, 1.0, 0.0)
    upto = (col >= lb) & (col <= row)
    below = (col >= lb) & (col < row)
    turned_upto = (row >= lb_row) & (row <= col)
    lane = iota((rows, HD), 1)
    logits = jnp.zeros((rows, HD), F32)
    top = jnp.zeros((PAD, HD), F32)
    xt, xh = xt_ref[...], xh_ref[...]
    part = jnp.zeros((rows, width), F32)
    ahead = jnp.zeros((PAD, width), F32)
    for h in range(heads):
        d_state = jnp.zeros((HD, HD), F32)
        for c in range(sources, 0, -1):
            before = pick(grads, ctx ^ c, h).astype(F32)
            if c < sources:
                before = before + mm(d_state, pick(maps, ctx ^ c, h, 0), NT)
            d_state = jnp.where(c > ctx, before, d_state)
        query, key, value = act_ref[h, 0], act_ref[h, 1], act_ref[h, 2]
        solved = y_ref[h]
        fresh, state, d_mixed = r_ref[h], s_ref[h], do_ref[h]
        beta = beta_ref[:, h : h + 1]
        d_fresh = dr_ref[h] + last * mm(key, d_state, NT)
        d_scores = jnp.where(upto, SCALE * mm(d_mixed, fresh, NT), 0.0)
        turned = jnp.where(turned_upto, SCALE * mm(fresh, d_mixed, NT), 0.0)
        d_query = mm(d_scores, key) + carried * (SCALE * mm(d_mixed, state))
        d_key = mm(turned, query) + mm(last * fresh, d_state)
        d_solved = jnp.concatenate([-carried * mm(d_fresh, state), d_fresh], -1)
        d_scaled = mm(tt_ref[h], d_solved)
        d_value = beta * d_scaled[:, HD:]
        d_key = d_key + beta * d_scaled[:, :HD]
        d_beta = jnp.sum(d_scaled[:, :HD] * key.astype(F32) + d_scaled[:, HD:] * value.astype(F32), -1, keepdims=True)
        d_lower = jnp.where(below, -mm(d_scaled, solved, NT), 0.0)
        d_beta = d_beta + jnp.sum(d_lower * pdot(key, key, NT), -1, keepdims=True)
        d_gram = beta * d_lower
        d_key = d_key + mm(d_gram, key) + mm(d_gram, key, TN)
        logits = jnp.where(lane == h, d_beta * beta * (1.0 - beta), logits)
        g_main, g_head = [], []
        for i, grad in enumerate((d_query, d_key, d_value)):
            taps = taps_ref[h, i]
            pre = pre_ref[h, i].astype(F32)
            total = conv_forward(pre, taps, age)
            sig = sigmoid(total)
            if i < 2:
                act = total * sig
                ratio = l2_ratio(act)
                unit = act * ratio
                grad = ratio * (grad - unit * jnp.sum(grad * unit, -1, keepdims=True))
            grad = grad * sig * (1.0 + total * (1.0 - sig))
            back = jnp.zeros((ext, HD), F32)
            for k in range(CONV):
                reach = CONV - 1 - k
                grad_k = jnp.where(age >= reach, grad, 0.0)
                cg_ref[h, i * CONV + k : i * CONV + k + 1, :] = jnp.sum(grad_k * conv_rows(pre, reach), 0, keepdims=True)
                padded = jnp.concatenate([top, grad_k])
                back = back + (pltpu.roll(padded, ext - reach, 0) if reach else padded) * taps[k : k + 1]
            g_main.append(back[PAD:].astype(BF16))
            g_head.append(back[:PAD].astype(BF16))
            part = part + pdot(g_main[i], w_ref[h, i], NT)
            ahead = ahead + pdot(g_head[i], w_ref[h, i], NT)
        piece = pdot(xt, jnp.concatenate(g_main, -1)) + pdot(xh, jnp.concatenate(g_head, -1))
        piece = piece.astype(BF16)
        places = (
            (keep_ref.at[0], keep_ref.at[1]),
            (x_ref.at[1], late_x_ref),
            (late_y_ref, y2_ref.at[1]),
            (x_ref.at[0], y2_ref.at[0]),
        )
        for j, (a, b) in enumerate(places):

            @pl.when(ctx ^ j == h)
            def _(a=a, b=b, j=j, piece=piece):
                a[...] = piece[:, : 2 * HD]
                b[:, :HD] = piece[:, 2 * HD :]
                b[:, HD:] = og_ref[j]

    logits = logits.astype(BF16)
    part_ref[:rows] = part + pdot(logits, bw_ref[...], NT)
    part_ref[rows:ext] = ahead
    part_ref[ext:] = jnp.zeros((PAD, width), F32)
    part_ref[ext : ext + 1, :HD] = sm_ref[1:2, :HD]
    bg_ref[...] = lax.dot_general(logits, xt, (((0,), (1,)), ((), ())), preferred_element_type=F32)[:PAD]


def last_kernel(x_ref, gain_ref, part_ref, other_ref, rim_ref, rim2_ref, gm_ref, sm_ref, st_ref, bg_ref, cg_ref, grad_ref, small_ref):
    rows, width = x_ref.shape
    heads = cg_ref.shape[0]
    total = part_ref[...] + other_ref[...]
    grad = jnp.concatenate([total[: rows - PAD], total[rows - PAD : rows] + (rim_ref[...] + rim2_ref[...])])
    value_grad, gain_grad = norm_back(x_ref[...].astype(F32), gain_ref[...], grad)
    grad_ref[...] = gm_ref[...] + value_grad
    small_ref[...] = jnp.zeros_like(small_ref)
    small_ref[0:1] = gain_grad
    small_ref[1:2] = sm_ref[0:1]
    small_ref[2 : 2 + heads] = bg_ref[:heads]
    small_ref[6:9] = st_ref[0:3]
    small_ref[9:11] = sm_ref[2:4]
    small_ref[11:12] = sm_ref[4:5]
    small_ref[12:13, :HD] = total[rows + PAD : rows + PAD + 1, :HD]
    per = width // HD
    for h in range(heads):
        for k in range(3 * CONV):
            at = h * 3 * CONV + k
            small_ref[13 + at // per : 14 + at // per, (at % per) * HD : (at % per + 1) * HD] = cg_ref[h, k : k + 1]


def gate_up_whole_kernel(meta, a0, b0, a1, b1, a2, b2, a3, b3, gu_ref):
    ctx = meta[0]
    units = gu_ref.shape[2]
    side = GU_BLOCKS // 2
    for q in range(4):
        for j, pair in enumerate(((a0, b0), (a1, b1), (a2, b2), (a3, b3))):

            @pl.when(ctx ^ j == q)
            def _(pair=pair, q=q):
                for k in range(GU_BLOCKS):
                    at = (q * GU_BLOCKS + k) * HD
                    if at < 2 * units:
                        block = pair[k // side][:, k % side * HD : (k % side + 1) * HD]
                        gu_ref[at // units, :, at % units : at % units + HD] = block.astype(F32)


def mixer_whole_kernel(meta, p0, p1, p2, p3, qkv_ref, out_ref):
    ctx = meta[0]
    for q in range(4):
        for j, ref in enumerate((p0, p1, p2, p3)):

            @pl.when(ctx ^ j == q)
            def _(ref=ref, q=q):
                for i in range(3):
                    qkv_ref[i, :, q * HD : (q + 1) * HD] = ref[:, i * HD : (i + 1) * HD].astype(F32)
                out_ref[q * HD : (q + 1) * HD, :] = ref[:, 3 * HD :].T.astype(F32)


def sds(*shape, dtype=F32):
    return jax.ShapeDtypeStruct(shape, dtype)


def call(body, name, out_shape, in_specs, args, scratch=(), gflops=1, mbytes=4):
    return pl.pallas_call(
        body,
        name=name,
        in_specs=in_specs,
        out_specs=jax.tree.map(lambda _: VMEM, out_shape),
        out_shape=out_shape,
        scratch_shapes=list(scratch),
        compiler_params=pltpu.CompilerParams(vmem_limit_bytes=56 * 1024 * 1024),
        cost_estimate=pl.CostEstimate(flops=int(COST * US[name] * 1_150_000_000), bytes_accessed=10**6, transcendentals=0),
    )(*args)


def shifted(value, axis, steps):
    count = lax.axis_size(axis)
    first, end = max(0, -steps), min(count, count - steps)
    return lax.ppermute(value, axis, [(s, s + steps) for s in range(first, end)])


def swapped(value, axis, mask):
    return lax.ppermute(value, axis, [(s, s ^ mask) for s in range(lax.axis_size(axis))])


def far_shards(value):
    count, here = lax.axis_size("fsdp"), lax.axis_index("fsdp")
    if count <= 4:
        turns = [[(s, (s + r) % count) for s in range(count)] for r in range(1, count)]
        return [lax.ppermute(value, "fsdp", turn)[None] for turn in turns]
    return [others(lax.all_gather(value, "fsdp", axis=0))]


def others(value):
    return jnp.concatenate([other(value, r) for r in range(1, lax.axis_size("fsdp"))])


def other(value, r):
    count, here = lax.axis_size("fsdp"), lax.axis_index("fsdp")
    return lax.dynamic_index_in_dim(value, (here + count - r) % count, 0)


def scatter_sum(halves):
    count, here = lax.axis_size("fsdp"), lax.axis_index("fsdp")
    if count > 4:
        return lax.psum_scatter(jnp.concatenate(halves, -1), "fsdp", scatter_dimension=0, tiled=True)
    value = jnp.concatenate(halves, -1)
    rows = value.shape[0] // count
    total = lax.dynamic_slice_in_dim(value, here * rows, rows, 0).astype(F32)
    for r in range(1, count):
        part = lax.dynamic_slice_in_dim(value, (here + r) % count * rows, rows, 0)
        total = total + lax.ppermute(part, "fsdp", [(s, (s + r) % count) for s in range(count)]).astype(F32)
    return total.astype(BF16)


def plane_gather(a, b):
    a1, b2 = swapped(a, "ctx", 1), swapped(b, "ctx", 2)
    b1, a2 = swapped(b, "ctx", 1), swapped(a, "ctx", 2)
    return [(a1, b1), (a2, b2), (swapped(a1, "ctx", 2), swapped(b2, "ctx", 1))]


def in_order(pieces):
    here = lax.axis_index("ctx")
    stacked = jnp.stack(pieces)
    return [lax.dynamic_index_in_dim(stacked, here ^ k, 0, False) for k in range(len(pieces))]


def plane_sum(pieces):
    return (pieces[0].astype(F32) + pieces[1].astype(F32)) + (pieces[2].astype(F32) + pieces[3].astype(F32))


def butterfly(value):
    for axis in ("ctx", "fsdp"):
        mask = 1
        while mask < lax.axis_size(axis):
            value = value + swapped(value, axis, mask)
            mask *= 2
    return value


def local(
    tokens, lengths, norm_gain, qkv_weight, beta_weight, conv_weight, head_gain, out_weight, mlp_gain, gate_up_weight, down_weight, cotangent
):
    rows, width = tokens.shape
    n_ctx, n_fsdp = lax.axis_size("ctx"), lax.axis_size("fsdp")
    ctx, fsdp = lax.axis_index("ctx"), lax.axis_index("fsdp")
    d_loc = qkv_weight.shape[1]
    heads = beta_weight.shape[1]
    units = down_weight.shape[0]
    hd_loc = head_gain.shape[0]
    n_len = lengths.shape[1]
    step = GU_BLOCKS * HD
    ext = rows + PAD
    meta = jnp.concatenate([jnp.stack([ctx, fsdp]).astype(jnp.int32), lengths[0]])

    small = jnp.concatenate([norm_gain, mlp_gain, head_gain, beta_weight.reshape(-1), conv_weight.reshape(-1)])
    small_rows = -(-small.shape[0] // (HD * 16)) * 16
    small = jnp.pad(small, (0, small_rows * HD - small.shape[0])).reshape(small_rows, HD)
    qkv_part = lax.dynamic_slice_in_dim(qkv_weight, ctx * HD, HD, 2).reshape(3 * d_loc, HD)
    out_part = lax.dynamic_slice_in_dim(out_weight, ctx * HD, HD, 0).T
    pack = jnp.concatenate([qkv_part, small])
    packs = lax.all_gather(pack, "fsdp", axis=0)
    pack_far = [others(packs)] if n_fsdp > 4 else [other(packs, r) for r in range(1, n_fsdp)]
    out_local = out_weight.T
    out_part, gate_up_weight, _ = lax.optimization_barrier((out_part, gate_up_weight, packs))
    out_far = far_shards(out_part)
    gu_local = jnp.concatenate(
        [gate_up_weight[0], gate_up_weight[1], jnp.zeros((d_loc, n_ctx * step - 2 * units), BF16)], -1
    )
    gu_own = lax.all_gather(lax.dynamic_slice_in_dim(gu_local, ctx * step, step, 1), "fsdp", axis=0)
    down_full = lax.all_gather(down_weight, "fsdp", axis=1, tiled=True)
    x_ext = jnp.concatenate([shifted(tokens[rows - PAD :], "ctx", 1), tokens])

    one = [swapped(p, "ctx", 1) for p in pack_far]
    two = [swapped(p, "ctx", 2) for p in pack_far]
    three = [swapped(two[k], "ctx", 1) if k % 2 else swapped(one[k], "ctx", 2) for k in range(len(pack_far))]
    out_far = jnp.concatenate(out_far)
    out_pieces = [out_far] + [swapped(out_far, "ctx", j) for j in range(1, n_ctx)]

    flat = packs[:, 3 * d_loc :].reshape(n_fsdp, -1)
    at = 0
    first_gain = flat[:, at : at + d_loc].reshape(1, width).astype(F32)
    at += d_loc
    second_gain = flat[:, at : at + d_loc].reshape(1, width).astype(F32)
    at += d_loc
    head_full = flat[:, at : at + hd_loc].reshape(1, HD).astype(F32)
    at += hd_loc
    beta_full = jnp.pad(flat[:, at : at + d_loc * heads].reshape(width, heads), ((0, 0), (0, HD - heads)))
    at += d_loc * heads
    conv_full = flat[:, at : at + 3 * CONV * heads * hd_loc].reshape(n_fsdp, 3, CONV, heads, hd_loc)
    conv_full = conv_full.transpose(3, 1, 2, 0, 4).reshape(heads, 3, CONV, HD).astype(F32)

    qkv_full, pre, acts, turned, solved, ends_map, normed_t, normed_far, beta = call(
        functools.partial(terms_kernel, lengths=n_len, n_fsdp=n_fsdp, n_blocks=len(pack_far)),
        "delta_terms",
        (
            sds(heads, 3, width, HD, dtype=BF16),
            sds(heads, 3, ext, HD, dtype=BF16),
            sds(heads, 3, rows, HD, dtype=BF16),
            sds(heads, rows, rows),
            sds(heads, rows, 2 * HD),
            sds(heads, 2, HD, HD, dtype=BF16),
            sds(width, rows, dtype=BF16),
            sds(width, PAD, dtype=BF16),
            sds(rows, HD),
        ),
        [SMEM] + [VMEM] * 4 + [ANY] * (2 + 4 * len(pack_far)),
        (meta, x_ext, first_gain, beta_full, conv_full, qkv_weight, pack, *pack_far, *one, *two, *three),
        [pltpu.SemaphoreType.DMA],
        gflops=15,
        mbytes=8,
    )
    arrived = [swapped(ends_map, "ctx", j) for j in range(1, n_ctx)]
    gu_far, _ = lax.optimization_barrier((others(gu_own), ends_map))
    gu_one, gu_two = swapped(gu_far, "ctx", 1), swapped(gu_far, "ctx", 2)
    gu_three = (swapped(gu_one[:, :, : step // 2], "ctx", 2), swapped(gu_two[:, :, step // 2 :], "ctx", 1))
    out_full, mixed, fresh, state, head_out, attn_part = call(
        functools.partial(output_kernel, lengths=n_len, sources=n_ctx - 1, n_fsdp=n_fsdp),
        "delta_outputs",
        (
            sds(heads, width, HD, dtype=BF16),
            sds(heads, rows, HD),
            sds(heads, rows, HD),
            sds(heads, HD, HD),
            sds(rows, heads * HD, dtype=BF16),
            sds(rows, width),
        ),
        [SMEM] + [VMEM] * 3 + [ANY] * (2 + n_ctx) + [VMEM] * len(arrived),
        (meta, solved, acts, head_full, out_local, out_part, *out_pieces, *arrived),
        [pltpu.SemaphoreType.DMA],
        gflops=6,
        mbytes=6,
    )
    attn_other = swapped(attn_part, "tp", 1)

    middle, normed_mid_t, act_t, g_gu, g_ffn, mlp_part, stats = call(
        functools.partial(mlp_kernel, lengths=n_len, n_fsdp=n_fsdp),
        "mlp",
        (
            sds(rows, width),
            sds(width, rows, dtype=BF16),
            sds(units, rows, dtype=BF16),
            sds(n_ctx, rows, step, dtype=BF16),
            sds(rows, width, dtype=BF16),
            sds(2 * rows, width),
            sds(8, width),
        ),
        [SMEM] + [VMEM] * 5 + [ANY] * 6 + [VMEM],
        (
            meta, tokens, attn_part, attn_other, second_gain, cotangent, gu_local, gu_own, gu_one, gu_two, *gu_three, down_full,
        ),
        [pltpu.VMEM((n_ctx, width, step), BF16), pltpu.VMEM((rows, n_ctx * step), F32), pltpu.SemaphoreType.DMA],
        gflops=10,
        mbytes=14,
    )
    mlp_other = swapped(mlp_part, "tp", 1)

    result, g_middle, out_grads, d_mixed, d_fresh, d_state, sums = call(
        functools.partial(middle_kernel, lengths=n_len),
        "middle_back",
        (
            sds(rows, width, dtype=BF16),
            sds(rows, width),
            sds(n_ctx, width, HD, dtype=BF16),
            sds(heads, rows, HD),
            sds(heads, rows, HD),
            sds(heads, HD, HD, dtype=BF16),
            sds(8, width),
        ),
        [SMEM] + [VMEM] * 11,
        (
            meta, mlp_part, mlp_other, middle, cotangent, second_gain, head_full, out_full, head_out, mixed, acts,
            solved,
        ),
        gflops=6,
        mbytes=12,
    )
    behind = [swapped(d_state, "ctx", j) for j in range(1, n_ctx)]

    normed_mid_t, g_gu, g_ffn, _ = lax.optimization_barrier((normed_mid_t, g_gu, g_ffn, d_state))
    quarter = sds(width, step // 2, dtype=BF16)
    double = sds(2, width, step // 2, dtype=BF16)
    gu_x, gu_y, gu_late_x, gu_late_y, gu_keep, down_grad = call(
        mlp_grads_kernel,
        "mlp_grads",
        (double, double, quarter, quarter, double, sds(units, width, dtype=BF16)),
        [VMEM] * 4,
        (normed_mid_t, g_gu, act_t, g_ffn),
        gflops=4,
        mbytes=12,
    )
    down_sh = lax.psum_scatter(down_grad, "fsdp", scatter_dimension=1, tiled=True)
    behind, gu_x, gu_y = lax.optimization_barrier((behind, gu_x, gu_y))
    from_x, from_y = swapped(gu_x, "ctx", 1), swapped(gu_y, "ctx", 2)

    half = sds(width, 2 * HD, dtype=BF16)
    double = sds(2, width, 2 * HD, dtype=BF16)
    back = call(
        functools.partial(delta_back_kernel, lengths=n_len, sources=n_ctx - 1),
        "delta_back",
        (double, double, double, half, half, sds(ext + PAD, width), sds(PAD, width), sds(heads, 16, HD)),
        [SMEM] + [VMEM] * (2 * n_ctx - 2 + 16),
        (
            meta, *behind, *arrived, pre, acts, turned, solved, fresh, state, d_mixed, d_fresh, beta, conv_full, qkv_full, beta_full,
            normed_t, normed_far, sums, out_grads,
        ),
        gflops=16,
        mbytes=16,
    )

    def add(left, right):
        return (left.astype(F32) + right.astype(F32)).astype(BF16)

    from_x, from_y, back = lax.optimization_barrier((from_x, from_y, back))
    mix_keep, mix_x, mix_y, mix_late_x, mix_late_y, in_part, beta_grad, conv_grad = back
    gu_late_y, gu_late_x = add(gu_late_y, from_x[0]), add(gu_late_x, from_y[0])
    rim = shifted(in_part[rows:ext], "ctx", -1)
    gu_late_y, gu_late_x, mix_x, mix_y = lax.optimization_barrier((gu_late_y, gu_late_x, mix_x, mix_y))
    gu_late_y, gu_late_x = swapped(gu_late_y, "ctx", 2), swapped(gu_late_x, "ctx", 1)
    mix_from_x, mix_from_y = swapped(mix_x, "ctx", 1), swapped(mix_y, "ctx", 2)
    in_other = swapped(in_part, "tp", 1)
    gu_sum = [
        (gu_keep[0].astype(F32) + from_x[1].astype(F32) + gu_late_y.astype(F32)).astype(BF16),
        (gu_keep[1].astype(F32) + from_y[1].astype(F32) + gu_late_x.astype(F32)).astype(BF16),
    ]
    gu_sh = lax.psum_scatter(jnp.concatenate(gu_sum, -1), "fsdp", scatter_dimension=0, tiled=True)

    mix_late_y, mix_late_x = add(mix_late_y, mix_from_x[0]), add(mix_late_x, mix_from_y[0])
    mix_late_y, mix_late_x, down_sh = lax.optimization_barrier((mix_late_y, mix_late_x, down_sh))
    mix_late_y, mix_late_x = swapped(mix_late_y, "ctx", 2), swapped(mix_late_x, "ctx", 1)
    side = units // 2
    down_a, down_b = down_sh[:side], down_sh[side:]
    down_a, down_b = add(down_a, swapped(down_a, "ctx", 1)), add(down_b, swapped(down_b, "ctx", 2))
    mix_sum = [
        (mix_keep[0].astype(F32) + mix_from_x[1].astype(F32) + mix_late_y.astype(F32)).astype(BF16),
        (mix_keep[1].astype(F32) + mix_from_y[1].astype(F32) + mix_late_x.astype(F32)).astype(BF16),
    ]
    rim_other = swapped(rim, "tp", 1)
    mix_sum, down_a, down_b, rim, rim_other = lax.optimization_barrier((mix_sum, down_a, down_b, rim, rim_other))
    mix_sh = scatter_sum(mix_sum)
    down_out = jnp.concatenate(
        [
            down_a.astype(F32) + swapped(down_a, "ctx", 2).astype(F32),
            down_b.astype(F32) + swapped(down_b, "ctx", 1).astype(F32),
        ]
    )

    input_grad, smalls = call(
        last_kernel,
        "input_back",
        (sds(rows, width), sds(SMALL_ROWS, width)),
        [VMEM] * 11,
        (tokens, first_gain, in_part, in_other, rim, rim_other, g_middle, sums, stats, beta_grad, conv_grad),
        gflops=1,
        mbytes=6,
    )
    smalls = butterfly(smalls)
    mine = lax.dynamic_slice_in_dim(smalls[:6], fsdp * d_loc, d_loc, 1)
    first_out, second_out, beta_out = mine[0], mine[1], mine[2 : 2 + heads].T
    head_out_grad = lax.dynamic_slice_in_dim(smalls[12], fsdp * hd_loc, hd_loc)
    conv_out = smalls[13 : 13 + heads * 3 * CONV * HD // width].reshape(heads, 3, CONV, HD)
    conv_out = lax.dynamic_slice_in_dim(conv_out, fsdp * hd_loc, hd_loc, 3).transpose(1, 2, 0, 3)
    stat = jnp.sum(smalls[6:12], -1)
    rms = jnp.sqrt(stat[:5] / (stat[5] * width))

    def pieces(part):
        return [part] + [swapped(part, "ctx", j) for j in range(1, n_ctx)]

    gu_pairs = plane_gather(gu_sh[:, : step // 2], gu_sh[:, step // 2 :])
    gu_out = call(
        gate_up_whole_kernel,
        "gate_up_whole",
        sds(2, d_loc, units),
        [SMEM] + [VMEM] * (2 * n_ctx),
        (meta, gu_sh[:, : step // 2], gu_sh[:, step // 2 :], *[p for pair in gu_pairs for p in pair]),
        gflops=1,
        mbytes=6,
    )
    qkv_out, out_out = call(
        mixer_whole_kernel,
        "mixer_whole",
        (sds(3, d_loc, heads * HD), sds(heads * HD, d_loc)),
        [SMEM] + [VMEM] * n_ctx,
        (meta, *pieces(mix_sh)),
        gflops=1,
        mbytes=4,
    )
    return (
        result,
        input_grad,
        first_out,
        qkv_out,
        beta_out,
        conv_out,
        head_out_grad,
        out_out,
        second_out,
        gu_out,
        down_out,
        rms,
    )


def solution(mesh):
    return jax.shard_map(
        local,
        mesh=mesh,
        in_specs=(
            P(("fsdp", "ctx"), None),
            P("fsdp", None),
            P("fsdp"),
            P(None, "fsdp", "tp"),
            P("fsdp", "tp"),
            P(None, None, "tp", "fsdp"),
            P("fsdp"),
            P("tp", "fsdp"),
            P("fsdp"),
            P(None, "fsdp", "tp"),
            P("tp", "fsdp"),
            P(("fsdp", "ctx"), None),
        ),
        out_specs=(
            P(("fsdp", "ctx"), None),
            P(("fsdp", "ctx"), None),
            P("fsdp"),
            P(None, "fsdp", "tp"),
            P("fsdp", "tp"),
            P(None, None, "tp", "fsdp"),
            P("fsdp"),
            P("tp", "fsdp"),
            P("fsdp"),
            P(None, "fsdp", "tp"),
            P("tp", "fsdp"),
            P(),
        ),
        check_vma=False,
    )
```

```python
import functools

import jax
import jax.numpy as jnp
from jax import lax
from jax.experimental import pallas as pl
from jax.experimental.pallas import tpu as pltpu
from jax.sharding import PartitionSpec as P

HD = 128
CONV = 4
PAD = 8
EPS = 1e-06
F32 = jnp.float32
BF16 = jnp.bfloat16
NN = (((1,), (0,)), ((), ()))
NT = (((1,), (1,)), ((), ()))
TN = (((0,), (0,)), ((), ()))
SCALE = HD ** (-0.5)
COST = 3.0
US = {'delta_terms': 12, 'delta_outputs': 6.5, 'mlp': 12.2, 'mlp_grads': 6.5, 'middle_back': 9.6, 'delta_back': 22, 'input_back': 3.7, 'mixer_sum': 3.5, 'mixer_total': 2.3, 'gate_up_whole': 3.3, 'mixer_whole': 2.9}
GU_BLOCKS = 6
SMALL_ROWS = 32
WIDE_ROWS = 6

ANY = pl.BlockSpec(memory_space=pl.ANY)
SMEM = pl.BlockSpec(memory_space=pltpu.SMEM)
VMEM = pl.BlockSpec(memory_space=pltpu.VMEM)


def parts_of(value, count):
    if value.dtype == BF16:
        return [value]
    pieces = []
    for left in range(count):
        piece = value.astype(BF16)
        pieces.append(piece)
        if left + 1 < count:
            value = value - piece.astype(F32)
    return pieces


def pdot(left, right, dims=NN):
    return lax.dot_general(left, right, dims, preferred_element_type=F32)


def mm_parts(lefts, rights, dims=NN):
    total = None
    for i, a in enumerate(lefts):
        for j, b in enumerate(rights):
            if i + j < max(len(lefts), len(rights)):
                term = pdot(a, b, dims)
                total = term if total is None else total + term
    return total


def mm(left, right, dims=NN, split=2):
    return mm_parts(parts_of(left, split), parts_of(right, split), dims)


def sigmoid(v):
    return 1.0 / (1.0 + jnp.exp(-v))


def iota(shape, axis):
    return lax.broadcasted_iota(jnp.int32, shape, axis)


def slots(meta, rows, axis, lengths):
    first = meta[0] * rows
    place = iota((rows, 1) if axis == 0 else (1, rows), axis) + first
    begins, end = jnp.zeros_like(place), 0
    for i in range(lengths):
        end = end + meta[2 + i]
        begins = jnp.where(end <= place, jnp.maximum(begins, end), begins)
    return begins - first, place < end


def unit_lower_inverses(lowers):
    n = lowers[0].shape[0]
    half = n // 2
    row, col = iota((half, half), 0), iota((half, half), 1)
    blocks = [low[at : at + half, at : at + half] for low in lowers for at in (0, half)]
    inverses = [jnp.where(row == col, 1.0, 0.0) - jnp.where(row // 2 == col // 2, b, 0.0) for b in blocks]
    split = [parts_of(b, 2) for b in blocks]
    zero = jnp.zeros((half, half), BF16)
    size = 2
    while size < half:
        inside = (row // (2 * size) == col // (2 * size)) & (row // size != col // size)
        pieces = [parts_of(inv, 2) for inv in inverses]
        steps = [mm_parts([jnp.where(inside, s, zero) for s in sp], pc) for sp, pc in zip(split, pieces, strict=True)]
        inverses = [inv - mm_parts(pc, parts_of(st, 2)) for inv, pc, st in zip(inverses, pieces, steps, strict=True)]
        size *= 2
    out = []
    for i, low in enumerate(lowers):
        top, bottom = inverses[2 * i], inverses[2 * i + 1]
        corner = -mm(bottom, mm(low[half:, :half], top))
        out.append((top, corner, bottom))
    return out


def conv_rows(pre, reach):
    return (pltpu.roll(pre, reach, 0) if reach else pre)[PAD:]


def conv_forward(pre, taps, age):
    total = jnp.zeros((pre.shape[0] - PAD, pre.shape[1]), F32)
    for k in range(CONV):
        reach = CONV - 1 - k
        total = total + jnp.where(age >= reach, conv_rows(pre, reach), 0.0) * taps[k : k + 1]
    return total


def pick(refs, j, *index):
    value = refs[-1][index]
    for k in range(len(refs) - 1, 0, -1):
        value = jnp.where(j == k, refs[k - 1][index], value)
    return value


def l2_ratio(values):
    return lax.rsqrt(jnp.sum(values * values, -1, keepdims=True) + EPS)


def rms_ratio(values):
    return lax.rsqrt(jnp.mean(values * values, -1, keepdims=True) + EPS)


def norm_back(values, gain, grad):
    ratio = rms_ratio(values)
    scaled = values * ratio
    weighted = grad * gain
    value_grad = ratio * (weighted - scaled * jnp.mean(weighted * scaled, -1, keepdims=True))
    return value_grad, jnp.sum(grad * scaled, 0, keepdims=True)


def terms_kernel(*refs, lengths, n_fsdp, cut):
    (meta, x_ref, gain_ref, bw_ref, taps_ref, local_ref, own_ref, one, two, three_a, three_b,
     w_ref, pre_ref, act_ref, tt_ref, y_ref, ms_ref, xt_ref, xh_ref, beta_ref, sem) = refs
    heads = w_ref.shape[0]
    d_loc = local_ref.shape[1]
    rows = x_ref.shape[0] - PAD
    ctx, fsdp = meta[0], meta[1]

    def fill(source, first, end, head, shard, skip=0):
        for i in range(3):
            start, stop = max(first, i * d_loc), min(end, (i + 1) * d_loc)
            if start < stop:
                at = pl.multiple_of(shard * d_loc + (start - i * d_loc), 16)
                target = w_ref.at[head, i, pl.ds(at, stop - start), :]
                pltpu.make_async_copy(source.at[pl.ds(start - skip, stop - start), :], target, sem).start()

    for f in range(n_fsdp):
        fill(own_ref.at[f], 0, 3 * d_loc, ctx, f)
    for j in range(1, 4):
        head = ctx ^ j
        for i in range(3):
            target = w_ref.at[head, i, pl.ds(pl.multiple_of(fsdp * d_loc, d_loc), d_loc), :]
            source = local_ref.at[i, :, pl.ds(pl.multiple_of(head * HD, HD), HD)]
            pltpu.make_async_copy(source, target, sem).start()
        for r in range(1, n_fsdp):
            shard = lax.rem(fsdp + n_fsdp - r, n_fsdp)
            if j < 3:
                fill((one, two)[j - 1].at[r - 1], 0, 3 * d_loc, head, shard)
            else:
                fill(three_a.at[r - 1], 0, cut, head, shard)
                fill(three_b.at[r - 1], cut, 3 * d_loc, head, shard, cut)

    x_wide = x_ref[...].astype(F32)
    normed = (x_wide * rms_ratio(x_wide) * gain_ref[...]).astype(BF16)
    xt_ref[...] = normed[PAD:].T
    xh_ref[...] = normed[:PAD].T
    beta = sigmoid(pdot(normed[PAD:], bw_ref[...]))
    beta_ref[...] = beta
    lb, _ = slots(meta, rows, 0, lengths)
    place = iota((rows, 1), 0)
    age = place - lb
    row, col = iota((rows, rows), 0), iota((rows, rows), 1)
    below = (col >= lb) & (col < row)
    lb_last = lb[rows - 1 :]
    last = jnp.where(place >= lb_last, 1.0, 0.0)
    keep = jnp.where(lb_last < 0, 1.0, 0.0)
    eye = jnp.where(iota((HD, HD), 0) == iota((HD, HD), 1), 1.0, 0.0)
    pltpu.make_async_copy(w_ref, w_ref, sem).wait()

    lowers, keys, scaled = [], [], []
    for h in range(heads):
        acts = []
        for i in range(3):
            pre = pdot(normed, w_ref[h, i]).astype(BF16)
            pre_ref[h, i] = pre
            total = conv_forward(pre.astype(F32), taps_ref[h, i], age)
            act = total * sigmoid(total)
            if i < 2:
                act = act * l2_ratio(act)
            acts.append(act.astype(BF16))
            act_ref[h, i] = acts[i]
        key, value = acts[1], acts[2]
        beta_h = beta[:, h : h + 1]
        lowers.append(jnp.where(below, beta_h * pdot(key, key, NT), 0.0))
        keys.append(key)
        scaled.append(beta_h * jnp.concatenate([key, value], -1).astype(F32))
    half = rows // 2
    for h, (top, corner, bottom) in enumerate(unit_lower_inverses(lowers)):
        tt_ref[h, :half, :half] = top.T
        tt_ref[h, :half, half:] = corner.T
        tt_ref[h, half:, :half] = jnp.zeros((half, half), F32)
        tt_ref[h, half:, half:] = bottom.T
        upper = mm(top, scaled[h][:half])
        lower = mm(jnp.concatenate([corner, bottom], -1), scaled[h])
        solved = jnp.concatenate([upper, lower])
        y_ref[h] = solved
        ms_ref[h, 0] = (keep * (eye - mm(solved[:, :HD], keys[h], TN))).astype(BF16)
        ms_ref[h, 1] = mm(last * solved[:, HD:], keys[h], TN).astype(BF16)


def output_kernel(*refs, lengths, sources, n_fsdp):
    (meta, y_ref, act_ref, gain_ref, local_ref, own_ref, o1, o2, o3), refs = refs[:9], refs[9:]
    arrived, (ow_ref, mixed_ref, r_ref, s_ref, n_ref, attn_ref, sem) = refs[:sources], refs[sources:]
    heads, rows = y_ref.shape[:2]
    ctx = meta[0]
    fsdp = meta[1]
    d_loc = local_ref.shape[0]

    def fill(source, head, shard):
        at = pl.multiple_of(shard * d_loc, d_loc)
        pltpu.make_async_copy(source, ow_ref.at[head, pl.ds(at, d_loc), :], sem).start()

    for j, piece in enumerate((own_ref, o1, o2, o3)):
        head = ctx ^ j
        fill(local_ref.at[:, pl.ds(pl.multiple_of(head * HD, HD), HD)], head, fsdp)
        for r in range(1, n_fsdp):
            fill(piece.at[r - 1], head, lax.rem(fsdp + n_fsdp - r, n_fsdp))
    lb, _ = slots(meta, rows, 0, lengths)
    row, col = iota((rows, rows), 0), iota((rows, rows), 1)
    upto = (col >= lb) & (col <= row)
    carried = jnp.where(lb < 0, 1.0, 0.0)
    normed = []
    for h in range(heads):
        state = jnp.zeros((HD, HD), F32)
        for c in range(sources):
            after = pick(arrived, ctx ^ c, h, 1).astype(F32)
            if c:
                after = after + mm(state, pick(arrived, ctx ^ c, h, 0))
            state = jnp.where(c < ctx, after, state)
        query, key = act_ref[h, 0], act_ref[h, 1]
        w_part, u_part = y_ref[h, :, :HD], y_ref[h, :, HD:]
        scores = jnp.where(upto, pdot(query, key, NT) * SCALE, 0.0)
        fresh = u_part - carried * mm(w_part, state, NT)
        mixed = carried * (SCALE * mm(query, state, NT)) + mm(scores, fresh)
        mixed_ref[h] = mixed
        r_ref[h] = fresh
        s_ref[h] = state
        out = (mixed * rms_ratio(mixed) * gain_ref[...]).astype(BF16)
        n_ref[:, h * HD : (h + 1) * HD] = out
        normed.append(out)
    pltpu.make_async_copy(ow_ref, ow_ref, sem).wait()
    total = pdot(normed[0], ow_ref[0], NT)
    for h in range(1, heads):
        total = total + pdot(normed[h], ow_ref[h], NT)
    attn_ref[...] = total


def mlp_kernel(*refs, lengths, n_fsdp):
    (meta, x_ref, attn_ref, other_ref, gain_ref, cot_ref, local_ref, own_ref, f1, f2, a3, b3, down_ref,
     mid_ref, nt_ref, at_ref, g_ref, gf_ref, part_ref, st_ref, w, gu, sem) = refs
    rows, width = x_ref.shape
    units = down_ref.shape[0]
    d_loc = local_ref.shape[0]
    step = GU_BLOCKS * HD
    half = step // 2
    quarters = w.shape[0]
    ctx, fsdp = meta[0], meta[1]

    def fill(source, quarter, shard, at, size):
        start = pl.multiple_of(shard * d_loc, d_loc)
        pltpu.make_async_copy(source, w.at[quarter, pl.ds(start, d_loc), pl.ds(at, size)], sem).start()

    for f in range(n_fsdp):
        fill(own_ref.at[f], ctx, f, 0, step)
    for j in range(1, 4):
        quarter = ctx ^ j
        fill(local_ref.at[:, pl.ds(pl.multiple_of(quarter * step, HD), step)], quarter, fsdp, 0, step)
        for r in range(1, n_fsdp):
            shard = lax.rem(fsdp + n_fsdp - r, n_fsdp)
            if j < 3:
                fill((f1, f2)[j - 1].at[r - 1], quarter, shard, 0, step)
            else:
                fill(a3.at[r - 1], quarter, shard, 0, half)
                fill(b3.at[r - 1], quarter, shard, half, half)

    _, inside = slots(meta, rows, 0, lengths)
    valid = jnp.where(inside, 1.0, 0.0)
    x_wide = x_ref[...].astype(F32)
    attn = (attn_ref[...] + other_ref[...]) * valid
    middle = x_wide + attn
    mid_ref[...] = middle
    for i, v in enumerate((x_wide, attn, middle)):
        st_ref[i : i + 1] = jnp.sum(valid * v * v, 0, keepdims=True)
    normed = (middle * rms_ratio(middle) * gain_ref[...]).astype(BF16)
    nt_ref[...] = normed.T
    g_ffn = (cot_ref[...].astype(F32) * valid).astype(BF16)
    gf_ref[...] = g_ffn
    g_act = pdot(g_ffn, down_ref[...], NT)
    pltpu.make_async_copy(w, w, sem).wait()
    for q in range(quarters):
        gu[:, q * step : (q + 1) * step] = pdot(normed, w[q])
    gate, up = gu[:, :units], gu[:, units : 2 * units]
    sig = sigmoid(gate)
    act = (gate * sig * up).astype(BF16)
    at_ref[...] = act.T
    g_up = g_act * gate * sig
    g_gate = g_act * up * sig * (1.0 + gate * (1.0 - sig))
    gu[:, :units] = g_gate
    gu[:, units : 2 * units] = g_up
    part = None
    for q in range(quarters):
        real = min(step, 2 * units - q * step)
        grad = gu[:, q * step : q * step + real].astype(BF16)
        if real < step:
            grad = jnp.concatenate([grad, jnp.zeros((rows, step - real), BF16)], -1)
        g_ref[ctx ^ q] = grad
        term = pdot(grad, w[q], NT)
        part = term if part is None else part + term
    part_ref[:rows] = part
    part_ref[rows:] = pdot(act, down_ref[...])


def mlp_grads_kernel(nt_ref, g_ref, at_ref, gf_ref, x3_ref, y3_ref, x1_ref, y2_ref, late_x_ref, late_y_ref, own_ref, down_ref):
    half = g_ref.shape[2] // 2
    nt = nt_ref[...]

    def put(ref, j, side):
        ref[...] = pdot(nt, g_ref[j, :, side * half : (side + 1) * half]).astype(BF16)

    put(x3_ref, 3, 0)
    put(y3_ref, 3, 1)
    put(x1_ref, 1, 0)
    put(y2_ref, 2, 1)
    put(late_x_ref, 1, 1)
    put(late_y_ref, 2, 0)
    put(own_ref.at[0], 0, 0)
    put(own_ref.at[1], 0, 1)
    down_ref[...] = pdot(at_ref[...], gf_ref[...]).astype(BF16)


def middle_kernel(
    meta, part_ref, other_ref, mid_ref, cot_ref, gain_ref, hgain_ref, ow_ref, n_ref, mixed_ref, act_ref, y_ref,
    out_ref, gm_ref, og_ref, do_ref, dr_ref, ds_ref, sm_ref, *, lengths
):
    heads, rows = mixed_ref.shape[:2]
    ctx = meta[0]
    lb, inside = slots(meta, rows, 0, lengths)
    lb_row, _ = slots(meta, rows, 1, lengths)
    valid = jnp.where(inside, 1.0, 0.0)
    row, col = iota((rows, rows), 0), iota((rows, rows), 1)
    upto = (row >= lb_row) & (row <= col)
    carried = jnp.where(lb < 0, 1.0, 0.0)
    middle = mid_ref[...]
    value_grad, gain_grad = norm_back(middle, gain_ref[...], part_ref[:rows] + other_ref[:rows])
    g_middle = cot_ref[...].astype(F32) + value_grad
    gm_ref[...] = g_middle
    g_attn = (g_middle * valid).astype(BF16)
    turned_grad = g_attn.T
    total = jnp.zeros((1, HD), F32)
    for h in range(heads):
        key = act_ref[h, 1]
        g_head = pdot(g_attn, ow_ref[h])
        d_mixed, part = norm_back(mixed_ref[h], hgain_ref[...], g_head)
        total = total + part
        turned = jnp.where(upto, pdot(key, act_ref[h, 0], NT) * SCALE, 0.0)
        d_fresh = mm(turned, d_mixed)
        do_ref[h] = d_mixed
        dr_ref[h] = d_fresh
        d_state = SCALE * mm(carried * d_mixed, act_ref[h, 0], TN) - mm(carried * d_fresh, y_ref[h, :, :HD], TN)
        ds_ref[h] = d_state.astype(BF16)
        og_ref[ctx ^ h] = pdot(turned_grad, n_ref[:, h * HD : (h + 1) * HD]).astype(BF16)
    ffn = (part_ref[rows:] + other_ref[rows:]) * valid
    result = middle + ffn
    out_ref[...] = result.astype(BF16)
    sm_ref[...] = jnp.zeros_like(sm_ref)
    sm_ref[0:1] = gain_grad
    sm_ref[1:2, :HD] = total
    sm_ref[2:3] = jnp.sum(valid * ffn * ffn, 0, keepdims=True)
    sm_ref[3:4] = jnp.sum(valid * result * result, 0, keepdims=True)
    sm_ref[4:5] = jnp.broadcast_to(jnp.sum(valid, 0, keepdims=True), gain_grad.shape) / gain_grad.shape[1]


def delta_back_kernel(*refs, lengths, sources):
    meta, grads, maps = refs[0], refs[1 : 1 + sources], refs[1 + sources : 1 + 2 * sources]
    (pre_ref, act_ref, tt_ref, y_ref, r_ref, s_ref, do_ref, dr_ref, beta_ref, taps_ref, w_ref, bw_ref, xt_ref, xh_ref, sm_ref, og_ref,
     keep_ref, x_ref, y2_ref, late_x_ref, late_y_ref, part_ref, bg_ref, cg_ref) = refs[1 + 2 * sources :]
    heads, rows = r_ref.shape[:2]
    width = w_ref.shape[2]
    ext = rows + PAD
    ctx = meta[0]
    lb, _ = slots(meta, rows, 0, lengths)
    lb_row, _ = slots(meta, rows, 1, lengths)
    place = iota((rows, 1), 0)
    age = place - lb
    row, col = iota((rows, rows), 0), iota((rows, rows), 1)
    last = jnp.where(place >= lb[rows - 1 :], 1.0, 0.0)
    carried = jnp.where(lb < 0, 1.0, 0.0)
    upto = (col >= lb) & (col <= row)
    below = (col >= lb) & (col < row)
    turned_upto = (row >= lb_row) & (row <= col)
    lane = iota((rows, HD), 1)
    logits = jnp.zeros((rows, HD), F32)
    top = jnp.zeros((PAD, HD), F32)
    xt, xh = xt_ref[...], xh_ref[...]
    part = jnp.zeros((rows, width), F32)
    ahead = jnp.zeros((PAD, width), F32)
    for h in range(heads):
        d_state = jnp.zeros((HD, HD), F32)
        for c in range(sources, 0, -1):
            before = pick(grads, ctx ^ c, h).astype(F32)
            if c < sources:
                before = before + mm(d_state, pick(maps, ctx ^ c, h, 0), NT)
            d_state = jnp.where(c > ctx, before, d_state)
        query, key, value = act_ref[h, 0], act_ref[h, 1], act_ref[h, 2]
        solved = y_ref[h]
        fresh, state, d_mixed = r_ref[h], s_ref[h], do_ref[h]
        beta = beta_ref[:, h : h + 1]
        d_fresh = dr_ref[h] + last * mm(key, d_state, NT)
        d_scores = jnp.where(upto, SCALE * mm(d_mixed, fresh, NT), 0.0)
        turned = jnp.where(turned_upto, SCALE * mm(fresh, d_mixed, NT), 0.0)
        d_query = mm(d_scores, key) + carried * (SCALE * mm(d_mixed, state))
        d_key = mm(turned, query) + mm(last * fresh, d_state)
        d_solved = jnp.concatenate([-carried * mm(d_fresh, state), d_fresh], -1)
        d_scaled = mm(tt_ref[h], d_solved)
        d_value = beta * d_scaled[:, HD:]
        d_key = d_key + beta * d_scaled[:, :HD]
        d_beta = jnp.sum(d_scaled[:, :HD] * key.astype(F32) + d_scaled[:, HD:] * value.astype(F32), -1, keepdims=True)
        d_lower = jnp.where(below, -mm(d_scaled, solved, NT), 0.0)
        d_beta = d_beta + jnp.sum(d_lower * pdot(key, key, NT), -1, keepdims=True)
        d_gram = beta * d_lower
        d_key = d_key + mm(d_gram, key) + mm(d_gram, key, TN)
        logits = jnp.where(lane == h, d_beta * beta * (1.0 - beta), logits)
        g_main, g_head = [], []
        for i, grad in enumerate((d_query, d_key, d_value)):
            taps = taps_ref[h, i]
            pre = pre_ref[h, i].astype(F32)
            total = conv_forward(pre, taps, age)
            sig = sigmoid(total)
            if i < 2:
                act = total * sig
                ratio = l2_ratio(act)
                unit = act * ratio
                grad = ratio * (grad - unit * jnp.sum(grad * unit, -1, keepdims=True))
            grad = grad * sig * (1.0 + total * (1.0 - sig))
            back = jnp.zeros((ext, HD), F32)
            for k in range(CONV):
                reach = CONV - 1 - k
                grad_k = jnp.where(age >= reach, grad, 0.0)
                cg_ref[h, i * CONV + k : i * CONV + k + 1, :] = jnp.sum(grad_k * conv_rows(pre, reach), 0, keepdims=True)
                padded = jnp.concatenate([top, grad_k])
                back = back + (pltpu.roll(padded, ext - reach, 0) if reach else padded) * taps[k : k + 1]
            g_main.append(back[PAD:].astype(BF16))
            g_head.append(back[:PAD].astype(BF16))
            part = part + pdot(g_main[i], w_ref[h, i], NT)
            ahead = ahead + pdot(g_head[i], w_ref[h, i], NT)
        piece = pdot(xt, jnp.concatenate(g_main, -1)) + pdot(xh, jnp.concatenate(g_head, -1))
        piece = piece.astype(BF16)
        places = (
            (keep_ref.at[0], keep_ref.at[1]),
            (x_ref.at[1], late_x_ref),
            (late_y_ref, y2_ref.at[1]),
            (x_ref.at[0], y2_ref.at[0]),
        )
        for j, (a, b) in enumerate(places):

            @pl.when(ctx ^ j == h)
            def _(a=a, b=b, j=j, piece=piece):
                a[...] = piece[:, : 2 * HD]
                b[:, :HD] = piece[:, 2 * HD :]
                b[:, HD:] = og_ref[j]

    logits = logits.astype(BF16)
    part_ref[:rows] = part + pdot(logits, bw_ref[...], NT)
    part_ref[rows:ext] = ahead
    part_ref[ext:] = jnp.zeros((PAD, width), F32)
    part_ref[ext : ext + 1, :HD] = sm_ref[1:2, :HD]
    bg_ref[...] = lax.dot_general(logits, xt, (((0,), (1,)), ((), ())), preferred_element_type=F32)[:PAD]


def last_kernel(x_ref, gain_ref, part_ref, other_ref, rim_ref, gm_ref, sm_ref, st_ref, bg_ref, cg_ref, grad_ref, small_ref):
    rows, width = x_ref.shape
    heads = cg_ref.shape[0]
    total = part_ref[...] + other_ref[...]
    grad = jnp.concatenate([total[: rows - PAD], total[rows - PAD : rows] + rim_ref[...]])
    value_grad, gain_grad = norm_back(x_ref[...].astype(F32), gain_ref[...], grad)
    grad_ref[...] = gm_ref[...] + value_grad
    small_ref[...] = jnp.zeros_like(small_ref)
    small_ref[0:1] = gain_grad
    small_ref[1:2] = sm_ref[0:1]
    small_ref[2 : 2 + heads] = bg_ref[:heads]
    small_ref[6:9] = st_ref[0:3]
    small_ref[9:11] = sm_ref[2:4]
    small_ref[11:12] = sm_ref[4:5]
    at = WIDE_ROWS + 6
    for h in range(heads):
        small_ref[at : at + 3 * CONV, h * HD : (h + 1) * HD] = cg_ref[h, : 3 * CONV]
    at += 3 * CONV
    small_ref[at : at + 1, :HD] = total[rows + PAD : rows + PAD + 1, :HD]


def mixer_sum_kernel(meta, keep_ref, x_ref, y_ref, late_y_ref, late_x_ref, s0, s1, s2, s3, *outs, n_fsdp):
    width, half = x_ref.shape[1:]
    d_loc = width // n_fsdp
    grouped = len(outs) < n_fsdp
    small = (s0[...] + s1[...]) + (s2[...] + s3[...])
    rows, lanes = iota((SMALL_ROWS, 2 * half), 0), iota((SMALL_ROWS, 2 * half), 1)
    stats = jnp.sum(small, -1, keepdims=True)
    high = stats.astype(BF16).astype(F32)
    common = jnp.where(rows < WIDE_ROWS + 6, jnp.where(lanes < half + HD, high, stats - high), small[:, : 2 * half])
    for r in range(n_fsdp):
        shard = r if grouped else lax.rem(meta[1] + r, n_fsdp)
        ref, first = (outs[0], r * (d_loc + SMALL_ROWS)) if grouped else (outs[r], 0)
        at = pl.ds(r * d_loc if grouped else pl.multiple_of(shard * d_loc, d_loc), d_loc)
        a = keep_ref[0, at, :].astype(F32) + x_ref[1, at, :].astype(F32) + late_y_ref[at, :].astype(F32)
        b = keep_ref[1, at, :].astype(F32) + y_ref[1, at, :].astype(F32) + late_x_ref[at, :].astype(F32)
        ref[first : first + d_loc, :half] = a.astype(BF16)
        ref[first : first + d_loc, half:] = b.astype(BF16)
        slices = [small[:, k * d_loc : (k + 1) * d_loc] for k in ([r] if grouped else range(n_fsdp))]
        mine = slices[0]
        for k in range(1, len(slices)):
            mine = jnp.where(shard == k, slices[k], mine)
        mine = jnp.concatenate([mine, jnp.zeros((SMALL_ROWS, 2 * half - d_loc), F32)], -1)
        ref[first + d_loc : first + d_loc + SMALL_ROWS] = jnp.where(rows < WIDE_ROWS, mine, common).astype(BF16)


def mixer_total_kernel(meta, own_ref, *refs, width):
    far, (mix_ref, first_ref, second_ref, beta_ref, conv_ref, head_ref, rms_ref) = refs[:-7], refs[-7:]
    count, rows = len(far) + 1, mix_ref.shape[0]
    heads, hd_loc = conv_ref.shape[1:]
    total = None
    for f in range(count):
        part = own_ref[...]
        for r, ref in enumerate(far):
            part = jnp.where(lax.rem(meta[1] + count - (r + 1), count) == f, ref[...], part)
        part = part.astype(F32)
        total = part if total is None else total + part
    mix_ref[...] = total[:rows].astype(BF16)
    small = total[rows:]
    first_ref[...] = small[0:1, :rows]
    second_ref[...] = small[1:2, :rows]
    beta_ref[...] = small[:8, :rows].T[:, 2 : 2 + heads]
    for h in range(heads):
        lanes = small[WIDE_ROWS + 6 :, h * HD : (h + 1) * HD]
        mine = lanes[:, :hd_loc]
        for k in range(1, HD // hd_loc):
            mine = jnp.where(meta[1] == k, lanes[:, k * hd_loc : (k + 1) * hd_loc], mine)
        conv_ref[:, h, :] = mine[: 3 * CONV]
        if h == 0:
            head_ref[...] = mine[3 * CONV : 3 * CONV + 1]
    stats = small[WIDE_ROWS : WIDE_ROWS + 6, 2 * HD : 2 * HD + 1] + small[WIDE_ROWS : WIDE_ROWS + 6, 3 * HD : 3 * HD + 1]
    rms_ref[...] = jnp.sqrt(stats[:5] / (stats[5:] * width))


def gate_up_whole_kernel(p_ref, d0, d1, e0, e1, gu_ref, down_ref):
    units = gu_ref.shape[2]
    down_ref[: d0.shape[0]] = d0[...].astype(F32) + d1[...].astype(F32)
    down_ref[d0.shape[0] :] = e0[...].astype(F32) + e1[...].astype(F32)
    for q in range(p_ref.shape[0]):
        for k in range(GU_BLOCKS):
            at = (q * GU_BLOCKS + k) * HD
            if at < 2 * units:
                gu_ref[at // units, :, at % units : at % units + HD] = p_ref[q, :, k * HD : (k + 1) * HD].astype(F32)


def mixer_whole_kernel(meta, p0, p1, p2, p3, qkv_ref, out_ref):
    ctx = meta[0]
    for q in range(4):
        for j, ref in enumerate((p0, p1, p2, p3)):

            @pl.when(ctx ^ j == q)
            def _(ref=ref, q=q):
                for i in range(3):
                    qkv_ref[i, :, q * HD : (q + 1) * HD] = ref[:, i * HD : (i + 1) * HD].astype(F32)
                out_ref[q * HD : (q + 1) * HD, :] = ref[:, 3 * HD :].T.astype(F32)


def sds(*shape, dtype=F32):
    return jax.ShapeDtypeStruct(shape, dtype)


def call(body, name, out_shape, in_specs, args, scratch=(), gflops=1, mbytes=4):
    return pl.pallas_call(
        body,
        name=name,
        in_specs=in_specs,
        out_specs=jax.tree.map(lambda _: VMEM, out_shape),
        out_shape=out_shape,
        scratch_shapes=list(scratch),
        compiler_params=pltpu.CompilerParams(vmem_limit_bytes=56 * 1024 * 1024),
        cost_estimate=pl.CostEstimate(flops=int(COST * US[name] * 1_150_000_000), bytes_accessed=10**6, transcendentals=0),
    )(*args)


def shifted(value, axis, steps):
    count = lax.axis_size(axis)
    first, end = max(0, -steps), min(count, count - steps)
    return lax.ppermute(value, axis, [(s, s + steps) for s in range(first, end)])


def swapped(value, axis, mask):
    return lax.ppermute(value, axis, [(s, s ^ mask) for s in range(lax.axis_size(axis))])


def far_shards(value):
    count = lax.axis_size("fsdp")
    if count <= 4:
        turns = [[(s, (s + r) % count) for s in range(count)] for r in range(1, count)]
        return [lax.ppermute(value, "fsdp", turn)[None] for turn in turns]
    return [others(lax.all_gather(value, "fsdp", axis=0))]


def others(value):
    return jnp.concatenate([other(value, r) for r in range(1, lax.axis_size("fsdp"))])


def other(value, r):
    count, here = lax.axis_size("fsdp"), lax.axis_index("fsdp")
    return lax.dynamic_index_in_dim(value, (here + count - r) % count, 0)


def local(
    tokens, lengths, norm_gain, qkv_weight, beta_weight, conv_weight, head_gain, out_weight, mlp_gain, gate_up_weight, down_weight, cotangent
):
    rows, width = tokens.shape
    n_ctx, n_fsdp = lax.axis_size("ctx"), lax.axis_size("fsdp")
    ctx, fsdp = lax.axis_index("ctx"), lax.axis_index("fsdp")
    d_loc = qkv_weight.shape[1]
    heads = beta_weight.shape[1]
    units = down_weight.shape[0]
    hd_loc = head_gain.shape[0]
    n_len = lengths.shape[1]
    step = GU_BLOCKS * HD
    ext = rows + PAD
    meta = jnp.concatenate([jnp.stack([ctx, fsdp]).astype(jnp.int32), lengths[0]])

    small = jnp.concatenate([norm_gain, mlp_gain, head_gain, beta_weight.reshape(-1), conv_weight.reshape(-1)])
    small_rows = -(-small.shape[0] // (HD * 16)) * 16
    small = jnp.pad(small, (0, small_rows * HD - small.shape[0])).reshape(small_rows, HD)
    qkv_part = lax.dynamic_slice_in_dim(qkv_weight, ctx * HD, HD, 2).reshape(3 * d_loc, HD)
    out_part = lax.dynamic_slice_in_dim(out_weight, ctx * HD, HD, 0).T
    pack = jnp.concatenate([qkv_part, small])
    packs = lax.all_gather(pack, "fsdp", axis=0)
    pack_far = others(packs)
    out_local = out_weight.T
    gu_local = jnp.concatenate(
        [gate_up_weight[0], gate_up_weight[1], jnp.zeros((d_loc, n_ctx * step - 2 * units), BF16)], -1
    )
    gu_part = lax.dynamic_slice_in_dim(gu_local, ctx * step, step, 1)
    gu_own = lax.all_gather(gu_part, "fsdp", axis=0)
    gu_far = others(gu_own)
    down_full = lax.all_gather(down_weight, "fsdp", axis=1, tiled=True)
    x_ext = jnp.concatenate([shifted(tokens[rows - PAD :], "ctx", 1), tokens])

    cut = 3 * d_loc // 2
    pack_far, out_part = lax.optimization_barrier((pack_far, out_part))
    one, two = swapped(pack_far, "ctx", 1), swapped(pack_far, "ctx", 2)
    out_far = far_shards(out_part)
    three_a, three_b = swapped(one[:, :cut], "ctx", 2), swapped(two[:, cut:], "ctx", 1)
    three_a, three_b, out_far = lax.optimization_barrier((three_a, three_b, out_far))
    out_far = jnp.concatenate(out_far)
    out_pieces = [swapped(out_far, "ctx", j) for j in range(1, n_ctx)]

    flat = packs[:, 3 * d_loc :].reshape(n_fsdp, -1)
    at = 0
    first_gain = flat[:, at : at + d_loc].reshape(1, width).astype(F32)
    at += d_loc
    second_gain = flat[:, at : at + d_loc].reshape(1, width).astype(F32)
    at += d_loc
    head_full = flat[:, at : at + hd_loc].reshape(1, HD).astype(F32)
    at += hd_loc
    beta_full = jnp.pad(flat[:, at : at + d_loc * heads].reshape(width, heads), ((0, 0), (0, HD - heads)))
    at += d_loc * heads
    conv_full = flat[:, at : at + 3 * CONV * heads * hd_loc].reshape(n_fsdp, 3, CONV, heads, hd_loc)
    conv_full = conv_full.transpose(3, 1, 2, 0, 4).reshape(heads, 3, CONV, HD).astype(F32)

    qkv_full, pre, acts, turned, solved, ends_map, normed_t, normed_far, beta = call(
        functools.partial(terms_kernel, lengths=n_len, n_fsdp=n_fsdp, cut=cut),
        "delta_terms",
        (
            sds(heads, 3, width, HD, dtype=BF16),
            sds(heads, 3, ext, HD, dtype=BF16),
            sds(heads, 3, rows, HD, dtype=BF16),
            sds(heads, rows, rows),
            sds(heads, rows, 2 * HD),
            sds(heads, 2, HD, HD, dtype=BF16),
            sds(width, rows, dtype=BF16),
            sds(width, PAD, dtype=BF16),
            sds(rows, HD),
        ),
        [SMEM] + [VMEM] * 4 + [ANY] * 6,
        (meta, x_ext, first_gain, beta_full, conv_full, qkv_weight, packs, one, two, three_a, three_b),
        [pltpu.SemaphoreType.DMA],
        gflops=15,
        mbytes=8,
    )
    arrived = [swapped(ends_map, "ctx", j) for j in range(1, n_ctx)]
    gu_one, gu_two = lax.optimization_barrier((swapped(gu_far, "ctx", 1), swapped(gu_far, "ctx", 2)))
    gu_three = (swapped(gu_one[:, :, : step // 2], "ctx", 2), swapped(gu_two[:, :, step // 2 :], "ctx", 1))
    out_full, mixed, fresh, state, head_out, attn_part = call(
        functools.partial(output_kernel, lengths=n_len, sources=n_ctx - 1, n_fsdp=n_fsdp),
        "delta_outputs",
        (
            sds(heads, width, HD, dtype=BF16),
            sds(heads, rows, HD),
            sds(heads, rows, HD),
            sds(heads, HD, HD),
            sds(rows, heads * HD, dtype=BF16),
            sds(rows, width),
        ),
        [SMEM] + [VMEM] * 3 + [ANY] * (1 + n_ctx) + [VMEM] * len(arrived),
        (meta, solved, acts, head_full, out_local, out_far, *out_pieces, *arrived),
        [pltpu.SemaphoreType.DMA],
        gflops=6,
        mbytes=6,
    )
    attn_other = swapped(attn_part, "tp", 1)

    middle, normed_mid_t, act_t, g_gu, g_ffn, mlp_part, stats = call(
        functools.partial(mlp_kernel, lengths=n_len, n_fsdp=n_fsdp),
        "mlp",
        (
            sds(rows, width),
            sds(width, rows, dtype=BF16),
            sds(units, rows, dtype=BF16),
            sds(n_ctx, rows, step, dtype=BF16),
            sds(rows, width, dtype=BF16),
            sds(2 * rows, width),
            sds(8, width),
        ),
        [SMEM] + [VMEM] * 5 + [ANY] * 6 + [VMEM],
        (
            meta, tokens, attn_part, attn_other, second_gain, cotangent, gu_local, gu_own, gu_one, gu_two, *gu_three, down_full,
        ),
        [pltpu.VMEM((n_ctx, width, step), BF16), pltpu.VMEM((rows, n_ctx * step), F32), pltpu.SemaphoreType.DMA],
        gflops=10,
        mbytes=14,
    )
    mlp_other = swapped(mlp_part, "tp", 1)
    quarter = sds(width, step // 2, dtype=BF16)
    double = sds(2, width, step // 2, dtype=BF16)
    gu_grads = call(
        mlp_grads_kernel,
        "mlp_grads",
        (quarter,) * 6 + (double, sds(units, width, dtype=BF16)),
        [VMEM] * 4,
        (normed_mid_t, g_gu, act_t, g_ffn),
        gflops=4,
        mbytes=12,
    )
    mlp_other, gu_grads = lax.optimization_barrier((mlp_other, gu_grads))
    gu_x3, gu_y3, gu_x1, gu_y2, gu_late_x, gu_late_y, gu_keep, down_grad = gu_grads
    from_x3, from_y3 = swapped(gu_x3, "ctx", 1), swapped(gu_y3, "ctx", 2)

    result, g_middle, out_grads, d_mixed, d_fresh, d_state, sums = call(
        functools.partial(middle_kernel, lengths=n_len),
        "middle_back",
        (
            sds(rows, width, dtype=BF16),
            sds(rows, width),
            sds(n_ctx, width, HD, dtype=BF16),
            sds(heads, rows, HD),
            sds(heads, rows, HD),
            sds(heads, HD, HD, dtype=BF16),
            sds(8, width),
        ),
        [SMEM] + [VMEM] * 11,
        (
            meta, mlp_part, mlp_other, middle, cotangent, second_gain, head_full, out_full, head_out, mixed, acts,
            solved,
        ),
        gflops=6,
        mbytes=12,
    )
    behind = [swapped(d_state, "ctx", j) for j in range(1, n_ctx)]

    down_sh = lax.psum_scatter(down_grad, "fsdp", scatter_dimension=1, tiled=True)

    def add(left, right):
        return (left.astype(F32) + right.astype(F32)).astype(BF16)

    gu_x1, gu_y2, _ = lax.optimization_barrier((gu_x1, gu_y2, d_state))
    from_x1, from_y2 = swapped(gu_x1, "ctx", 1), swapped(gu_y2, "ctx", 2)
    gu_late_y, gu_late_x = add(gu_late_y, from_x3), add(gu_late_x, from_y3)
    behind, gu_late_x, gu_late_y = lax.optimization_barrier((behind, gu_late_x, gu_late_y))
    gu_late_y, gu_late_x = swapped(gu_late_y, "ctx", 2), swapped(gu_late_x, "ctx", 1)
    half = sds(width, 2 * HD, dtype=BF16)
    double = sds(2, width, 2 * HD, dtype=BF16)
    back = call(
        functools.partial(delta_back_kernel, lengths=n_len, sources=n_ctx - 1),
        "delta_back",
        (double, double, double, half, half, sds(ext + PAD, width), sds(PAD, width), sds(heads, 16, HD)),
        [SMEM] + [VMEM] * (2 * n_ctx - 2 + 16),
        (
            meta, *behind, *arrived, pre, acts, turned, solved, fresh, state, d_mixed, d_fresh, beta, conv_full, qkv_full, beta_full,
            normed_t, normed_far, sums, out_grads,
        ),
        gflops=16,
        mbytes=16,
    )

    mix_keep, mix_x, mix_y, mix_late_x, mix_late_y, in_part, beta_grad, conv_grad = back
    from_x1, from_y2, gu_late_x, gu_late_y, mix_keep, down_sh = lax.optimization_barrier(
        (from_x1, from_y2, gu_late_x, gu_late_y, mix_keep, down_sh)
    )
    in_other = swapped(in_part, "tp", 1)
    rim = shifted(in_part[rows:ext] + in_other[rows:ext], "ctx", -1)
    mix_from_x, mix_from_y = swapped(mix_x, "ctx", 1), swapped(mix_y, "ctx", 2)
    mix_from_x, mix_from_y, rim, down_sh = lax.optimization_barrier((mix_from_x, mix_from_y, rim, down_sh))
    input_grad, smalls = call(
        last_kernel,
        "input_back",
        (sds(rows, width), sds(SMALL_ROWS, width)),
        [VMEM] * 10,
        (tokens, first_gain, in_part, in_other, rim, g_middle, sums, stats, beta_grad, conv_grad),
        gflops=1,
        mbytes=6,
    )
    small_pieces = [smalls] + [swapped(smalls, "ctx", j) for j in range(1, n_ctx)]
    gu_sum = [
        (gu_keep[0].astype(F32) + from_x1.astype(F32) + gu_late_y.astype(F32)).astype(BF16),
        (gu_keep[1].astype(F32) + from_y2.astype(F32) + gu_late_x.astype(F32)).astype(BF16),
    ]
    gu_sh = lax.psum_scatter(jnp.concatenate(gu_sum, -1), "fsdp", scatter_dimension=0, tiled=True)

    mix_late_y, mix_late_x = add(mix_late_y, mix_from_x[0]), add(mix_late_x, mix_from_y[0])
    mix_late_y, mix_late_x = lax.optimization_barrier((swapped(mix_late_y, "ctx", 2), swapped(mix_late_x, "ctx", 1)))
    side = units // 2
    down_a, down_b = down_sh[:side], down_sh[side:]
    down_other = swapped(down_a, "ctx", 1), swapped(down_b, "ctx", 2)
    count = n_fsdp if n_fsdp <= 4 else 1
    mix_rows = n_fsdp // count * (d_loc + SMALL_ROWS)
    mix_own, *mix_far = call(
        functools.partial(mixer_sum_kernel, n_fsdp=n_fsdp),
        "mixer_sum",
        (sds(mix_rows, 4 * HD, dtype=BF16),) * count,
        [SMEM] + [VMEM] * (5 + n_ctx),
        (meta, mix_keep, mix_from_x, mix_from_y, mix_late_y, mix_late_x, *small_pieces),
        gflops=1,
        mbytes=6,
    )
    mix_own, down_other, gu_sh = lax.optimization_barrier((mix_own, down_other, gu_sh))
    down_a, down_b = add(down_a, down_other[0]), add(down_b, down_other[1])
    down_parts = (down_a, swapped(down_a, "ctx", 2), down_b, swapped(down_b, "ctx", 1))
    gu_all = lax.all_gather(gu_sh, "ctx", axis=0)
    if count > 1:
        turns = [[(i, (i + r) % n_fsdp) for i in range(n_fsdp)] for r in range(1, n_fsdp)]
        mix_far = [lax.ppermute(part, "fsdp", turn) for part, turn in zip(mix_far, turns, strict=True)]
        mix_far, down_a, down_b = lax.optimization_barrier((mix_far, down_a, down_b))
    else:
        mix_own = lax.psum_scatter(mix_own, "fsdp", scatter_dimension=0, tiled=True)
    mix_sh, first_out, second_out, beta_out, conv_out, head_out_grad, rms = call(
        functools.partial(mixer_total_kernel, width=width),
        "mixer_total",
        (
            sds(d_loc, 4 * HD, dtype=BF16),
            sds(1, d_loc),
            sds(1, d_loc),
            sds(d_loc, heads),
            sds(3 * CONV, heads, hd_loc),
            sds(1, hd_loc),
            sds(5, 1),
        ),
        [SMEM] + [VMEM] * count,
        (meta, mix_own, *mix_far),
        gflops=1,
        mbytes=1,
    )
    def pieces(part):
        return [part] + [swapped(part, "ctx", j) for j in range(1, n_ctx)]

    gu_out, down_out = call(
        gate_up_whole_kernel,
        "gate_up_whole",
        (sds(2, d_loc, units), sds(units, d_loc)),
        [VMEM] * 5,
        (gu_all, *down_parts),
        gflops=1,
        mbytes=6,
    )
    qkv_out, out_out = call(
        mixer_whole_kernel,
        "mixer_whole",
        (sds(3, d_loc, heads * HD), sds(heads * HD, d_loc)),
        [SMEM] + [VMEM] * n_ctx,
        (meta, *pieces(mix_sh)),
        gflops=1,
        mbytes=4,
    )
    return (
        result,
        input_grad,
        first_out.reshape(-1),
        qkv_out,
        beta_out,
        conv_out.reshape(3, CONV, heads, hd_loc),
        head_out_grad.reshape(-1),
        out_out,
        second_out.reshape(-1),
        gu_out,
        down_out,
        rms.reshape(-1),
    )


def solution(mesh):
    return jax.shard_map(
        local,
        mesh=mesh,
        in_specs=(
            P(("fsdp", "ctx"), None),
            P("fsdp", None),
            P("fsdp"),
            P(None, "fsdp", "tp"),
            P("fsdp", "tp"),
            P(None, None, "tp", "fsdp"),
            P("fsdp"),
            P("tp", "fsdp"),
            P("fsdp"),
            P(None, "fsdp", "tp"),
            P("tp", "fsdp"),
            P(("fsdp", "ctx"), None),
        ),
        out_specs=(
            P(("fsdp", "ctx"), None),
            P(("fsdp", "ctx"), None),
            P("fsdp"),
            P(None, "fsdp", "tp"),
            P("fsdp", "tp"),
            P(None, None, "tp", "fsdp"),
            P("fsdp"),
            P("tp", "fsdp"),
            P("fsdp"),
            P(None, "fsdp", "tp"),
            P("tp", "fsdp"),
            P(),
        ),
        check_vma=False,
    )
```

```python
import functools

import jax
import jax.numpy as jnp
from jax import lax
from jax.experimental import pallas as pl
from jax.experimental.pallas import tpu as pltpu
from jax.sharding import PartitionSpec as P

HD = 128
CONV = 4
PAD = 8
EPS = 1e-06
F32 = jnp.float32
BF16 = jnp.bfloat16
NN = (((1,), (0,)), ((), ()))
NT = (((1,), (1,)), ((), ()))
TN = (((0,), (0,)), ((), ()))
SCALE = HD ** (-0.5)
COST = 1.0
US = {'delta_terms': 108, 'delta_outputs': 58.5, 'mlp': 36.6, 'mlp_grads': 19.5, 'middle_back': 14.4, 'delta_back': 396, 'input_back': 1.1, 'mixer_sum': 10.5, 'mixer_total': 6.9, 'gate_up_whole': 9.9, 'mixer_whole': 8.7}
GU_BLOCKS = 6
SMALL_ROWS = 32
WIDE_ROWS = 6

ANY = pl.BlockSpec(memory_space=pl.ANY)
SMEM = pl.BlockSpec(memory_space=pltpu.SMEM)
VMEM = pl.BlockSpec(memory_space=pltpu.VMEM)


def parts_of(value, count):
    if value.dtype == BF16:
        return [value]
    pieces = []
    for left in range(count):
        piece = value.astype(BF16)
        pieces.append(piece)
        if left + 1 < count:
            value = value - piece.astype(F32)
    return pieces


def pdot(left, right, dims=NN):
    return lax.dot_general(left, right, dims, preferred_element_type=F32)


def mm_parts(lefts, rights, dims=NN):
    total = None
    for i, a in enumerate(lefts):
        for j, b in enumerate(rights):
            if i + j < max(len(lefts), len(rights)):
                term = pdot(a, b, dims)
                total = term if total is None else total + term
    return total


def mm(left, right, dims=NN, split=2):
    return mm_parts(parts_of(left, split), parts_of(right, split), dims)


def sigmoid(v):
    return 1.0 / (1.0 + jnp.exp(-v))


def iota(shape, axis):
    return lax.broadcasted_iota(jnp.int32, shape, axis)


def slots(meta, rows, axis, lengths):
    first = meta[0] * rows
    place = iota((rows, 1) if axis == 0 else (1, rows), axis) + first
    begins, end = jnp.zeros_like(place), 0
    for i in range(lengths):
        end = end + meta[2 + i]
        begins = jnp.where(end <= place, jnp.maximum(begins, end), begins)
    return begins - first, place < end


def unit_lower_inverses(lowers):
    n = lowers[0].shape[0]
    half = n // 2
    row, col = iota((half, half), 0), iota((half, half), 1)
    blocks = [low[at : at + half, at : at + half] for low in lowers for at in (0, half)]
    inverses = [jnp.where(row == col, 1.0, 0.0) - jnp.where(row // 2 == col // 2, b, 0.0) for b in blocks]
    split = [parts_of(b, 2) for b in blocks]
    zero = jnp.zeros((half, half), BF16)
    size = 2
    while size < half:
        inside = (row // (2 * size) == col // (2 * size)) & (row // size != col // size)
        pieces = [parts_of(inv, 2) for inv in inverses]
        steps = [mm_parts([jnp.where(inside, s, zero) for s in sp], pc) for sp, pc in zip(split, pieces, strict=True)]
        inverses = [inv - mm_parts(pc, parts_of(st, 2)) for inv, pc, st in zip(inverses, pieces, steps, strict=True)]
        size *= 2
    out = []
    for i, low in enumerate(lowers):
        top, bottom = inverses[2 * i], inverses[2 * i + 1]
        corner = -mm(bottom, mm(low[half:, :half], top))
        out.append((top, corner, bottom))
    return out


def conv_rows(pre, reach):
    return (pltpu.roll(pre, reach, 0) if reach else pre)[PAD:]


def conv_forward(pre, taps, age):
    total = jnp.zeros((pre.shape[0] - PAD, pre.shape[1]), F32)
    for k in range(CONV):
        reach = CONV - 1 - k
        total = total + jnp.where(age >= reach, conv_rows(pre, reach), 0.0) * taps[k : k + 1]
    return total


def pick(refs, j, *index):
    value = refs[-1][index]
    for k in range(len(refs) - 1, 0, -1):
        value = jnp.where(j == k, refs[k - 1][index], value)
    return value


def l2_ratio(values):
    return lax.rsqrt(jnp.sum(values * values, -1, keepdims=True) + EPS)


def rms_ratio(values):
    return lax.rsqrt(jnp.mean(values * values, -1, keepdims=True) + EPS)


def norm_back(values, gain, grad):
    ratio = rms_ratio(values)
    scaled = values * ratio
    weighted = grad * gain
    value_grad = ratio * (weighted - scaled * jnp.mean(weighted * scaled, -1, keepdims=True))
    return value_grad, jnp.sum(grad * scaled, 0, keepdims=True)


def terms_kernel(*refs, lengths, n_fsdp, cut):
    (meta, x_ref, gain_ref, bw_ref, taps_ref, local_ref, own_ref, one, two, three_a, three_b,
     w_ref, pre_ref, act_ref, tt_ref, y_ref, ms_ref, xt_ref, xh_ref, beta_ref, sem) = refs
    heads = w_ref.shape[0]
    d_loc = local_ref.shape[1]
    rows = x_ref.shape[0] - PAD
    ctx, fsdp = meta[0], meta[1]

    def fill(source, first, end, head, shard, skip=0):
        for i in range(3):
            start, stop = max(first, i * d_loc), min(end, (i + 1) * d_loc)
            if start < stop:
                at = pl.multiple_of(shard * d_loc + (start - i * d_loc), 16)
                target = w_ref.at[head, i, pl.ds(at, stop - start), :]
                pltpu.make_async_copy(source.at[pl.ds(start - skip, stop - start), :], target, sem).start()

    for f in range(n_fsdp):
        fill(own_ref.at[f], 0, 3 * d_loc, ctx, f)
    for j in range(1, 4):
        head = ctx ^ j
        for i in range(3):
            target = w_ref.at[head, i, pl.ds(pl.multiple_of(fsdp * d_loc, d_loc), d_loc), :]
            source = local_ref.at[i, :, pl.ds(pl.multiple_of(head * HD, HD), HD)]
            pltpu.make_async_copy(source, target, sem).start()
        for r in range(1, n_fsdp):
            shard = lax.rem(fsdp + n_fsdp - r, n_fsdp)
            if j < 3:
                fill((one, two)[j - 1].at[r - 1], 0, 3 * d_loc, head, shard)
            else:
                fill(three_a.at[r - 1], 0, cut, head, shard)
                fill(three_b.at[r - 1], cut, 3 * d_loc, head, shard, cut)

    x_wide = x_ref[...].astype(F32)
    normed = (x_wide * rms_ratio(x_wide) * gain_ref[...]).astype(BF16)
    xt_ref[...] = normed[PAD:].T
    xh_ref[...] = normed[:PAD].T
    beta = sigmoid(pdot(normed[PAD:], bw_ref[...]))
    beta_ref[...] = beta
    lb, _ = slots(meta, rows, 0, lengths)
    place = iota((rows, 1), 0)
    age = place - lb
    row, col = iota((rows, rows), 0), iota((rows, rows), 1)
    below = (col >= lb) & (col < row)
    lb_last = lb[rows - 1 :]
    last = jnp.where(place >= lb_last, 1.0, 0.0)
    keep = jnp.where(lb_last < 0, 1.0, 0.0)
    eye = jnp.where(iota((HD, HD), 0) == iota((HD, HD), 1), 1.0, 0.0)
    pltpu.make_async_copy(w_ref, w_ref, sem).wait()

    lowers, keys, scaled = [], [], []
    for h in range(heads):
        acts = []
        for i in range(3):
            pre = pdot(normed, w_ref[h, i]).astype(BF16)
            pre_ref[h, i] = pre
            total = conv_forward(pre.astype(F32), taps_ref[h, i], age)
            act = total * sigmoid(total)
            if i < 2:
                act = act * l2_ratio(act)
            acts.append(act.astype(BF16))
            act_ref[h, i] = acts[i]
        key, value = acts[1], acts[2]
        beta_h = beta[:, h : h + 1]
        lowers.append(jnp.where(below, beta_h * pdot(key, key, NT), 0.0))
        keys.append(key)
        scaled.append(beta_h * jnp.concatenate([key, value], -1).astype(F32))
    half = rows // 2
    for h, (top, corner, bottom) in enumerate(unit_lower_inverses(lowers)):
        tt_ref[h, :half, :half] = top.T
        tt_ref[h, :half, half:] = corner.T
        tt_ref[h, half:, :half] = jnp.zeros((half, half), F32)
        tt_ref[h, half:, half:] = bottom.T
        upper = mm(top, scaled[h][:half])
        lower = mm(jnp.concatenate([corner, bottom], -1), scaled[h])
        solved = jnp.concatenate([upper, lower])
        y_ref[h] = solved
        ms_ref[h, 0] = (keep * (eye - mm(solved[:, :HD], keys[h], TN))).astype(BF16)
        ms_ref[h, 1] = mm(last * solved[:, HD:], keys[h], TN).astype(BF16)


def output_kernel(*refs, lengths, sources, n_fsdp):
    (meta, y_ref, act_ref, gain_ref, local_ref, own_ref, o1, o2, o3), refs = refs[:9], refs[9:]
    arrived, (ow_ref, mixed_ref, r_ref, s_ref, n_ref, attn_ref, sem) = refs[:sources], refs[sources:]
    heads, rows = y_ref.shape[:2]
    ctx = meta[0]
    fsdp = meta[1]
    d_loc = local_ref.shape[0]

    def fill(source, head, shard):
        at = pl.multiple_of(shard * d_loc, d_loc)
        pltpu.make_async_copy(source, ow_ref.at[head, pl.ds(at, d_loc), :], sem).start()

    for j, piece in enumerate((own_ref, o1, o2, o3)):
        head = ctx ^ j
        fill(local_ref.at[:, pl.ds(pl.multiple_of(head * HD, HD), HD)], head, fsdp)
        for r in range(1, n_fsdp):
            fill(piece.at[r - 1], head, lax.rem(fsdp + n_fsdp - r, n_fsdp))
    lb, _ = slots(meta, rows, 0, lengths)
    row, col = iota((rows, rows), 0), iota((rows, rows), 1)
    upto = (col >= lb) & (col <= row)
    carried = jnp.where(lb < 0, 1.0, 0.0)
    normed = []
    for h in range(heads):
        state = jnp.zeros((HD, HD), F32)
        for c in range(sources):
            after = pick(arrived, ctx ^ c, h, 1).astype(F32)
            if c:
                after = after + mm(state, pick(arrived, ctx ^ c, h, 0))
            state = jnp.where(c < ctx, after, state)
        query, key = act_ref[h, 0], act_ref[h, 1]
        w_part, u_part = y_ref[h, :, :HD], y_ref[h, :, HD:]
        scores = jnp.where(upto, pdot(query, key, NT) * SCALE, 0.0)
        fresh = u_part - carried * mm(w_part, state, NT)
        mixed = carried * (SCALE * mm(query, state, NT)) + mm(scores, fresh)
        mixed_ref[h] = mixed
        r_ref[h] = fresh
        s_ref[h] = state
        out = (mixed * rms_ratio(mixed) * gain_ref[...]).astype(BF16)
        n_ref[:, h * HD : (h + 1) * HD] = out
        normed.append(out)
    pltpu.make_async_copy(ow_ref, ow_ref, sem).wait()
    total = pdot(normed[0], ow_ref[0], NT)
    for h in range(1, heads):
        total = total + pdot(normed[h], ow_ref[h], NT)
    attn_ref[...] = total


def mlp_kernel(*refs, lengths, n_fsdp):
    (meta, x_ref, attn_ref, other_ref, gain_ref, cot_ref, local_ref, own_ref, f1, f2, a3, b3, down_ref,
     mid_ref, nt_ref, at_ref, g_ref, gf_ref, part_ref, st_ref, w, gu, sem) = refs
    rows, width = x_ref.shape
    units = down_ref.shape[0]
    d_loc = local_ref.shape[0]
    step = GU_BLOCKS * HD
    half = step // 2
    quarters = w.shape[0]
    ctx, fsdp = meta[0], meta[1]

    def fill(source, quarter, shard, at, size):
        start = pl.multiple_of(shard * d_loc, d_loc)
        pltpu.make_async_copy(source, w.at[quarter, pl.ds(start, d_loc), pl.ds(at, size)], sem).start()

    for f in range(n_fsdp):
        fill(own_ref.at[f], ctx, f, 0, step)
    for j in range(1, 4):
        quarter = ctx ^ j
        fill(local_ref.at[:, pl.ds(pl.multiple_of(quarter * step, HD), step)], quarter, fsdp, 0, step)
        for r in range(1, n_fsdp):
            shard = lax.rem(fsdp + n_fsdp - r, n_fsdp)
            if j < 3:
                fill((f1, f2)[j - 1].at[r - 1], quarter, shard, 0, step)
            else:
                fill(a3.at[r - 1], quarter, shard, 0, half)
                fill(b3.at[r - 1], quarter, shard, half, half)

    _, inside = slots(meta, rows, 0, lengths)
    valid = jnp.where(inside, 1.0, 0.0)
    x_wide = x_ref[...].astype(F32)
    attn = (attn_ref[...] + other_ref[...]) * valid
    middle = x_wide + attn
    mid_ref[...] = middle
    for i, v in enumerate((x_wide, attn, middle)):
        st_ref[i : i + 1] = jnp.sum(valid * v * v, 0, keepdims=True)
    normed = (middle * rms_ratio(middle) * gain_ref[...]).astype(BF16)
    nt_ref[...] = normed.T
    g_ffn = (cot_ref[...].astype(F32) * valid).astype(BF16)
    gf_ref[...] = g_ffn
    g_act = pdot(g_ffn, down_ref[...], NT)
    pltpu.make_async_copy(w, w, sem).wait()
    for q in range(quarters):
        gu[:, q * step : (q + 1) * step] = pdot(normed, w[q])
    gate, up = gu[:, :units], gu[:, units : 2 * units]
    sig = sigmoid(gate)
    act = (gate * sig * up).astype(BF16)
    at_ref[...] = act.T
    g_up = g_act * gate * sig
    g_gate = g_act * up * sig * (1.0 + gate * (1.0 - sig))
    gu[:, :units] = g_gate
    gu[:, units : 2 * units] = g_up
    part = None
    for q in range(quarters):
        real = min(step, 2 * units - q * step)
        grad = gu[:, q * step : q * step + real].astype(BF16)
        if real < step:
            grad = jnp.concatenate([grad, jnp.zeros((rows, step - real), BF16)], -1)
        g_ref[ctx ^ q] = grad
        term = pdot(grad, w[q], NT)
        part = term if part is None else part + term
    part_ref[:rows] = part
    part_ref[rows:] = pdot(act, down_ref[...])


def mlp_grads_kernel(nt_ref, g_ref, at_ref, gf_ref, x3_ref, y3_ref, x1_ref, y2_ref, late_x_ref, late_y_ref, own_ref, down_ref):
    half = g_ref.shape[2] // 2
    nt = nt_ref[...]

    def put(ref, j, side):
        ref[...] = pdot(nt, g_ref[j, :, side * half : (side + 1) * half]).astype(BF16)

    put(x3_ref, 3, 0)
    put(y3_ref, 3, 1)
    put(x1_ref, 1, 0)
    put(y2_ref, 2, 1)
    put(late_x_ref, 1, 1)
    put(late_y_ref, 2, 0)
    put(own_ref.at[0], 0, 0)
    put(own_ref.at[1], 0, 1)
    down_ref[...] = pdot(at_ref[...], gf_ref[...]).astype(BF16)


def middle_kernel(
    meta, part_ref, other_ref, mid_ref, cot_ref, gain_ref, hgain_ref, ow_ref, n_ref, mixed_ref, act_ref, y_ref,
    out_ref, gm_ref, og_ref, do_ref, dr_ref, ds_ref, sm_ref, *, lengths
):
    heads, rows = mixed_ref.shape[:2]
    ctx = meta[0]
    lb, inside = slots(meta, rows, 0, lengths)
    lb_row, _ = slots(meta, rows, 1, lengths)
    valid = jnp.where(inside, 1.0, 0.0)
    row, col = iota((rows, rows), 0), iota((rows, rows), 1)
    upto = (row >= lb_row) & (row <= col)
    carried = jnp.where(lb < 0, 1.0, 0.0)
    middle = mid_ref[...]
    value_grad, gain_grad = norm_back(middle, gain_ref[...], part_ref[:rows] + other_ref[:rows])
    g_middle = cot_ref[...].astype(F32) + value_grad
    gm_ref[...] = g_middle
    g_attn = (g_middle * valid).astype(BF16)
    turned_grad = g_attn.T
    total = jnp.zeros((1, HD), F32)
    for h in range(heads):
        key = act_ref[h, 1]
        g_head = pdot(g_attn, ow_ref[h])
        d_mixed, part = norm_back(mixed_ref[h], hgain_ref[...], g_head)
        total = total + part
        turned = jnp.where(upto, pdot(key, act_ref[h, 0], NT) * SCALE, 0.0)
        d_fresh = mm(turned, d_mixed)
        do_ref[h] = d_mixed
        dr_ref[h] = d_fresh
        d_state = SCALE * mm(carried * d_mixed, act_ref[h, 0], TN) - mm(carried * d_fresh, y_ref[h, :, :HD], TN)
        ds_ref[h] = d_state.astype(BF16)
        og_ref[ctx ^ h] = pdot(turned_grad, n_ref[:, h * HD : (h + 1) * HD]).astype(BF16)
    ffn = (part_ref[rows:] + other_ref[rows:]) * valid
    result = middle + ffn
    out_ref[...] = result.astype(BF16)
    sm_ref[...] = jnp.zeros_like(sm_ref)
    sm_ref[0:1] = gain_grad
    sm_ref[1:2, :HD] = total
    sm_ref[2:3] = jnp.sum(valid * ffn * ffn, 0, keepdims=True)
    sm_ref[3:4] = jnp.sum(valid * result * result, 0, keepdims=True)
    sm_ref[4:5] = jnp.broadcast_to(jnp.sum(valid, 0, keepdims=True), gain_grad.shape) / gain_grad.shape[1]


def delta_back_kernel(*refs, lengths, sources):
    meta, grads, maps = refs[0], refs[1 : 1 + sources], refs[1 + sources : 1 + 2 * sources]
    (pre_ref, act_ref, tt_ref, y_ref, r_ref, s_ref, do_ref, dr_ref, beta_ref, taps_ref, w_ref, bw_ref, xt_ref, xh_ref, sm_ref, og_ref,
     keep_ref, x_ref, y2_ref, late_x_ref, late_y_ref, part_ref, bg_ref, cg_ref) = refs[1 + 2 * sources :]
    heads, rows = r_ref.shape[:2]
    width = w_ref.shape[2]
    ext = rows + PAD
    ctx = meta[0]
    lb, _ = slots(meta, rows, 0, lengths)
    lb_row, _ = slots(meta, rows, 1, lengths)
    place = iota((rows, 1), 0)
    age = place - lb
    row, col = iota((rows, rows), 0), iota((rows, rows), 1)
    last = jnp.where(place >= lb[rows - 1 :], 1.0, 0.0)
    carried = jnp.where(lb < 0, 1.0, 0.0)
    upto = (col >= lb) & (col <= row)
    below = (col >= lb) & (col < row)
    turned_upto = (row >= lb_row) & (row <= col)
    lane = iota((rows, HD), 1)
    logits = jnp.zeros((rows, HD), F32)
    top = jnp.zeros((PAD, HD), F32)
    xt, xh = xt_ref[...], xh_ref[...]
    part = jnp.zeros((rows, width), F32)
    ahead = jnp.zeros((PAD, width), F32)
    for h in range(heads):
        d_state = jnp.zeros((HD, HD), F32)
        for c in range(sources, 0, -1):
            before = pick(grads, ctx ^ c, h).astype(F32)
            if c < sources:
                before = before + mm(d_state, pick(maps, ctx ^ c, h, 0), NT)
            d_state = jnp.where(c > ctx, before, d_state)
        query, key, value = act_ref[h, 0], act_ref[h, 1], act_ref[h, 2]
        solved = y_ref[h]
        fresh, state, d_mixed = r_ref[h], s_ref[h], do_ref[h]
        beta = beta_ref[:, h : h + 1]
        d_fresh = dr_ref[h] + last * mm(key, d_state, NT)
        d_scores = jnp.where(upto, SCALE * mm(d_mixed, fresh, NT), 0.0)
        turned = jnp.where(turned_upto, SCALE * mm(fresh, d_mixed, NT), 0.0)
        d_query = mm(d_scores, key) + carried * (SCALE * mm(d_mixed, state))
        d_key = mm(turned, query) + mm(last * fresh, d_state)
        d_solved = jnp.concatenate([-carried * mm(d_fresh, state), d_fresh], -1)
        d_scaled = mm(tt_ref[h], d_solved)
        d_value = beta * d_scaled[:, HD:]
        d_key = d_key + beta * d_scaled[:, :HD]
        d_beta = jnp.sum(d_scaled[:, :HD] * key.astype(F32) + d_scaled[:, HD:] * value.astype(F32), -1, keepdims=True)
        d_lower = jnp.where(below, -mm(d_scaled, solved, NT), 0.0)
        d_beta = d_beta + jnp.sum(d_lower * pdot(key, key, NT), -1, keepdims=True)
        d_gram = beta * d_lower
        d_key = d_key + mm(d_gram, key) + mm(d_gram, key, TN)
        logits = jnp.where(lane == h, d_beta * beta * (1.0 - beta), logits)
        g_main, g_head = [], []
        for i, grad in enumerate((d_query, d_key, d_value)):
            taps = taps_ref[h, i]
            pre = pre_ref[h, i].astype(F32)
            total = conv_forward(pre, taps, age)
            sig = sigmoid(total)
            if i < 2:
                act = total * sig
                ratio = l2_ratio(act)
                unit = act * ratio
                grad = ratio * (grad - unit * jnp.sum(grad * unit, -1, keepdims=True))
            grad = grad * sig * (1.0 + total * (1.0 - sig))
            back = jnp.zeros((ext, HD), F32)
            for k in range(CONV):
                reach = CONV - 1 - k
                grad_k = jnp.where(age >= reach, grad, 0.0)
                cg_ref[h, i * CONV + k : i * CONV + k + 1, :] = jnp.sum(grad_k * conv_rows(pre, reach), 0, keepdims=True)
                padded = jnp.concatenate([top, grad_k])
                back = back + (pltpu.roll(padded, ext - reach, 0) if reach else padded) * taps[k : k + 1]
            g_main.append(back[PAD:].astype(BF16))
            g_head.append(back[:PAD].astype(BF16))
            part = part + pdot(g_main[i], w_ref[h, i], NT)
            ahead = ahead + pdot(g_head[i], w_ref[h, i], NT)
        piece = pdot(xt, jnp.concatenate(g_main, -1)) + pdot(xh, jnp.concatenate(g_head, -1))
        piece = piece.astype(BF16)
        places = (
            (keep_ref.at[0], keep_ref.at[1]),
            (x_ref.at[1], late_x_ref),
            (late_y_ref, y2_ref.at[1]),
            (x_ref.at[0], y2_ref.at[0]),
        )
        for j, (a, b) in enumerate(places):

            @pl.when(ctx ^ j == h)
            def _(a=a, b=b, j=j, piece=piece):
                a[...] = piece[:, : 2 * HD]
                b[:, :HD] = piece[:, 2 * HD :]
                b[:, HD:] = og_ref[j]

    logits = logits.astype(BF16)
    part_ref[:rows] = part + pdot(logits, bw_ref[...], NT)
    part_ref[rows:ext] = ahead
    part_ref[ext:] = jnp.zeros((PAD, width), F32)
    part_ref[ext : ext + 1, :HD] = sm_ref[1:2, :HD]
    bg_ref[...] = lax.dot_general(logits, xt, (((0,), (1,)), ((), ())), preferred_element_type=F32)[:PAD]


def last_kernel(x_ref, gain_ref, part_ref, other_ref, rim_ref, gm_ref, sm_ref, st_ref, bg_ref, cg_ref, grad_ref, small_ref):
    rows, width = x_ref.shape
    heads = cg_ref.shape[0]
    total = part_ref[...] + other_ref[...]
    grad = jnp.concatenate([total[: rows - PAD], total[rows - PAD : rows] + rim_ref[...]])
    value_grad, gain_grad = norm_back(x_ref[...].astype(F32), gain_ref[...], grad)
    grad_ref[...] = gm_ref[...] + value_grad
    small_ref[...] = jnp.zeros_like(small_ref)
    small_ref[0:1] = gain_grad
    small_ref[1:2] = sm_ref[0:1]
    small_ref[2 : 2 + heads] = bg_ref[:heads]
    small_ref[6:9] = st_ref[0:3]
    small_ref[9:11] = sm_ref[2:4]
    small_ref[11:12] = sm_ref[4:5]
    at = WIDE_ROWS + 6
    for h in range(heads):
        small_ref[at : at + 3 * CONV, h * HD : (h + 1) * HD] = cg_ref[h, : 3 * CONV]
    at += 3 * CONV
    small_ref[at : at + 1, :HD] = total[rows + PAD : rows + PAD + 1, :HD]


def mixer_sum_kernel(meta, keep_ref, x_ref, y_ref, late_y_ref, late_x_ref, s0, s1, s2, s3, *outs, n_fsdp):
    width, half = x_ref.shape[1:]
    d_loc = width // n_fsdp
    grouped = len(outs) < n_fsdp
    small = (s0[...] + s1[...]) + (s2[...] + s3[...])
    rows, lanes = iota((SMALL_ROWS, 2 * half), 0), iota((SMALL_ROWS, 2 * half), 1)
    stats = jnp.sum(small, -1, keepdims=True)
    high = stats.astype(BF16).astype(F32)
    common = jnp.where(rows < WIDE_ROWS + 6, jnp.where(lanes < half + HD, high, stats - high), small[:, : 2 * half])
    for r in range(n_fsdp):
        shard = r if grouped else lax.rem(meta[1] + r, n_fsdp)
        ref, first = (outs[0], r * (d_loc + SMALL_ROWS)) if grouped else (outs[r], 0)
        at = pl.ds(r * d_loc if grouped else pl.multiple_of(shard * d_loc, d_loc), d_loc)
        a = keep_ref[0, at, :].astype(F32) + x_ref[1, at, :].astype(F32) + late_y_ref[at, :].astype(F32)
        b = keep_ref[1, at, :].astype(F32) + y_ref[1, at, :].astype(F32) + late_x_ref[at, :].astype(F32)
        ref[first : first + d_loc, :half] = a.astype(BF16)
        ref[first : first + d_loc, half:] = b.astype(BF16)
        slices = [small[:, k * d_loc : (k + 1) * d_loc] for k in ([r] if grouped else range(n_fsdp))]
        mine = slices[0]
        for k in range(1, len(slices)):
            mine = jnp.where(shard == k, slices[k], mine)
        mine = jnp.concatenate([mine, jnp.zeros((SMALL_ROWS, 2 * half - d_loc), F32)], -1)
        ref[first + d_loc : first + d_loc + SMALL_ROWS] = jnp.where(rows < WIDE_ROWS, mine, common).astype(BF16)


def mixer_total_kernel(meta, own_ref, *refs, width):
    far, (mix_ref, first_ref, second_ref, beta_ref, conv_ref, head_ref, rms_ref) = refs[:-7], refs[-7:]
    count, rows = len(far) + 1, mix_ref.shape[0]
    heads, hd_loc = conv_ref.shape[1:]
    total = None
    for f in range(count):
        part = own_ref[...]
        for r, ref in enumerate(far):
            part = jnp.where(lax.rem(meta[1] + count - (r + 1), count) == f, ref[...], part)
        part = part.astype(F32)
        total = part if total is None else total + part
    mix_ref[...] = total[:rows].astype(BF16)
    small = total[rows:]
    first_ref[...] = small[0:1, :rows]
    second_ref[...] = small[1:2, :rows]
    beta_ref[...] = small[:8, :rows].T[:, 2 : 2 + heads]
    for h in range(heads):
        lanes = small[WIDE_ROWS + 6 :, h * HD : (h + 1) * HD]
        mine = lanes[:, :hd_loc]
        for k in range(1, HD // hd_loc):
            mine = jnp.where(meta[1] == k, lanes[:, k * hd_loc : (k + 1) * hd_loc], mine)
        conv_ref[:, h, :] = mine[: 3 * CONV]
        if h == 0:
            head_ref[...] = mine[3 * CONV : 3 * CONV + 1]
    stats = small[WIDE_ROWS : WIDE_ROWS + 6, 2 * HD : 2 * HD + 1] + small[WIDE_ROWS : WIDE_ROWS + 6, 3 * HD : 3 * HD + 1]
    rms_ref[...] = jnp.sqrt(stats[:5] / (stats[5:] * width))


def gate_up_whole_kernel(p_ref, d0, d1, e0, e1, gu_ref, down_ref):
    units = gu_ref.shape[2]
    down_ref[: d0.shape[0]] = d0[...].astype(F32) + d1[...].astype(F32)
    down_ref[d0.shape[0] :] = e0[...].astype(F32) + e1[...].astype(F32)
    for q in range(p_ref.shape[0]):
        for k in range(GU_BLOCKS):
            at = (q * GU_BLOCKS + k) * HD
            if at < 2 * units:
                gu_ref[at // units, :, at % units : at % units + HD] = p_ref[q, :, k * HD : (k + 1) * HD].astype(F32)


def mixer_whole_kernel(meta, p0, p1, p2, p3, qkv_ref, out_ref):
    ctx = meta[0]
    for q in range(4):
        for j, ref in enumerate((p0, p1, p2, p3)):

            @pl.when(ctx ^ j == q)
            def _(ref=ref, q=q):
                for i in range(3):
                    qkv_ref[i, :, q * HD : (q + 1) * HD] = ref[:, i * HD : (i + 1) * HD].astype(F32)
                out_ref[q * HD : (q + 1) * HD, :] = ref[:, 3 * HD :].T.astype(F32)


def sds(*shape, dtype=F32):
    return jax.ShapeDtypeStruct(shape, dtype)


def call(body, name, out_shape, in_specs, args, scratch=(), gflops=1, mbytes=4):
    return pl.pallas_call(
        body,
        name=name,
        in_specs=in_specs,
        out_specs=jax.tree.map(lambda _: VMEM, out_shape),
        out_shape=out_shape,
        scratch_shapes=list(scratch),
        compiler_params=pltpu.CompilerParams(vmem_limit_bytes=56 * 1024 * 1024),
        cost_estimate=pl.CostEstimate(flops=int(COST * US[name] * 1_150_000_000), bytes_accessed=10**6, transcendentals=0),
    )(*args)


def shifted(value, axis, steps):
    count = lax.axis_size(axis)
    first, end = max(0, -steps), min(count, count - steps)
    return lax.ppermute(value, axis, [(s, s + steps) for s in range(first, end)])


def swapped(value, axis, mask):
    return lax.ppermute(value, axis, [(s, s ^ mask) for s in range(lax.axis_size(axis))])


def far_shards(value):
    count = lax.axis_size("fsdp")
    if count <= 4:
        turns = [[(s, (s + r) % count) for s in range(count)] for r in range(1, count)]
        return [lax.ppermute(value, "fsdp", turn)[None] for turn in turns]
    return [others(lax.all_gather(value, "fsdp", axis=0))]


def others(value):
    return jnp.concatenate([other(value, r) for r in range(1, lax.axis_size("fsdp"))])


def other(value, r):
    count, here = lax.axis_size("fsdp"), lax.axis_index("fsdp")
    return lax.dynamic_index_in_dim(value, (here + count - r) % count, 0)


def local(
    tokens, lengths, norm_gain, qkv_weight, beta_weight, conv_weight, head_gain, out_weight, mlp_gain, gate_up_weight, down_weight, cotangent
):
    rows, width = tokens.shape
    n_ctx, n_fsdp = lax.axis_size("ctx"), lax.axis_size("fsdp")
    ctx, fsdp = lax.axis_index("ctx"), lax.axis_index("fsdp")
    d_loc = qkv_weight.shape[1]
    heads = beta_weight.shape[1]
    units = down_weight.shape[0]
    hd_loc = head_gain.shape[0]
    n_len = lengths.shape[1]
    step = GU_BLOCKS * HD
    ext = rows + PAD
    meta = jnp.concatenate([jnp.stack([ctx, fsdp]).astype(jnp.int32), lengths[0]])

    small = jnp.concatenate([norm_gain, mlp_gain, head_gain, beta_weight.reshape(-1), conv_weight.reshape(-1)])
    small_rows = -(-small.shape[0] // (HD * 16)) * 16
    small = jnp.pad(small, (0, small_rows * HD - small.shape[0])).reshape(small_rows, HD)
    qkv_part = lax.dynamic_slice_in_dim(qkv_weight, ctx * HD, HD, 2).reshape(3 * d_loc, HD)
    out_part = lax.dynamic_slice_in_dim(out_weight, ctx * HD, HD, 0).T
    pack = jnp.concatenate([qkv_part, small])
    packs = lax.all_gather(pack, "fsdp", axis=0)
    pack_far = others(packs)
    out_local = out_weight.T
    gu_local = jnp.concatenate(
        [gate_up_weight[0], gate_up_weight[1], jnp.zeros((d_loc, n_ctx * step - 2 * units), BF16)], -1
    )
    gu_part = lax.dynamic_slice_in_dim(gu_local, ctx * step, step, 1)
    gu_own = lax.all_gather(gu_part, "fsdp", axis=0)
    gu_far = others(gu_own)
    down_full = lax.all_gather(down_weight, "fsdp", axis=1, tiled=True)
    x_ext = jnp.concatenate([shifted(tokens[rows - PAD :], "ctx", 1), tokens])

    cut = 3 * d_loc // 2
    pack_far, out_part = lax.optimization_barrier((pack_far, out_part))
    one, two = swapped(pack_far, "ctx", 1), swapped(pack_far, "ctx", 2)
    out_far = far_shards(out_part)
    three_a, three_b = swapped(one[:, :cut], "ctx", 2), swapped(two[:, cut:], "ctx", 1)
    three_a, three_b, out_far = lax.optimization_barrier((three_a, three_b, out_far))
    out_far = jnp.concatenate(out_far)
    out_pieces = [swapped(out_far, "ctx", j) for j in range(1, n_ctx)]

    flat = packs[:, 3 * d_loc :].reshape(n_fsdp, -1)
    at = 0
    first_gain = flat[:, at : at + d_loc].reshape(1, width).astype(F32)
    at += d_loc
    second_gain = flat[:, at : at + d_loc].reshape(1, width).astype(F32)
    at += d_loc
    head_full = flat[:, at : at + hd_loc].reshape(1, HD).astype(F32)
    at += hd_loc
    beta_full = jnp.pad(flat[:, at : at + d_loc * heads].reshape(width, heads), ((0, 0), (0, HD - heads)))
    at += d_loc * heads
    conv_full = flat[:, at : at + 3 * CONV * heads * hd_loc].reshape(n_fsdp, 3, CONV, heads, hd_loc)
    conv_full = conv_full.transpose(3, 1, 2, 0, 4).reshape(heads, 3, CONV, HD).astype(F32)

    qkv_full, pre, acts, turned, solved, ends_map, normed_t, normed_far, beta = call(
        functools.partial(terms_kernel, lengths=n_len, n_fsdp=n_fsdp, cut=cut),
        "delta_terms",
        (
            sds(heads, 3, width, HD, dtype=BF16),
            sds(heads, 3, ext, HD, dtype=BF16),
            sds(heads, 3, rows, HD, dtype=BF16),
            sds(heads, rows, rows),
            sds(heads, rows, 2 * HD),
            sds(heads, 2, HD, HD, dtype=BF16),
            sds(width, rows, dtype=BF16),
            sds(width, PAD, dtype=BF16),
            sds(rows, HD),
        ),
        [SMEM] + [VMEM] * 4 + [ANY] * 6,
        (meta, x_ext, first_gain, beta_full, conv_full, qkv_weight, packs, one, two, three_a, three_b),
        [pltpu.SemaphoreType.DMA],
        gflops=15,
        mbytes=8,
    )
    arrived = [swapped(ends_map, "ctx", j) for j in range(1, n_ctx)]
    gu_one, gu_two = lax.optimization_barrier((swapped(gu_far, "ctx", 1), swapped(gu_far, "ctx", 2)))
    gu_three = (swapped(gu_one[:, :, : step // 2], "ctx", 2), swapped(gu_two[:, :, step // 2 :], "ctx", 1))
    out_full, mixed, fresh, state, head_out, attn_part = call(
        functools.partial(output_kernel, lengths=n_len, sources=n_ctx - 1, n_fsdp=n_fsdp),
        "delta_outputs",
        (
            sds(heads, width, HD, dtype=BF16),
            sds(heads, rows, HD),
            sds(heads, rows, HD),
            sds(heads, HD, HD),
            sds(rows, heads * HD, dtype=BF16),
            sds(rows, width),
        ),
        [SMEM] + [VMEM] * 3 + [ANY] * (1 + n_ctx) + [VMEM] * len(arrived),
        (meta, solved, acts, head_full, out_local, out_far, *out_pieces, *arrived),
        [pltpu.SemaphoreType.DMA],
        gflops=6,
        mbytes=6,
    )
    attn_other = swapped(attn_part, "tp", 1)

    middle, normed_mid_t, act_t, g_gu, g_ffn, mlp_part, stats = call(
        functools.partial(mlp_kernel, lengths=n_len, n_fsdp=n_fsdp),
        "mlp",
        (
            sds(rows, width),
            sds(width, rows, dtype=BF16),
            sds(units, rows, dtype=BF16),
            sds(n_ctx, rows, step, dtype=BF16),
            sds(rows, width, dtype=BF16),
            sds(2 * rows, width),
            sds(8, width),
        ),
        [SMEM] + [VMEM] * 5 + [ANY] * 6 + [VMEM],
        (
            meta, tokens, attn_part, attn_other, second_gain, cotangent, gu_local, gu_own, gu_one, gu_two, *gu_three, down_full,
        ),
        [pltpu.VMEM((n_ctx, width, step), BF16), pltpu.VMEM((rows, n_ctx * step), F32), pltpu.SemaphoreType.DMA],
        gflops=10,
        mbytes=14,
    )
    mlp_other = swapped(mlp_part, "tp", 1)
    quarter = sds(width, step // 2, dtype=BF16)
    double = sds(2, width, step // 2, dtype=BF16)
    gu_grads = call(
        mlp_grads_kernel,
        "mlp_grads",
        (quarter,) * 6 + (double, sds(units, width, dtype=BF16)),
        [VMEM] * 4,
        (normed_mid_t, g_gu, act_t, g_ffn),
        gflops=4,
        mbytes=12,
    )
    mlp_other, gu_grads = lax.optimization_barrier((mlp_other, gu_grads))
    gu_x3, gu_y3, gu_x1, gu_y2, gu_late_x, gu_late_y, gu_keep, down_grad = gu_grads
    from_x3, from_y3 = swapped(gu_x3, "ctx", 1), swapped(gu_y3, "ctx", 2)

    result, g_middle, out_grads, d_mixed, d_fresh, d_state, sums = call(
        functools.partial(middle_kernel, lengths=n_len),
        "middle_back",
        (
            sds(rows, width, dtype=BF16),
            sds(rows, width),
            sds(n_ctx, width, HD, dtype=BF16),
            sds(heads, rows, HD),
            sds(heads, rows, HD),
            sds(heads, HD, HD, dtype=BF16),
            sds(8, width),
        ),
        [SMEM] + [VMEM] * 11,
        (
            meta, mlp_part, mlp_other, middle, cotangent, second_gain, head_full, out_full, head_out, mixed, acts,
            solved,
        ),
        gflops=6,
        mbytes=12,
    )
    behind = [swapped(d_state, "ctx", j) for j in range(1, n_ctx)]

    down_sh = lax.psum_scatter(down_grad, "fsdp", scatter_dimension=1, tiled=True)

    def add(left, right):
        return (left.astype(F32) + right.astype(F32)).astype(BF16)

    gu_x1, gu_y2, _ = lax.optimization_barrier((gu_x1, gu_y2, d_state))
    from_x1, from_y2 = swapped(gu_x1, "ctx", 1), swapped(gu_y2, "ctx", 2)
    gu_late_y, gu_late_x = add(gu_late_y, from_x3), add(gu_late_x, from_y3)
    behind, gu_late_x, gu_late_y = lax.optimization_barrier((behind, gu_late_x, gu_late_y))
    gu_late_y, gu_late_x = swapped(gu_late_y, "ctx", 2), swapped(gu_late_x, "ctx", 1)
    half = sds(width, 2 * HD, dtype=BF16)
    double = sds(2, width, 2 * HD, dtype=BF16)
    back = call(
        functools.partial(delta_back_kernel, lengths=n_len, sources=n_ctx - 1),
        "delta_back",
        (double, double, double, half, half, sds(ext + PAD, width), sds(PAD, width), sds(heads, 16, HD)),
        [SMEM] + [VMEM] * (2 * n_ctx - 2 + 16),
        (
            meta, *behind, *arrived, pre, acts, turned, solved, fresh, state, d_mixed, d_fresh, beta, conv_full, qkv_full, beta_full,
            normed_t, normed_far, sums, out_grads,
        ),
        gflops=16,
        mbytes=16,
    )

    mix_keep, mix_x, mix_y, mix_late_x, mix_late_y, in_part, beta_grad, conv_grad = back
    from_x1, from_y2, gu_late_x, gu_late_y, mix_keep, down_sh = lax.optimization_barrier(
        (from_x1, from_y2, gu_late_x, gu_late_y, mix_keep, down_sh)
    )
    in_other = swapped(in_part, "tp", 1)
    rim = shifted(in_part[rows:ext] + in_other[rows:ext], "ctx", -1)
    mix_from_x, mix_from_y = swapped(mix_x, "ctx", 1), swapped(mix_y, "ctx", 2)
    mix_from_x, mix_from_y, rim, down_sh = lax.optimization_barrier((mix_from_x, mix_from_y, rim, down_sh))
    input_grad, smalls = call(
        last_kernel,
        "input_back",
        (sds(rows, width), sds(SMALL_ROWS, width)),
        [VMEM] * 10,
        (tokens, first_gain, in_part, in_other, rim, g_middle, sums, stats, beta_grad, conv_grad),
        gflops=1,
        mbytes=6,
    )
    small_pieces = [smalls] + [swapped(smalls, "ctx", j) for j in range(1, n_ctx)]
    gu_sum = [
        (gu_keep[0].astype(F32) + from_x1.astype(F32) + gu_late_y.astype(F32)).astype(BF16),
        (gu_keep[1].astype(F32) + from_y2.astype(F32) + gu_late_x.astype(F32)).astype(BF16),
    ]
    gu_sh = lax.psum_scatter(jnp.concatenate(gu_sum, -1), "fsdp", scatter_dimension=0, tiled=True)

    mix_late_y, mix_late_x = add(mix_late_y, mix_from_x[0]), add(mix_late_x, mix_from_y[0])
    mix_late_y, mix_late_x = lax.optimization_barrier((swapped(mix_late_y, "ctx", 2), swapped(mix_late_x, "ctx", 1)))
    side = units // 2
    down_a, down_b = down_sh[:side], down_sh[side:]
    down_other = swapped(down_a, "ctx", 1), swapped(down_b, "ctx", 2)
    count = n_fsdp if n_fsdp <= 4 else 1
    mix_rows = n_fsdp // count * (d_loc + SMALL_ROWS)
    mix_own, *mix_far = call(
        functools.partial(mixer_sum_kernel, n_fsdp=n_fsdp),
        "mixer_sum",
        (sds(mix_rows, 4 * HD, dtype=BF16),) * count,
        [SMEM] + [VMEM] * (5 + n_ctx),
        (meta, mix_keep, mix_from_x, mix_from_y, mix_late_y, mix_late_x, *small_pieces),
        gflops=1,
        mbytes=6,
    )
    mix_own, down_other, gu_sh = lax.optimization_barrier((mix_own, down_other, gu_sh))
    down_a, down_b = add(down_a, down_other[0]), add(down_b, down_other[1])
    down_parts = (down_a, swapped(down_a, "ctx", 2), down_b, swapped(down_b, "ctx", 1))
    gu_all = lax.all_gather(gu_sh, "ctx", axis=0)
    if count > 1:
        turns = [[(i, (i + r) % n_fsdp) for i in range(n_fsdp)] for r in range(1, n_fsdp)]
        mix_far = [lax.ppermute(part, "fsdp", turn) for part, turn in zip(mix_far, turns, strict=True)]
        mix_far, down_parts = lax.optimization_barrier((mix_far, down_parts))
    else:
        mix_own = lax.psum_scatter(mix_own, "fsdp", scatter_dimension=0, tiled=True)
    mix_sh, first_out, second_out, beta_out, conv_out, head_out_grad, rms = call(
        functools.partial(mixer_total_kernel, width=width),
        "mixer_total",
        (
            sds(d_loc, 4 * HD, dtype=BF16),
            sds(1, d_loc),
            sds(1, d_loc),
            sds(d_loc, heads),
            sds(3 * CONV, heads, hd_loc),
            sds(1, hd_loc),
            sds(5, 1),
        ),
        [SMEM] + [VMEM] * count,
        (meta, mix_own, *mix_far),
        gflops=1,
        mbytes=1,
    )
    def pieces(part):
        return [part] + [swapped(part, "ctx", j) for j in range(1, n_ctx)]

    gu_out, down_out = call(
        gate_up_whole_kernel,
        "gate_up_whole",
        (sds(2, d_loc, units), sds(units, d_loc)),
        [VMEM] * 5,
        (gu_all, *down_parts),
        gflops=1,
        mbytes=6,
    )
    qkv_out, out_out = call(
        mixer_whole_kernel,
        "mixer_whole",
        (sds(3, d_loc, heads * HD), sds(heads * HD, d_loc)),
        [SMEM] + [VMEM] * n_ctx,
        (meta, *pieces(mix_sh)),
        gflops=1,
        mbytes=4,
    )
    return (
        result,
        input_grad,
        first_out.reshape(-1),
        qkv_out,
        beta_out,
        conv_out.reshape(3, CONV, heads, hd_loc),
        head_out_grad.reshape(-1),
        out_out,
        second_out.reshape(-1),
        gu_out,
        down_out,
        rms.reshape(-1),
    )


def solution(mesh):
    return jax.shard_map(
        local,
        mesh=mesh,
        in_specs=(
            P(("fsdp", "ctx"), None),
            P("fsdp", None),
            P("fsdp"),
            P(None, "fsdp", "tp"),
            P("fsdp", "tp"),
            P(None, None, "tp", "fsdp"),
            P("fsdp"),
            P("tp", "fsdp"),
            P("fsdp"),
            P(None, "fsdp", "tp"),
            P("tp", "fsdp"),
            P(("fsdp", "ctx"), None),
        ),
        out_specs=(
            P(("fsdp", "ctx"), None),
            P(("fsdp", "ctx"), None),
            P("fsdp"),
            P(None, "fsdp", "tp"),
            P("fsdp", "tp"),
            P(None, None, "tp", "fsdp"),
            P("fsdp"),
            P("tp", "fsdp"),
            P("fsdp"),
            P(None, "fsdp", "tp"),
            P("tp", "fsdp"),
            P(),
        ),
        check_vma=False,
    )
```

```python
import functools

import jax
import jax.numpy as jnp
from jax import lax
from jax.experimental import pallas as pl
from jax.experimental.pallas import tpu as pltpu
from jax.sharding import PartitionSpec as P

HD = 128
CONV = 4
PAD = 8
EPS = 1e-06
F32 = jnp.float32
BF16 = jnp.bfloat16
NN = (((1,), (0,)), ((), ()))
NT = (((1,), (1,)), ((), ()))
TN = (((0,), (0,)), ((), ()))
SCALE = HD ** (-0.5)
COST = 1.0
US = {'delta_terms': 108, 'delta_outputs': 58.5, 'mlp': 36.6, 'mlp_grads': 19.5, 'middle_back': 14.4, 'delta_back': 396, 'input_back': 1.1, 'mixer_sum': 10.5, 'mixer_total': 6.9, 'gate_up_whole': 9.9, 'mixer_whole': 8.7}
GU_BLOCKS = 6
SMALL_ROWS = 32
WIDE_ROWS = 6

ANY = pl.BlockSpec(memory_space=pl.ANY)
SMEM = pl.BlockSpec(memory_space=pltpu.SMEM)
VMEM = pl.BlockSpec(memory_space=pltpu.VMEM)


def parts_of(value, count):
    if value.dtype == BF16:
        return [value]
    pieces = []
    for left in range(count):
        piece = value.astype(BF16)
        pieces.append(piece)
        if left + 1 < count:
            value = value - piece.astype(F32)
    return pieces


def pdot(left, right, dims=NN):
    return lax.dot_general(left, right, dims, preferred_element_type=F32)


def mm_parts(lefts, rights, dims=NN):
    total = None
    for i, a in enumerate(lefts):
        for j, b in enumerate(rights):
            if i + j < max(len(lefts), len(rights)):
                term = pdot(a, b, dims)
                total = term if total is None else total + term
    return total


def mm(left, right, dims=NN, split=2):
    return mm_parts(parts_of(left, split), parts_of(right, split), dims)


def sigmoid(v):
    return 1.0 / (1.0 + jnp.exp(-v))


def iota(shape, axis):
    return lax.broadcasted_iota(jnp.int32, shape, axis)


def slots(meta, rows, axis, lengths):
    first = meta[0] * rows
    place = iota((rows, 1) if axis == 0 else (1, rows), axis) + first
    begins, end = jnp.zeros_like(place), 0
    for i in range(lengths):
        end = end + meta[2 + i]
        begins = jnp.where(end <= place, jnp.maximum(begins, end), begins)
    return begins - first, place < end


def unit_lower_inverses(lowers):
    n = lowers[0].shape[0]
    half = n // 2
    row, col = iota((half, half), 0), iota((half, half), 1)
    blocks = [low[at : at + half, at : at + half] for low in lowers for at in (0, half)]
    inverses = [jnp.where(row == col, 1.0, 0.0) - jnp.where(row // 2 == col // 2, b, 0.0) for b in blocks]
    split = [parts_of(b, 2) for b in blocks]
    zero = jnp.zeros((half, half), BF16)
    size = 2
    while size < half:
        inside = (row // (2 * size) == col // (2 * size)) & (row // size != col // size)
        pieces = [parts_of(inv, 2) for inv in inverses]
        steps = [mm_parts([jnp.where(inside, s, zero) for s in sp], pc) for sp, pc in zip(split, pieces, strict=True)]
        inverses = [inv - mm_parts(pc, parts_of(st, 2)) for inv, pc, st in zip(inverses, pieces, steps, strict=True)]
        size *= 2
    out = []
    for i, low in enumerate(lowers):
        top, bottom = inverses[2 * i], inverses[2 * i + 1]
        corner = -mm(bottom, mm(low[half:, :half], top))
        out.append((top, corner, bottom))
    return out


def conv_rows(pre, reach):
    return (pltpu.roll(pre, reach, 0) if reach else pre)[PAD:]


def conv_forward(pre, taps, age):
    total = jnp.zeros((pre.shape[0] - PAD, pre.shape[1]), F32)
    for k in range(CONV):
        reach = CONV - 1 - k
        total = total + jnp.where(age >= reach, conv_rows(pre, reach), 0.0) * taps[k : k + 1]
    return total


def pick(refs, j, *index):
    value = refs[-1][index]
    for k in range(len(refs) - 1, 0, -1):
        value = jnp.where(j == k, refs[k - 1][index], value)
    return value


def l2_ratio(values):
    return lax.rsqrt(jnp.sum(values * values, -1, keepdims=True) + EPS)


def rms_ratio(values):
    return lax.rsqrt(jnp.mean(values * values, -1, keepdims=True) + EPS)


def norm_back(values, gain, grad):
    ratio = rms_ratio(values)
    scaled = values * ratio
    weighted = grad * gain
    value_grad = ratio * (weighted - scaled * jnp.mean(weighted * scaled, -1, keepdims=True))
    return value_grad, jnp.sum(grad * scaled, 0, keepdims=True)


def terms_kernel(*refs, lengths, n_fsdp, cut):
    (meta, x_ref, gain_ref, bw_ref, taps_ref, local_ref, own_ref, one, two, three_a, three_b,
     w_ref, pre_ref, act_ref, tt_ref, y_ref, ms_ref, xt_ref, xh_ref, beta_ref, sem) = refs
    heads = w_ref.shape[0]
    d_loc = local_ref.shape[1]
    rows = x_ref.shape[0] - PAD
    ctx, fsdp = meta[0], meta[1]

    def fill(source, first, end, head, shard, skip=0):
        for i in range(3):
            start, stop = max(first, i * d_loc), min(end, (i + 1) * d_loc)
            if start < stop:
                at = pl.multiple_of(shard * d_loc + (start - i * d_loc), 16)
                target = w_ref.at[head, i, pl.ds(at, stop - start), :]
                pltpu.make_async_copy(source.at[pl.ds(start - skip, stop - start), :], target, sem).start()

    for f in range(n_fsdp):
        fill(own_ref.at[f], 0, 3 * d_loc, ctx, f)
    for j in range(1, 4):
        head = ctx ^ j
        for i in range(3):
            target = w_ref.at[head, i, pl.ds(pl.multiple_of(fsdp * d_loc, d_loc), d_loc), :]
            source = local_ref.at[i, :, pl.ds(pl.multiple_of(head * HD, HD), HD)]
            pltpu.make_async_copy(source, target, sem).start()
        for r in range(1, n_fsdp):
            shard = lax.rem(fsdp + n_fsdp - r, n_fsdp)
            if j < 3:
                fill((one, two)[j - 1].at[r - 1], 0, 3 * d_loc, head, shard)
            else:
                fill(three_a.at[r - 1], 0, cut, head, shard)
                fill(three_b.at[r - 1], cut, 3 * d_loc, head, shard, cut)

    x_wide = x_ref[...].astype(F32)
    normed = (x_wide * rms_ratio(x_wide) * gain_ref[...]).astype(BF16)
    xt_ref[...] = normed[PAD:].T
    xh_ref[...] = normed[:PAD].T
    beta = sigmoid(pdot(normed[PAD:], bw_ref[...]))
    beta_ref[...] = beta
    lb, _ = slots(meta, rows, 0, lengths)
    place = iota((rows, 1), 0)
    age = place - lb
    row, col = iota((rows, rows), 0), iota((rows, rows), 1)
    below = (col >= lb) & (col < row)
    lb_last = lb[rows - 1 :]
    last = jnp.where(place >= lb_last, 1.0, 0.0)
    keep = jnp.where(lb_last < 0, 1.0, 0.0)
    eye = jnp.where(iota((HD, HD), 0) == iota((HD, HD), 1), 1.0, 0.0)
    pltpu.make_async_copy(w_ref, w_ref, sem).wait()

    lowers, keys, scaled = [], [], []
    for h in range(heads):
        acts = []
        for i in range(3):
            pre = pdot(normed, w_ref[h, i]).astype(BF16)
            pre_ref[h, i] = pre
            total = conv_forward(pre.astype(F32), taps_ref[h, i], age)
            act = total * sigmoid(total)
            if i < 2:
                act = act * l2_ratio(act)
            acts.append(act.astype(BF16))
            act_ref[h, i] = acts[i]
        key, value = acts[1], acts[2]
        beta_h = beta[:, h : h + 1]
        lowers.append(jnp.where(below, beta_h * pdot(key, key, NT), 0.0))
        keys.append(key)
        scaled.append(beta_h * jnp.concatenate([key, value], -1).astype(F32))
    half = rows // 2
    for h, (top, corner, bottom) in enumerate(unit_lower_inverses(lowers)):
        tt_ref[h, :half, :half] = top.T
        tt_ref[h, :half, half:] = corner.T
        tt_ref[h, half:, :half] = jnp.zeros((half, half), F32)
        tt_ref[h, half:, half:] = bottom.T
        upper = mm(top, scaled[h][:half])
        lower = mm(jnp.concatenate([corner, bottom], -1), scaled[h])
        solved = jnp.concatenate([upper, lower])
        y_ref[h] = solved
        ms_ref[h, 0] = (keep * (eye - mm(solved[:, :HD], keys[h], TN))).astype(BF16)
        ms_ref[h, 1] = mm(last * solved[:, HD:], keys[h], TN).astype(BF16)


def output_kernel(*refs, lengths, sources, n_fsdp):
    (meta, y_ref, act_ref, gain_ref, local_ref, own_ref, o1, o2, o3), refs = refs[:9], refs[9:]
    arrived, (ow_ref, mixed_ref, r_ref, s_ref, n_ref, attn_ref, sem) = refs[:sources], refs[sources:]
    heads, rows = y_ref.shape[:2]
    ctx = meta[0]
    fsdp = meta[1]
    d_loc = local_ref.shape[0]

    def fill(source, head, shard):
        at = pl.multiple_of(shard * d_loc, d_loc)
        pltpu.make_async_copy(source, ow_ref.at[head, pl.ds(at, d_loc), :], sem).start()

    for j, piece in enumerate((own_ref, o1, o2, o3)):
        head = ctx ^ j
        fill(local_ref.at[:, pl.ds(pl.multiple_of(head * HD, HD), HD)], head, fsdp)
        for r in range(1, n_fsdp):
            fill(piece.at[r - 1], head, lax.rem(fsdp + n_fsdp - r, n_fsdp))
    lb, _ = slots(meta, rows, 0, lengths)
    row, col = iota((rows, rows), 0), iota((rows, rows), 1)
    upto = (col >= lb) & (col <= row)
    carried = jnp.where(lb < 0, 1.0, 0.0)
    normed = []
    for h in range(heads):
        state = jnp.zeros((HD, HD), F32)
        for c in range(sources):
            after = pick(arrived, ctx ^ c, h, 1).astype(F32)
            if c:
                after = after + mm(state, pick(arrived, ctx ^ c, h, 0))
            state = jnp.where(c < ctx, after, state)
        query, key = act_ref[h, 0], act_ref[h, 1]
        w_part, u_part = y_ref[h, :, :HD], y_ref[h, :, HD:]
        scores = jnp.where(upto, pdot(query, key, NT) * SCALE, 0.0)
        fresh = u_part - carried * mm(w_part, state, NT)
        mixed = carried * (SCALE * mm(query, state, NT)) + mm(scores, fresh)
        mixed_ref[h] = mixed
        r_ref[h] = fresh
        s_ref[h] = state
        out = (mixed * rms_ratio(mixed) * gain_ref[...]).astype(BF16)
        n_ref[:, h * HD : (h + 1) * HD] = out
        normed.append(out)
    pltpu.make_async_copy(ow_ref, ow_ref, sem).wait()
    total = pdot(normed[0], ow_ref[0], NT)
    for h in range(1, heads):
        total = total + pdot(normed[h], ow_ref[h], NT)
    attn_ref[...] = total


def mlp_kernel(*refs, lengths, n_fsdp):
    (meta, x_ref, attn_ref, other_ref, gain_ref, cot_ref, local_ref, own_ref, f1, f2, a3, b3, down_ref,
     mid_ref, nt_ref, at_ref, g_ref, gf_ref, part_ref, st_ref, x3_ref, y3_ref, w, gu, sem) = refs
    rows, width = x_ref.shape
    units = down_ref.shape[0]
    d_loc = local_ref.shape[0]
    step = GU_BLOCKS * HD
    half = step // 2
    quarters = w.shape[0]
    ctx, fsdp = meta[0], meta[1]

    def fill(source, quarter, shard, at, size):
        start = pl.multiple_of(shard * d_loc, d_loc)
        pltpu.make_async_copy(source, w.at[quarter, pl.ds(start, d_loc), pl.ds(at, size)], sem).start()

    for f in range(n_fsdp):
        fill(own_ref.at[f], ctx, f, 0, step)
    for j in range(1, 4):
        quarter = ctx ^ j
        fill(local_ref.at[:, pl.ds(pl.multiple_of(quarter * step, HD), step)], quarter, fsdp, 0, step)
        for r in range(1, n_fsdp):
            shard = lax.rem(fsdp + n_fsdp - r, n_fsdp)
            if j < 3:
                fill((f1, f2)[j - 1].at[r - 1], quarter, shard, 0, step)
            else:
                fill(a3.at[r - 1], quarter, shard, 0, half)
                fill(b3.at[r - 1], quarter, shard, half, half)

    _, inside = slots(meta, rows, 0, lengths)
    valid = jnp.where(inside, 1.0, 0.0)
    x_wide = x_ref[...].astype(F32)
    attn = (attn_ref[...] + other_ref[...]) * valid
    middle = x_wide + attn
    mid_ref[...] = middle
    for i, v in enumerate((x_wide, attn, middle)):
        st_ref[i : i + 1] = jnp.sum(valid * v * v, 0, keepdims=True)
    normed = (middle * rms_ratio(middle) * gain_ref[...]).astype(BF16)
    nt_ref[...] = normed.T
    g_ffn = (cot_ref[...].astype(F32) * valid).astype(BF16)
    gf_ref[...] = g_ffn
    g_act = pdot(g_ffn, down_ref[...], NT)
    pltpu.make_async_copy(w, w, sem).wait()
    for q in range(quarters):
        gu[:, q * step : (q + 1) * step] = pdot(normed, w[q])
    gate, up = gu[:, :units], gu[:, units : 2 * units]
    sig = sigmoid(gate)
    act = (gate * sig * up).astype(BF16)
    at_ref[...] = act.T
    g_up = g_act * gate * sig
    g_gate = g_act * up * sig * (1.0 + gate * (1.0 - sig))
    gu[:, :units] = g_gate
    gu[:, units : 2 * units] = g_up
    part = None
    for q in range(quarters):
        real = min(step, 2 * units - q * step)
        grad = gu[:, q * step : q * step + real].astype(BF16)
        if real < step:
            grad = jnp.concatenate([grad, jnp.zeros((rows, step - real), BF16)], -1)
        g_ref[ctx ^ q] = grad
        term = pdot(grad, w[q], NT)
        part = term if part is None else part + term
    part_ref[:rows] = part
    part_ref[rows:] = pdot(act, down_ref[...])
    x3_ref[...] = pdot(nt_ref[...], g_ref[3, :, :half]).astype(BF16)
    y3_ref[...] = pdot(nt_ref[...], g_ref[3, :, half:]).astype(BF16)


def mlp_grads_kernel(nt_ref, g_ref, at_ref, gf_ref, x1_ref, y2_ref, late_x_ref, late_y_ref, own_ref, down_ref):
    half = g_ref.shape[2] // 2
    nt = nt_ref[...]

    def put(ref, j, side):
        ref[...] = pdot(nt, g_ref[j, :, side * half : (side + 1) * half]).astype(BF16)

    put(x1_ref, 1, 0)
    put(y2_ref, 2, 1)
    put(late_x_ref, 1, 1)
    put(late_y_ref, 2, 0)
    put(own_ref.at[0], 0, 0)
    put(own_ref.at[1], 0, 1)
    down_ref[...] = pdot(at_ref[...], gf_ref[...]).astype(BF16)


def middle_kernel(
    meta, part_ref, other_ref, mid_ref, cot_ref, gain_ref, hgain_ref, ow_ref, n_ref, mixed_ref, act_ref, y_ref,
    out_ref, gm_ref, og_ref, do_ref, dr_ref, ds_ref, sm_ref, *, lengths
):
    heads, rows = mixed_ref.shape[:2]
    ctx = meta[0]
    lb, inside = slots(meta, rows, 0, lengths)
    lb_row, _ = slots(meta, rows, 1, lengths)
    valid = jnp.where(inside, 1.0, 0.0)
    row, col = iota((rows, rows), 0), iota((rows, rows), 1)
    upto = (row >= lb_row) & (row <= col)
    carried = jnp.where(lb < 0, 1.0, 0.0)
    middle = mid_ref[...]
    value_grad, gain_grad = norm_back(middle, gain_ref[...], part_ref[:rows] + other_ref[:rows])
    g_middle = cot_ref[...].astype(F32) + value_grad
    gm_ref[...] = g_middle
    g_attn = (g_middle * valid).astype(BF16)
    turned_grad = g_attn.T
    total = jnp.zeros((1, HD), F32)
    for h in range(heads):
        key = act_ref[h, 1]
        g_head = pdot(g_attn, ow_ref[h])
        d_mixed, part = norm_back(mixed_ref[h], hgain_ref[...], g_head)
        total = total + part
        turned = jnp.where(upto, pdot(key, act_ref[h, 0], NT) * SCALE, 0.0)
        d_fresh = mm(turned, d_mixed)
        do_ref[h] = d_mixed
        dr_ref[h] = d_fresh
        d_state = SCALE * mm(carried * d_mixed, act_ref[h, 0], TN) - mm(carried * d_fresh, y_ref[h, :, :HD], TN)
        ds_ref[h] = d_state.astype(BF16)
        og_ref[ctx ^ h] = pdot(turned_grad, n_ref[:, h * HD : (h + 1) * HD]).astype(BF16)
    ffn = (part_ref[rows:] + other_ref[rows:]) * valid
    result = middle + ffn
    out_ref[...] = result.astype(BF16)
    sm_ref[...] = jnp.zeros_like(sm_ref)
    sm_ref[0:1] = gain_grad
    sm_ref[1:2, :HD] = total
    sm_ref[2:3] = jnp.sum(valid * ffn * ffn, 0, keepdims=True)
    sm_ref[3:4] = jnp.sum(valid * result * result, 0, keepdims=True)
    sm_ref[4:5] = jnp.broadcast_to(jnp.sum(valid, 0, keepdims=True), gain_grad.shape) / gain_grad.shape[1]


def delta_back_kernel(*refs, lengths, sources):
    meta, grads, maps = refs[0], refs[1 : 1 + sources], refs[1 + sources : 1 + 2 * sources]
    (pre_ref, act_ref, tt_ref, y_ref, r_ref, s_ref, do_ref, dr_ref, beta_ref, taps_ref, w_ref, bw_ref, xt_ref, xh_ref, sm_ref, og_ref,
     keep_ref, x_ref, y2_ref, late_x_ref, late_y_ref, part_ref, bg_ref, cg_ref) = refs[1 + 2 * sources :]
    heads, rows = r_ref.shape[:2]
    width = w_ref.shape[2]
    ext = rows + PAD
    ctx = meta[0]
    lb, _ = slots(meta, rows, 0, lengths)
    lb_row, _ = slots(meta, rows, 1, lengths)
    place = iota((rows, 1), 0)
    age = place - lb
    row, col = iota((rows, rows), 0), iota((rows, rows), 1)
    last = jnp.where(place >= lb[rows - 1 :], 1.0, 0.0)
    carried = jnp.where(lb < 0, 1.0, 0.0)
    upto = (col >= lb) & (col <= row)
    below = (col >= lb) & (col < row)
    turned_upto = (row >= lb_row) & (row <= col)
    lane = iota((rows, HD), 1)
    logits = jnp.zeros((rows, HD), F32)
    top = jnp.zeros((PAD, HD), F32)
    xt, xh = xt_ref[...], xh_ref[...]
    part = jnp.zeros((rows, width), F32)
    ahead = jnp.zeros((PAD, width), F32)
    for h in range(heads):
        d_state = jnp.zeros((HD, HD), F32)
        for c in range(sources, 0, -1):
            before = pick(grads, ctx ^ c, h).astype(F32)
            if c < sources:
                before = before + mm(d_state, pick(maps, ctx ^ c, h, 0), NT)
            d_state = jnp.where(c > ctx, before, d_state)
        query, key, value = act_ref[h, 0], act_ref[h, 1], act_ref[h, 2]
        solved = y_ref[h]
        fresh, state, d_mixed = r_ref[h], s_ref[h], do_ref[h]
        beta = beta_ref[:, h : h + 1]
        d_fresh = dr_ref[h] + last * mm(key, d_state, NT)
        d_scores = jnp.where(upto, SCALE * mm(d_mixed, fresh, NT), 0.0)
        turned = jnp.where(turned_upto, SCALE * mm(fresh, d_mixed, NT), 0.0)
        d_query = mm(d_scores, key) + carried * (SCALE * mm(d_mixed, state))
        d_key = mm(turned, query) + mm(last * fresh, d_state)
        d_solved = jnp.concatenate([-carried * mm(d_fresh, state), d_fresh], -1)
        d_scaled = mm(tt_ref[h], d_solved)
        d_value = beta * d_scaled[:, HD:]
        d_key = d_key + beta * d_scaled[:, :HD]
        d_beta = jnp.sum(d_scaled[:, :HD] * key.astype(F32) + d_scaled[:, HD:] * value.astype(F32), -1, keepdims=True)
        d_lower = jnp.where(below, -mm(d_scaled, solved, NT), 0.0)
        d_beta = d_beta + jnp.sum(d_lower * pdot(key, key, NT), -1, keepdims=True)
        d_gram = beta * d_lower
        d_key = d_key + mm(d_gram, key) + mm(d_gram, key, TN)
        logits = jnp.where(lane == h, d_beta * beta * (1.0 - beta), logits)
        g_main, g_head = [], []
        for i, grad in enumerate((d_query, d_key, d_value)):
            taps = taps_ref[h, i]
            pre = pre_ref[h, i].astype(F32)
            total = conv_forward(pre, taps, age)
            sig = sigmoid(total)
            if i < 2:
                act = total * sig
                ratio = l2_ratio(act)
                unit = act * ratio
                grad = ratio * (grad - unit * jnp.sum(grad * unit, -1, keepdims=True))
            grad = grad * sig * (1.0 + total * (1.0 - sig))
            back = jnp.zeros((ext, HD), F32)
            for k in range(CONV):
                reach = CONV - 1 - k
                grad_k = jnp.where(age >= reach, grad, 0.0)
                cg_ref[h, i * CONV + k : i * CONV + k + 1, :] = jnp.sum(grad_k * conv_rows(pre, reach), 0, keepdims=True)
                padded = jnp.concatenate([top, grad_k])
                back = back + (pltpu.roll(padded, ext - reach, 0) if reach else padded) * taps[k : k + 1]
            g_main.append(back[PAD:].astype(BF16))
            g_head.append(back[:PAD].astype(BF16))
            part = part + pdot(g_main[i], w_ref[h, i], NT)
            ahead = ahead + pdot(g_head[i], w_ref[h, i], NT)
        piece = pdot(xt, jnp.concatenate(g_main, -1)) + pdot(xh, jnp.concatenate(g_head, -1))
        piece = piece.astype(BF16)
        places = (
            (keep_ref.at[0], keep_ref.at[1]),
            (x_ref.at[1], late_x_ref),
            (late_y_ref, y2_ref.at[1]),
            (x_ref.at[0], y2_ref.at[0]),
        )
        for j, (a, b) in enumerate(places):

            @pl.when(ctx ^ j == h)
            def _(a=a, b=b, j=j, piece=piece):
                a[...] = piece[:, : 2 * HD]
                b[:, :HD] = piece[:, 2 * HD :]
                b[:, HD:] = og_ref[j]

    logits = logits.astype(BF16)
    part_ref[:rows] = part + pdot(logits, bw_ref[...], NT)
    part_ref[rows:ext] = ahead
    part_ref[ext:] = jnp.zeros((PAD, width), F32)
    part_ref[ext : ext + 1, :HD] = sm_ref[1:2, :HD]
    bg_ref[...] = lax.dot_general(logits, xt, (((0,), (1,)), ((), ())), preferred_element_type=F32)[:PAD]


def last_kernel(x_ref, gain_ref, part_ref, other_ref, rim_ref, gm_ref, sm_ref, st_ref, bg_ref, cg_ref, grad_ref, small_ref):
    rows, width = x_ref.shape
    heads = cg_ref.shape[0]
    total = part_ref[...] + other_ref[...]
    grad = jnp.concatenate([total[: rows - PAD], total[rows - PAD : rows] + rim_ref[...]])
    value_grad, gain_grad = norm_back(x_ref[...].astype(F32), gain_ref[...], grad)
    grad_ref[...] = gm_ref[...] + value_grad
    small_ref[...] = jnp.zeros_like(small_ref)
    small_ref[0:1] = gain_grad
    small_ref[1:2] = sm_ref[0:1]
    small_ref[2 : 2 + heads] = bg_ref[:heads]
    small_ref[6:9] = st_ref[0:3]
    small_ref[9:11] = sm_ref[2:4]
    small_ref[11:12] = sm_ref[4:5]
    at = WIDE_ROWS + 6
    for h in range(heads):
        small_ref[at : at + 3 * CONV, h * HD : (h + 1) * HD] = cg_ref[h, : 3 * CONV]
    at += 3 * CONV
    small_ref[at : at + 1, :HD] = total[rows + PAD : rows + PAD + 1, :HD]


def mixer_sum_kernel(meta, keep_ref, x_ref, y_ref, late_y_ref, late_x_ref, s0, s1, s2, s3, *outs, n_fsdp):
    width, half = x_ref.shape[1:]
    d_loc = width // n_fsdp
    grouped = len(outs) < n_fsdp
    small = (s0[...] + s1[...]) + (s2[...] + s3[...])
    rows, lanes = iota((SMALL_ROWS, 2 * half), 0), iota((SMALL_ROWS, 2 * half), 1)
    stats = jnp.sum(small, -1, keepdims=True)
    high = stats.astype(BF16).astype(F32)
    common = jnp.where(rows < WIDE_ROWS + 6, jnp.where(lanes < half + HD, high, stats - high), small[:, : 2 * half])
    for r in range(n_fsdp):
        shard = r if grouped else lax.rem(meta[1] + r, n_fsdp)
        ref, first = (outs[0], r * (d_loc + SMALL_ROWS)) if grouped else (outs[r], 0)
        at = pl.ds(r * d_loc if grouped else pl.multiple_of(shard * d_loc, d_loc), d_loc)
        a = keep_ref[0, at, :].astype(F32) + x_ref[1, at, :].astype(F32) + late_y_ref[at, :].astype(F32)
        b = keep_ref[1, at, :].astype(F32) + y_ref[1, at, :].astype(F32) + late_x_ref[at, :].astype(F32)
        ref[first : first + d_loc, :half] = a.astype(BF16)
        ref[first : first + d_loc, half:] = b.astype(BF16)
        slices = [small[:, k * d_loc : (k + 1) * d_loc] for k in ([r] if grouped else range(n_fsdp))]
        mine = slices[0]
        for k in range(1, len(slices)):
            mine = jnp.where(shard == k, slices[k], mine)
        mine = jnp.concatenate([mine, jnp.zeros((SMALL_ROWS, 2 * half - d_loc), F32)], -1)
        ref[first + d_loc : first + d_loc + SMALL_ROWS] = jnp.where(rows < WIDE_ROWS, mine, common).astype(BF16)


def mixer_total_kernel(meta, own_ref, *refs, width):
    far, (mix_ref, first_ref, second_ref, beta_ref, conv_ref, head_ref, rms_ref) = refs[:-7], refs[-7:]
    count, rows = len(far) + 1, mix_ref.shape[0]
    heads, hd_loc = conv_ref.shape[1:]
    total = None
    for f in range(count):
        part = own_ref[...]
        for r, ref in enumerate(far):
            part = jnp.where(lax.rem(meta[1] + count - (r + 1), count) == f, ref[...], part)
        part = part.astype(F32)
        total = part if total is None else total + part
    mix_ref[...] = total[:rows].astype(BF16)
    small = total[rows:]
    first_ref[...] = small[0:1, :rows]
    second_ref[...] = small[1:2, :rows]
    beta_ref[...] = small[:8, :rows].T[:, 2 : 2 + heads]
    for h in range(heads):
        lanes = small[WIDE_ROWS + 6 :, h * HD : (h + 1) * HD]
        mine = lanes[:, :hd_loc]
        for k in range(1, HD // hd_loc):
            mine = jnp.where(meta[1] == k, lanes[:, k * hd_loc : (k + 1) * hd_loc], mine)
        conv_ref[:, h, :] = mine[: 3 * CONV]
        if h == 0:
            head_ref[...] = mine[3 * CONV : 3 * CONV + 1]
    stats = small[WIDE_ROWS : WIDE_ROWS + 6, 2 * HD : 2 * HD + 1] + small[WIDE_ROWS : WIDE_ROWS + 6, 3 * HD : 3 * HD + 1]
    rms_ref[...] = jnp.sqrt(stats[:5] / (stats[5:] * width))


def gate_up_whole_kernel(p_ref, d0, d1, e0, e1, gu_ref, down_ref):
    units = gu_ref.shape[2]
    down_ref[: d0.shape[0]] = d0[...].astype(F32) + d1[...].astype(F32)
    down_ref[d0.shape[0] :] = e0[...].astype(F32) + e1[...].astype(F32)
    for q in range(p_ref.shape[0]):
        for k in range(GU_BLOCKS):
            at = (q * GU_BLOCKS + k) * HD
            if at < 2 * units:
                gu_ref[at // units, :, at % units : at % units + HD] = p_ref[q, :, k * HD : (k + 1) * HD].astype(F32)


def mixer_whole_kernel(meta, p0, p1, p2, p3, qkv_ref, out_ref):
    ctx = meta[0]
    for q in range(4):
        for j, ref in enumerate((p0, p1, p2, p3)):

            @pl.when(ctx ^ j == q)
            def _(ref=ref, q=q):
                for i in range(3):
                    qkv_ref[i, :, q * HD : (q + 1) * HD] = ref[:, i * HD : (i + 1) * HD].astype(F32)
                out_ref[q * HD : (q + 1) * HD, :] = ref[:, 3 * HD :].T.astype(F32)


def sds(*shape, dtype=F32):
    return jax.ShapeDtypeStruct(shape, dtype)


def call(body, name, out_shape, in_specs, args, scratch=(), gflops=1, mbytes=4):
    return pl.pallas_call(
        body,
        name=name,
        in_specs=in_specs,
        out_specs=jax.tree.map(lambda _: VMEM, out_shape),
        out_shape=out_shape,
        scratch_shapes=list(scratch),
        compiler_params=pltpu.CompilerParams(vmem_limit_bytes=56 * 1024 * 1024),
        cost_estimate=pl.CostEstimate(flops=int(COST * US[name] * 1_150_000_000), bytes_accessed=10**6, transcendentals=0),
    )(*args)


def shifted(value, axis, steps):
    count = lax.axis_size(axis)
    first, end = max(0, -steps), min(count, count - steps)
    return lax.ppermute(value, axis, [(s, s + steps) for s in range(first, end)])


def swapped(value, axis, mask):
    return lax.ppermute(value, axis, [(s, s ^ mask) for s in range(lax.axis_size(axis))])


def far_shards(value):
    count = lax.axis_size("fsdp")
    if count <= 4:
        turns = [[(s, (s + r) % count) for s in range(count)] for r in range(1, count)]
        return [lax.ppermute(value, "fsdp", turn)[None] for turn in turns]
    return [others(lax.all_gather(value, "fsdp", axis=0))]


def others(value):
    return jnp.concatenate([other(value, r) for r in range(1, lax.axis_size("fsdp"))])


def other(value, r):
    count, here = lax.axis_size("fsdp"), lax.axis_index("fsdp")
    return lax.dynamic_index_in_dim(value, (here + count - r) % count, 0)


def local(
    tokens, lengths, norm_gain, qkv_weight, beta_weight, conv_weight, head_gain, out_weight, mlp_gain, gate_up_weight, down_weight, cotangent
):
    rows, width = tokens.shape
    n_ctx, n_fsdp = lax.axis_size("ctx"), lax.axis_size("fsdp")
    ctx, fsdp = lax.axis_index("ctx"), lax.axis_index("fsdp")
    d_loc = qkv_weight.shape[1]
    heads = beta_weight.shape[1]
    units = down_weight.shape[0]
    hd_loc = head_gain.shape[0]
    n_len = lengths.shape[1]
    step = GU_BLOCKS * HD
    ext = rows + PAD
    meta = jnp.concatenate([jnp.stack([ctx, fsdp]).astype(jnp.int32), lengths[0]])

    small = jnp.concatenate([norm_gain, mlp_gain, head_gain, beta_weight.reshape(-1), conv_weight.reshape(-1)])
    small_rows = -(-small.shape[0] // (HD * 16)) * 16
    small = jnp.pad(small, (0, small_rows * HD - small.shape[0])).reshape(small_rows, HD)
    qkv_part = lax.dynamic_slice_in_dim(qkv_weight, ctx * HD, HD, 2).reshape(3 * d_loc, HD)
    out_part = lax.dynamic_slice_in_dim(out_weight, ctx * HD, HD, 0).T
    pack = jnp.concatenate([qkv_part, small])
    packs = lax.all_gather(pack, "fsdp", axis=0)
    pack_far = others(packs)
    out_local = out_weight.T
    gu_local = jnp.concatenate(
        [gate_up_weight[0], gate_up_weight[1], jnp.zeros((d_loc, n_ctx * step - 2 * units), BF16)], -1
    )
    gu_part = lax.dynamic_slice_in_dim(gu_local, ctx * step, step, 1)
    gu_own = lax.all_gather(gu_part, "fsdp", axis=0)
    gu_far = others(gu_own)
    down_full = lax.all_gather(down_weight, "fsdp", axis=1, tiled=True)
    x_ext = jnp.concatenate([shifted(tokens[rows - PAD :], "ctx", 1), tokens])

    cut = 3 * d_loc // 2
    pack_far, out_part = lax.optimization_barrier((pack_far, out_part))
    one, two = swapped(pack_far, "ctx", 1), swapped(pack_far, "ctx", 2)
    out_far = far_shards(out_part)
    three_a, three_b = swapped(one[:, :cut], "ctx", 2), swapped(two[:, cut:], "ctx", 1)
    three_a, three_b, out_far = lax.optimization_barrier((three_a, three_b, out_far))
    out_far = jnp.concatenate(out_far)
    out_pieces = [swapped(out_far, "ctx", j) for j in range(1, n_ctx)]

    flat = packs[:, 3 * d_loc :].reshape(n_fsdp, -1)
    at = 0
    first_gain = flat[:, at : at + d_loc].reshape(1, width).astype(F32)
    at += d_loc
    second_gain = flat[:, at : at + d_loc].reshape(1, width).astype(F32)
    at += d_loc
    head_full = flat[:, at : at + hd_loc].reshape(1, HD).astype(F32)
    at += hd_loc
    beta_full = jnp.pad(flat[:, at : at + d_loc * heads].reshape(width, heads), ((0, 0), (0, HD - heads)))
    at += d_loc * heads
    conv_full = flat[:, at : at + 3 * CONV * heads * hd_loc].reshape(n_fsdp, 3, CONV, heads, hd_loc)
    conv_full = conv_full.transpose(3, 1, 2, 0, 4).reshape(heads, 3, CONV, HD).astype(F32)

    qkv_full, pre, acts, turned, solved, ends_map, normed_t, normed_far, beta = call(
        functools.partial(terms_kernel, lengths=n_len, n_fsdp=n_fsdp, cut=cut),
        "delta_terms",
        (
            sds(heads, 3, width, HD, dtype=BF16),
            sds(heads, 3, ext, HD, dtype=BF16),
            sds(heads, 3, rows, HD, dtype=BF16),
            sds(heads, rows, rows),
            sds(heads, rows, 2 * HD),
            sds(heads, 2, HD, HD, dtype=BF16),
            sds(width, rows, dtype=BF16),
            sds(width, PAD, dtype=BF16),
            sds(rows, HD),
        ),
        [SMEM] + [VMEM] * 4 + [ANY] * 6,
        (meta, x_ext, first_gain, beta_full, conv_full, qkv_weight, packs, one, two, three_a, three_b),
        [pltpu.SemaphoreType.DMA],
        gflops=15,
        mbytes=8,
    )
    arrived = [swapped(ends_map, "ctx", j) for j in range(1, n_ctx)]
    gu_one, gu_two = lax.optimization_barrier((swapped(gu_far, "ctx", 1), swapped(gu_far, "ctx", 2)))
    gu_three = (swapped(gu_one[:, :, : step // 2], "ctx", 2), swapped(gu_two[:, :, step // 2 :], "ctx", 1))
    out_full, mixed, fresh, state, head_out, attn_part = call(
        functools.partial(output_kernel, lengths=n_len, sources=n_ctx - 1, n_fsdp=n_fsdp),
        "delta_outputs",
        (
            sds(heads, width, HD, dtype=BF16),
            sds(heads, rows, HD),
            sds(heads, rows, HD),
            sds(heads, HD, HD),
            sds(rows, heads * HD, dtype=BF16),
            sds(rows, width),
        ),
        [SMEM] + [VMEM] * 3 + [ANY] * (1 + n_ctx) + [VMEM] * len(arrived),
        (meta, solved, acts, head_full, out_local, out_far, *out_pieces, *arrived),
        [pltpu.SemaphoreType.DMA],
        gflops=6,
        mbytes=6,
    )
    attn_other = swapped(attn_part, "tp", 1)

    middle, normed_mid_t, act_t, g_gu, g_ffn, mlp_part, stats, gu_x3, gu_y3 = call(
        functools.partial(mlp_kernel, lengths=n_len, n_fsdp=n_fsdp),
        "mlp",
        (
            sds(rows, width),
            sds(width, rows, dtype=BF16),
            sds(units, rows, dtype=BF16),
            sds(n_ctx, rows, step, dtype=BF16),
            sds(rows, width, dtype=BF16),
            sds(2 * rows, width),
            sds(8, width),
            sds(width, step // 2, dtype=BF16),
            sds(width, step // 2, dtype=BF16),
        ),
        [SMEM] + [VMEM] * 5 + [ANY] * 6 + [VMEM],
        (
            meta, tokens, attn_part, attn_other, second_gain, cotangent, gu_local, gu_own, gu_one, gu_two, *gu_three, down_full,
        ),
        [pltpu.VMEM((n_ctx, width, step), BF16), pltpu.VMEM((rows, n_ctx * step), F32), pltpu.SemaphoreType.DMA],
        gflops=10,
        mbytes=14,
    )
    mlp_other = swapped(mlp_part, "tp", 1)
    quarter = sds(width, step // 2, dtype=BF16)
    double = sds(2, width, step // 2, dtype=BF16)
    gu_grads = call(
        mlp_grads_kernel,
        "mlp_grads",
        (quarter,) * 4 + (double, sds(units, width, dtype=BF16)),
        [VMEM] * 4,
        (normed_mid_t, g_gu, act_t, g_ffn),
        gflops=4,
        mbytes=12,
    )
    mlp_other, gu_grads = lax.optimization_barrier((mlp_other, gu_grads))
    gu_x1, gu_y2, gu_late_x, gu_late_y, gu_keep, down_grad = gu_grads
    from_x3, from_y3 = swapped(gu_x3, "ctx", 1), swapped(gu_y3, "ctx", 2)

    result, g_middle, out_grads, d_mixed, d_fresh, d_state, sums = call(
        functools.partial(middle_kernel, lengths=n_len),
        "middle_back",
        (
            sds(rows, width, dtype=BF16),
            sds(rows, width),
            sds(n_ctx, width, HD, dtype=BF16),
            sds(heads, rows, HD),
            sds(heads, rows, HD),
            sds(heads, HD, HD, dtype=BF16),
            sds(8, width),
        ),
        [SMEM] + [VMEM] * 11,
        (
            meta, mlp_part, mlp_other, middle, cotangent, second_gain, head_full, out_full, head_out, mixed, acts,
            solved,
        ),
        gflops=6,
        mbytes=12,
    )
    behind = [swapped(d_state, "ctx", j) for j in range(1, n_ctx)]

    down_sh = lax.psum_scatter(down_grad, "fsdp", scatter_dimension=1, tiled=True)

    def add(left, right):
        return (left.astype(F32) + right.astype(F32)).astype(BF16)

    gu_x1, gu_y2, _ = lax.optimization_barrier((gu_x1, gu_y2, d_state))
    from_x1, from_y2 = swapped(gu_x1, "ctx", 1), swapped(gu_y2, "ctx", 2)
    gu_late_y, gu_late_x = add(gu_late_y, from_x3), add(gu_late_x, from_y3)
    behind, gu_late_x, gu_late_y = lax.optimization_barrier((behind, gu_late_x, gu_late_y))
    gu_late_y, gu_late_x = swapped(gu_late_y, "ctx", 2), swapped(gu_late_x, "ctx", 1)
    half = sds(width, 2 * HD, dtype=BF16)
    double = sds(2, width, 2 * HD, dtype=BF16)
    back = call(
        functools.partial(delta_back_kernel, lengths=n_len, sources=n_ctx - 1),
        "delta_back",
        (double, double, double, half, half, sds(ext + PAD, width), sds(PAD, width), sds(heads, 16, HD)),
        [SMEM] + [VMEM] * (2 * n_ctx - 2 + 16),
        (
            meta, *behind, *arrived, pre, acts, turned, solved, fresh, state, d_mixed, d_fresh, beta, conv_full, qkv_full, beta_full,
            normed_t, normed_far, sums, out_grads,
        ),
        gflops=16,
        mbytes=16,
    )

    mix_keep, mix_x, mix_y, mix_late_x, mix_late_y, in_part, beta_grad, conv_grad = back
    from_x1, from_y2, gu_late_x, gu_late_y, mix_keep, down_sh = lax.optimization_barrier(
        (from_x1, from_y2, gu_late_x, gu_late_y, mix_keep, down_sh)
    )
    in_other = swapped(in_part, "tp", 1)
    rim = shifted(in_part[rows:ext] + in_other[rows:ext], "ctx", -1)
    mix_from_x, mix_from_y = swapped(mix_x, "ctx", 1), swapped(mix_y, "ctx", 2)
    mix_from_x, mix_from_y, rim, down_sh = lax.optimization_barrier((mix_from_x, mix_from_y, rim, down_sh))
    input_grad, smalls = call(
        last_kernel,
        "input_back",
        (sds(rows, width), sds(SMALL_ROWS, width)),
        [VMEM] * 10,
        (tokens, first_gain, in_part, in_other, rim, g_middle, sums, stats, beta_grad, conv_grad),
        gflops=1,
        mbytes=6,
    )
    small_pieces = [smalls] + [swapped(smalls, "ctx", j) for j in range(1, n_ctx)]
    gu_sum = [
        (gu_keep[0].astype(F32) + from_x1.astype(F32) + gu_late_y.astype(F32)).astype(BF16),
        (gu_keep[1].astype(F32) + from_y2.astype(F32) + gu_late_x.astype(F32)).astype(BF16),
    ]
    gu_sh = lax.psum_scatter(jnp.concatenate(gu_sum, -1), "fsdp", scatter_dimension=0, tiled=True)

    mix_late_y, mix_late_x = add(mix_late_y, mix_from_x[0]), add(mix_late_x, mix_from_y[0])
    mix_late_y, mix_late_x = lax.optimization_barrier((swapped(mix_late_y, "ctx", 2), swapped(mix_late_x, "ctx", 1)))
    side = units // 2
    down_a, down_b = down_sh[:side], down_sh[side:]
    down_other = swapped(down_a, "ctx", 1), swapped(down_b, "ctx", 2)
    count = n_fsdp if n_fsdp <= 4 else 1
    mix_rows = n_fsdp // count * (d_loc + SMALL_ROWS)
    mix_own, *mix_far = call(
        functools.partial(mixer_sum_kernel, n_fsdp=n_fsdp),
        "mixer_sum",
        (sds(mix_rows, 4 * HD, dtype=BF16),) * count,
        [SMEM] + [VMEM] * (5 + n_ctx),
        (meta, mix_keep, mix_from_x, mix_from_y, mix_late_y, mix_late_x, *small_pieces),
        gflops=1,
        mbytes=6,
    )
    mix_own, down_other, gu_sh = lax.optimization_barrier((mix_own, down_other, gu_sh))
    down_a, down_b = add(down_a, down_other[0]), add(down_b, down_other[1])
    down_parts = (down_a, swapped(down_a, "ctx", 2), down_b, swapped(down_b, "ctx", 1))
    gu_all = lax.all_gather(gu_sh, "ctx", axis=0)
    if count > 1:
        turns = [[(i, (i + r) % n_fsdp) for i in range(n_fsdp)] for r in range(1, n_fsdp)]
        mix_far = [lax.ppermute(part, "fsdp", turn) for part, turn in zip(mix_far, turns, strict=True)]
        mix_far, down_parts = lax.optimization_barrier((mix_far, down_parts))
    else:
        mix_own = lax.psum_scatter(mix_own, "fsdp", scatter_dimension=0, tiled=True)
    mix_sh, first_out, second_out, beta_out, conv_out, head_out_grad, rms = call(
        functools.partial(mixer_total_kernel, width=width),
        "mixer_total",
        (
            sds(d_loc, 4 * HD, dtype=BF16),
            sds(1, d_loc),
            sds(1, d_loc),
            sds(d_loc, heads),
            sds(3 * CONV, heads, hd_loc),
            sds(1, hd_loc),
            sds(5, 1),
        ),
        [SMEM] + [VMEM] * count,
        (meta, mix_own, *mix_far),
        gflops=1,
        mbytes=1,
    )
    def pieces(part):
        return [part] + [swapped(part, "ctx", j) for j in range(1, n_ctx)]

    gu_out, down_out = call(
        gate_up_whole_kernel,
        "gate_up_whole",
        (sds(2, d_loc, units), sds(units, d_loc)),
        [VMEM] * 5,
        (gu_all, *down_parts),
        gflops=1,
        mbytes=6,
    )
    qkv_out, out_out = call(
        mixer_whole_kernel,
        "mixer_whole",
        (sds(3, d_loc, heads * HD), sds(heads * HD, d_loc)),
        [SMEM] + [VMEM] * n_ctx,
        (meta, *pieces(mix_sh)),
        gflops=1,
        mbytes=4,
    )
    return (
        result,
        input_grad,
        first_out.reshape(-1),
        qkv_out,
        beta_out,
        conv_out.reshape(3, CONV, heads, hd_loc),
        head_out_grad.reshape(-1),
        out_out,
        second_out.reshape(-1),
        gu_out,
        down_out,
        rms.reshape(-1),
    )


def solution(mesh):
    return jax.shard_map(
        local,
        mesh=mesh,
        in_specs=(
            P(("fsdp", "ctx"), None),
            P("fsdp", None),
            P("fsdp"),
            P(None, "fsdp", "tp"),
            P("fsdp", "tp"),
            P(None, None, "tp", "fsdp"),
            P("fsdp"),
            P("tp", "fsdp"),
            P("fsdp"),
            P(None, "fsdp", "tp"),
            P("tp", "fsdp"),
            P(("fsdp", "ctx"), None),
        ),
        out_specs=(
            P(("fsdp", "ctx"), None),
            P(("fsdp", "ctx"), None),
            P("fsdp"),
            P(None, "fsdp", "tp"),
            P("fsdp", "tp"),
            P(None, None, "tp", "fsdp"),
            P("fsdp"),
            P("tp", "fsdp"),
            P("fsdp"),
            P(None, "fsdp", "tp"),
            P("tp", "fsdp"),
            P(),
        ),
        check_vma=False,
    )
```

```python
import functools

import jax
import jax.numpy as jnp
from jax import lax
from jax.experimental import pallas as pl
from jax.experimental.pallas import tpu as pltpu
from jax.sharding import PartitionSpec as P

HD = 128
CONV = 4
PAD = 8
EPS = 1e-06
F32 = jnp.float32
BF16 = jnp.bfloat16
NN = (((1,), (0,)), ((), ()))
NT = (((1,), (1,)), ((), ()))
TN = (((0,), (0,)), ((), ()))
SCALE = HD ** (-0.5)
COST = 1.0
US = {'delta_terms': 108, 'delta_outputs': 58.5, 'mlp': 36.6, 'mlp_grads': 19.5, 'middle_back': 14.4, 'delta_back': 396, 'input_back': 1.1, 'mixer_sum': 10.5, 'mixer_total': 6.9, 'gate_up_whole': 9.9, 'mixer_whole': 8.7}
GU_BLOCKS = 6
SMALL_ROWS = 32
WIDE_ROWS = 6

ANY = pl.BlockSpec(memory_space=pl.ANY)
SMEM = pl.BlockSpec(memory_space=pltpu.SMEM)
VMEM = pl.BlockSpec(memory_space=pltpu.VMEM)


def parts_of(value, count):
    if value.dtype == BF16:
        return [value]
    pieces = []
    for left in range(count):
        piece = value.astype(BF16)
        pieces.append(piece)
        if left + 1 < count:
            value = value - piece.astype(F32)
    return pieces


def pdot(left, right, dims=NN):
    return lax.dot_general(left, right, dims, preferred_element_type=F32)


def mm_parts(lefts, rights, dims=NN):
    total = None
    for i, a in enumerate(lefts):
        for j, b in enumerate(rights):
            if i + j < max(len(lefts), len(rights)):
                term = pdot(a, b, dims)
                total = term if total is None else total + term
    return total


def mm(left, right, dims=NN, split=2):
    return mm_parts(parts_of(left, split), parts_of(right, split), dims)


def sigmoid(v):
    return 1.0 / (1.0 + jnp.exp(-v))


def iota(shape, axis):
    return lax.broadcasted_iota(jnp.int32, shape, axis)


def slots(meta, rows, axis, lengths):
    first = meta[0] * rows
    place = iota((rows, 1) if axis == 0 else (1, rows), axis) + first
    begins, end = jnp.zeros_like(place), 0
    for i in range(lengths):
        end = end + meta[2 + i]
        begins = jnp.where(end <= place, jnp.maximum(begins, end), begins)
    return begins - first, place < end


def unit_lower_inverses(lowers):
    n = lowers[0].shape[0]
    half = n // 2
    row, col = iota((half, half), 0), iota((half, half), 1)
    blocks = [low[at : at + half, at : at + half] for low in lowers for at in (0, half)]
    inverses = [jnp.where(row == col, 1.0, 0.0) - jnp.where(row // 2 == col // 2, b, 0.0) for b in blocks]
    split = [parts_of(b, 2) for b in blocks]
    zero = jnp.zeros((half, half), BF16)
    size = 2
    while size < half:
        inside = (row // (2 * size) == col // (2 * size)) & (row // size != col // size)
        pieces = [parts_of(inv, 2) for inv in inverses]
        steps = [mm_parts([jnp.where(inside, s, zero) for s in sp], pc) for sp, pc in zip(split, pieces, strict=True)]
        inverses = [inv - mm_parts(pc, parts_of(st, 2)) for inv, pc, st in zip(inverses, pieces, steps, strict=True)]
        size *= 2
    out = []
    for i, low in enumerate(lowers):
        top, bottom = inverses[2 * i], inverses[2 * i + 1]
        corner = -mm(bottom, mm(low[half:, :half], top))
        out.append((top, corner, bottom))
    return out


def conv_rows(pre, reach):
    return (pltpu.roll(pre, reach, 0) if reach else pre)[PAD:]


def conv_forward(pre, taps, age):
    total = jnp.zeros((pre.shape[0] - PAD, pre.shape[1]), F32)
    for k in range(CONV):
        reach = CONV - 1 - k
        total = total + jnp.where(age >= reach, conv_rows(pre, reach), 0.0) * taps[k : k + 1]
    return total


def pick(refs, j, *index):
    value = refs[-1][index]
    for k in range(len(refs) - 1, 0, -1):
        value = jnp.where(j == k, refs[k - 1][index], value)
    return value


def l2_ratio(values):
    return lax.rsqrt(jnp.sum(values * values, -1, keepdims=True) + EPS)


def rms_ratio(values):
    return lax.rsqrt(jnp.mean(values * values, -1, keepdims=True) + EPS)


def norm_back(values, gain, grad):
    ratio = rms_ratio(values)
    scaled = values * ratio
    weighted = grad * gain
    value_grad = ratio * (weighted - scaled * jnp.mean(weighted * scaled, -1, keepdims=True))
    return value_grad, jnp.sum(grad * scaled, 0, keepdims=True)


def terms_kernel(*refs, lengths, n_fsdp, cut):
    (meta, x_ref, gain_ref, bw_ref, taps_ref, local_ref, own_ref, one, two, three_a, three_b,
     w_ref, pre_ref, act_ref, tt_ref, y_ref, ms_ref, xt_ref, xh_ref, beta_ref, sem) = refs
    heads = w_ref.shape[0]
    d_loc = local_ref.shape[1]
    rows = x_ref.shape[0] - PAD
    ctx, fsdp = meta[0], meta[1]

    def fill(source, first, end, head, shard, skip=0):
        for i in range(3):
            start, stop = max(first, i * d_loc), min(end, (i + 1) * d_loc)
            if start < stop:
                at = pl.multiple_of(shard * d_loc + (start - i * d_loc), 16)
                target = w_ref.at[head, i, pl.ds(at, stop - start), :]
                pltpu.make_async_copy(source.at[pl.ds(start - skip, stop - start), :], target, sem).start()

    for f in range(n_fsdp):
        fill(own_ref.at[f], 0, 3 * d_loc, ctx, f)
    for j in range(1, 4):
        head = ctx ^ j
        for i in range(3):
            target = w_ref.at[head, i, pl.ds(pl.multiple_of(fsdp * d_loc, d_loc), d_loc), :]
            source = local_ref.at[i, :, pl.ds(pl.multiple_of(head * HD, HD), HD)]
            pltpu.make_async_copy(source, target, sem).start()
        for r in range(1, n_fsdp):
            shard = lax.rem(fsdp + n_fsdp - r, n_fsdp)
            if j < 3:
                fill((one, two)[j - 1].at[r - 1], 0, 3 * d_loc, head, shard)
            else:
                fill(three_a.at[r - 1], 0, cut, head, shard)
                fill(three_b.at[r - 1], cut, 3 * d_loc, head, shard, cut)

    x_wide = x_ref[...].astype(F32)
    normed = (x_wide * rms_ratio(x_wide) * gain_ref[...]).astype(BF16)
    xt_ref[...] = normed[PAD:].T
    xh_ref[...] = normed[:PAD].T
    beta = sigmoid(pdot(normed[PAD:], bw_ref[...]))
    beta_ref[...] = beta
    lb, _ = slots(meta, rows, 0, lengths)
    place = iota((rows, 1), 0)
    age = place - lb
    row, col = iota((rows, rows), 0), iota((rows, rows), 1)
    below = (col >= lb) & (col < row)
    lb_last = lb[rows - 1 :]
    last = jnp.where(place >= lb_last, 1.0, 0.0)
    keep = jnp.where(lb_last < 0, 1.0, 0.0)
    eye = jnp.where(iota((HD, HD), 0) == iota((HD, HD), 1), 1.0, 0.0)
    pltpu.make_async_copy(w_ref, w_ref, sem).wait()

    lowers, keys, scaled = [], [], []
    for h in range(heads):
        acts = []
        for i in range(3):
            pre = pdot(normed, w_ref[h, i]).astype(BF16)
            pre_ref[h, i] = pre
            total = conv_forward(pre.astype(F32), taps_ref[h, i], age)
            act = total * sigmoid(total)
            if i < 2:
                act = act * l2_ratio(act)
            acts.append(act.astype(BF16))
            act_ref[h, i] = acts[i]
        key, value = acts[1], acts[2]
        beta_h = beta[:, h : h + 1]
        lowers.append(jnp.where(below, beta_h * pdot(key, key, NT), 0.0))
        keys.append(key)
        scaled.append(beta_h * jnp.concatenate([key, value], -1).astype(F32))
    half = rows // 2
    for h, (top, corner, bottom) in enumerate(unit_lower_inverses(lowers)):
        tt_ref[h, :half, :half] = top.T
        tt_ref[h, :half, half:] = corner.T
        tt_ref[h, half:, :half] = jnp.zeros((half, half), F32)
        tt_ref[h, half:, half:] = bottom.T
        upper = mm(top, scaled[h][:half])
        lower = mm(jnp.concatenate([corner, bottom], -1), scaled[h])
        solved = jnp.concatenate([upper, lower])
        y_ref[h] = solved
        ms_ref[h, 0] = (keep * (eye - mm(solved[:, :HD], keys[h], TN, 1))).astype(BF16)
        ms_ref[h, 1] = mm(last * solved[:, HD:], keys[h], TN, 1).astype(BF16)


def output_kernel(*refs, lengths, sources, n_fsdp):
    (meta, y_ref, act_ref, gain_ref, local_ref, own_ref, o1, o2, o3), refs = refs[:9], refs[9:]
    arrived, (ow_ref, mixed_ref, r_ref, s_ref, n_ref, attn_ref, sem) = refs[:sources], refs[sources:]
    heads, rows = y_ref.shape[:2]
    ctx = meta[0]
    fsdp = meta[1]
    d_loc = local_ref.shape[0]

    def fill(source, head, shard):
        at = pl.multiple_of(shard * d_loc, d_loc)
        pltpu.make_async_copy(source, ow_ref.at[head, pl.ds(at, d_loc), :], sem).start()

    for j, piece in enumerate((own_ref, o1, o2, o3)):
        head = ctx ^ j
        fill(local_ref.at[:, pl.ds(pl.multiple_of(head * HD, HD), HD)], head, fsdp)
        for r in range(1, n_fsdp):
            fill(piece.at[r - 1], head, lax.rem(fsdp + n_fsdp - r, n_fsdp))
    lb, _ = slots(meta, rows, 0, lengths)
    row, col = iota((rows, rows), 0), iota((rows, rows), 1)
    upto = (col >= lb) & (col <= row)
    carried = jnp.where(lb < 0, 1.0, 0.0)
    normed = []
    for h in range(heads):
        state = jnp.zeros((HD, HD), F32)
        for c in range(sources):
            after = pick(arrived, ctx ^ c, h, 1).astype(F32)
            if c:
                after = after + mm(state, pick(arrived, ctx ^ c, h, 0))
            state = jnp.where(c < ctx, after, state)
        query, key = act_ref[h, 0], act_ref[h, 1]
        w_part, u_part = y_ref[h, :, :HD], y_ref[h, :, HD:]
        scores = jnp.where(upto, pdot(query, key, NT) * SCALE, 0.0)
        fresh = u_part - carried * mm(w_part, state, NT)
        mixed = carried * (SCALE * mm(query, state, NT)) + mm(scores, fresh)
        mixed_ref[h] = mixed
        r_ref[h] = fresh
        s_ref[h] = state
        out = (mixed * rms_ratio(mixed) * gain_ref[...]).astype(BF16)
        n_ref[:, h * HD : (h + 1) * HD] = out
        normed.append(out)
    pltpu.make_async_copy(ow_ref, ow_ref, sem).wait()
    total = pdot(normed[0], ow_ref[0], NT)
    for h in range(1, heads):
        total = total + pdot(normed[h], ow_ref[h], NT)
    attn_ref[...] = total


def mlp_kernel(*refs, lengths, n_fsdp):
    (meta, x_ref, attn_ref, other_ref, gain_ref, cot_ref, local_ref, own_ref, f1, f2, a3, b3, down_ref,
     mid_ref, nt_ref, at_ref, g_ref, gf_ref, part_ref, st_ref, x3_ref, y3_ref, w, gu, sem) = refs
    rows, width = x_ref.shape
    units = down_ref.shape[0]
    d_loc = local_ref.shape[0]
    step = GU_BLOCKS * HD
    half = step // 2
    quarters = w.shape[0]
    ctx, fsdp = meta[0], meta[1]

    def fill(source, quarter, shard, at, size):
        start = pl.multiple_of(shard * d_loc, d_loc)
        pltpu.make_async_copy(source, w.at[quarter, pl.ds(start, d_loc), pl.ds(at, size)], sem).start()

    for f in range(n_fsdp):
        fill(own_ref.at[f], ctx, f, 0, step)
    for j in range(1, 4):
        quarter = ctx ^ j
        fill(local_ref.at[:, pl.ds(pl.multiple_of(quarter * step, HD), step)], quarter, fsdp, 0, step)
        for r in range(1, n_fsdp):
            shard = lax.rem(fsdp + n_fsdp - r, n_fsdp)
            if j < 3:
                fill((f1, f2)[j - 1].at[r - 1], quarter, shard, 0, step)
            else:
                fill(a3.at[r - 1], quarter, shard, 0, half)
                fill(b3.at[r - 1], quarter, shard, half, half)

    _, inside = slots(meta, rows, 0, lengths)
    valid = jnp.where(inside, 1.0, 0.0)
    x_wide = x_ref[...].astype(F32)
    attn = (attn_ref[...] + other_ref[...]) * valid
    middle = x_wide + attn
    mid_ref[...] = middle
    for i, v in enumerate((x_wide, attn, middle)):
        st_ref[i : i + 1] = jnp.sum(valid * v * v, 0, keepdims=True)
    normed = (middle * rms_ratio(middle) * gain_ref[...]).astype(BF16)
    nt_ref[...] = normed.T
    g_ffn = (cot_ref[...].astype(F32) * valid).astype(BF16)
    gf_ref[...] = g_ffn
    g_act = pdot(g_ffn, down_ref[...], NT)
    pltpu.make_async_copy(w, w, sem).wait()
    for q in range(quarters):
        gu[:, q * step : (q + 1) * step] = pdot(normed, w[q])
    gate, up = gu[:, :units], gu[:, units : 2 * units]
    sig = sigmoid(gate)
    act = (gate * sig * up).astype(BF16)
    at_ref[...] = act.T
    g_up = g_act * gate * sig
    g_gate = g_act * up * sig * (1.0 + gate * (1.0 - sig))
    gu[:, :units] = g_gate
    gu[:, units : 2 * units] = g_up
    part = None
    for q in range(quarters):
        real = min(step, 2 * units - q * step)
        grad = gu[:, q * step : q * step + real].astype(BF16)
        if real < step:
            grad = jnp.concatenate([grad, jnp.zeros((rows, step - real), BF16)], -1)
        g_ref[ctx ^ q] = grad
        term = pdot(grad, w[q], NT)
        part = term if part is None else part + term
    part_ref[:rows] = part
    part_ref[rows:] = pdot(act, down_ref[...])
    x3_ref[...] = pdot(nt_ref[...], g_ref[3, :, :half]).astype(BF16)
    y3_ref[...] = pdot(nt_ref[...], g_ref[3, :, half:]).astype(BF16)


def mlp_grads_kernel(nt_ref, g_ref, at_ref, gf_ref, x1_ref, y2_ref, late_x_ref, late_y_ref, own_ref, down_ref):
    half = g_ref.shape[2] // 2
    nt = nt_ref[...]

    def put(ref, j, side):
        ref[...] = pdot(nt, g_ref[j, :, side * half : (side + 1) * half]).astype(BF16)

    put(x1_ref, 1, 0)
    put(y2_ref, 2, 1)
    put(late_x_ref, 1, 1)
    put(late_y_ref, 2, 0)
    put(own_ref.at[0], 0, 0)
    put(own_ref.at[1], 0, 1)
    down_ref[...] = pdot(at_ref[...], gf_ref[...]).astype(BF16)


def middle_kernel(
    meta, part_ref, other_ref, mid_ref, cot_ref, gain_ref, hgain_ref, ow_ref, n_ref, mixed_ref, act_ref, y_ref,
    out_ref, gm_ref, og_ref, do_ref, dr_ref, ds_ref, sm_ref, *, lengths
):
    heads, rows = mixed_ref.shape[:2]
    ctx = meta[0]
    lb, inside = slots(meta, rows, 0, lengths)
    lb_row, _ = slots(meta, rows, 1, lengths)
    valid = jnp.where(inside, 1.0, 0.0)
    row, col = iota((rows, rows), 0), iota((rows, rows), 1)
    upto = (row >= lb_row) & (row <= col)
    carried = jnp.where(lb < 0, 1.0, 0.0)
    middle = mid_ref[...]
    value_grad, gain_grad = norm_back(middle, gain_ref[...], part_ref[:rows] + other_ref[:rows])
    g_middle = cot_ref[...].astype(F32) + value_grad
    gm_ref[...] = g_middle
    g_attn = (g_middle * valid).astype(BF16)
    turned_grad = g_attn.T
    total = jnp.zeros((1, HD), F32)
    for h in range(heads):
        key = act_ref[h, 1]
        g_head = pdot(g_attn, ow_ref[h])
        d_mixed, part = norm_back(mixed_ref[h], hgain_ref[...], g_head)
        total = total + part
        turned = jnp.where(upto, pdot(key, act_ref[h, 0], NT) * SCALE, 0.0)
        d_fresh = mm(turned, d_mixed)
        do_ref[h] = d_mixed
        dr_ref[h] = d_fresh
        d_state = SCALE * mm(carried * d_mixed, act_ref[h, 0], TN) - mm(carried * d_fresh, y_ref[h, :, :HD], TN)
        ds_ref[h] = d_state.astype(BF16)
        og_ref[ctx ^ h] = pdot(turned_grad, n_ref[:, h * HD : (h + 1) * HD]).astype(BF16)
    ffn = (part_ref[rows:] + other_ref[rows:]) * valid
    result = middle + ffn
    out_ref[...] = result.astype(BF16)
    sm_ref[...] = jnp.zeros_like(sm_ref)
    sm_ref[0:1] = gain_grad
    sm_ref[1:2, :HD] = total
    sm_ref[2:3] = jnp.sum(valid * ffn * ffn, 0, keepdims=True)
    sm_ref[3:4] = jnp.sum(valid * result * result, 0, keepdims=True)
    sm_ref[4:5] = jnp.broadcast_to(jnp.sum(valid, 0, keepdims=True), gain_grad.shape) / gain_grad.shape[1]


def delta_back_kernel(*refs, lengths, sources):
    meta, grads, maps = refs[0], refs[1 : 1 + sources], refs[1 + sources : 1 + 2 * sources]
    (pre_ref, act_ref, tt_ref, y_ref, r_ref, s_ref, do_ref, dr_ref, beta_ref, taps_ref, w_ref, bw_ref, xt_ref, xh_ref, sm_ref, og_ref,
     keep_ref, x_ref, y2_ref, late_x_ref, late_y_ref, part_ref, bg_ref, cg_ref) = refs[1 + 2 * sources :]
    heads, rows = r_ref.shape[:2]
    width = w_ref.shape[2]
    ext = rows + PAD
    ctx = meta[0]
    lb, _ = slots(meta, rows, 0, lengths)
    lb_row, _ = slots(meta, rows, 1, lengths)
    place = iota((rows, 1), 0)
    age = place - lb
    row, col = iota((rows, rows), 0), iota((rows, rows), 1)
    last = jnp.where(place >= lb[rows - 1 :], 1.0, 0.0)
    carried = jnp.where(lb < 0, 1.0, 0.0)
    upto = (col >= lb) & (col <= row)
    below = (col >= lb) & (col < row)
    turned_upto = (row >= lb_row) & (row <= col)
    lane = iota((rows, HD), 1)
    logits = jnp.zeros((rows, HD), F32)
    top = jnp.zeros((PAD, HD), F32)
    xt, xh = xt_ref[...], xh_ref[...]
    part = jnp.zeros((rows, width), F32)
    ahead = jnp.zeros((PAD, width), F32)
    for h in range(heads):
        d_state = jnp.zeros((HD, HD), F32)
        for c in range(sources, 0, -1):
            before = pick(grads, ctx ^ c, h).astype(F32)
            if c < sources:
                before = before + mm(d_state, pick(maps, ctx ^ c, h, 0), NT)
            d_state = jnp.where(c > ctx, before, d_state)
        query, key, value = act_ref[h, 0], act_ref[h, 1], act_ref[h, 2]
        solved = y_ref[h]
        fresh, state, d_mixed = r_ref[h], s_ref[h], do_ref[h]
        beta = beta_ref[:, h : h + 1]
        d_fresh = dr_ref[h] + last * mm(key, d_state, NT)
        d_scores = jnp.where(upto, SCALE * mm(d_mixed, fresh, NT), 0.0)
        turned = jnp.where(turned_upto, SCALE * mm(fresh, d_mixed, NT), 0.0)
        d_query = mm(d_scores, key) + carried * (SCALE * mm(d_mixed, state))
        d_key = mm(turned, query) + mm(last * fresh, d_state)
        d_solved = jnp.concatenate([-carried * mm(d_fresh, state), d_fresh], -1)
        d_scaled = mm(tt_ref[h], d_solved)
        d_value = beta * d_scaled[:, HD:]
        d_key = d_key + beta * d_scaled[:, :HD]
        d_beta = jnp.sum(d_scaled[:, :HD] * key.astype(F32) + d_scaled[:, HD:] * value.astype(F32), -1, keepdims=True)
        d_lower = jnp.where(below, -mm(d_scaled, solved, NT), 0.0)
        d_beta = d_beta + jnp.sum(d_lower * pdot(key, key, NT), -1, keepdims=True)
        d_gram = beta * d_lower
        d_key = d_key + mm(d_gram, key) + mm(d_gram, key, TN)
        logits = jnp.where(lane == h, d_beta * beta * (1.0 - beta), logits)
        g_main, g_head = [], []
        for i, grad in enumerate((d_query, d_key, d_value)):
            taps = taps_ref[h, i]
            pre = pre_ref[h, i].astype(F32)
            total = conv_forward(pre, taps, age)
            sig = sigmoid(total)
            if i < 2:
                act = total * sig
                ratio = l2_ratio(act)
                unit = act * ratio
                grad = ratio * (grad - unit * jnp.sum(grad * unit, -1, keepdims=True))
            grad = grad * sig * (1.0 + total * (1.0 - sig))
            back = jnp.zeros((ext, HD), F32)
            for k in range(CONV):
                reach = CONV - 1 - k
                grad_k = jnp.where(age >= reach, grad, 0.0)
                cg_ref[h, i * CONV + k : i * CONV + k + 1, :] = jnp.sum(grad_k * conv_rows(pre, reach), 0, keepdims=True)
                padded = jnp.concatenate([top, grad_k])
                back = back + (pltpu.roll(padded, ext - reach, 0) if reach else padded) * taps[k : k + 1]
            g_main.append(back[PAD:].astype(BF16))
            g_head.append(back[:PAD].astype(BF16))
            part = part + pdot(g_main[i], w_ref[h, i], NT)
            ahead = ahead + pdot(g_head[i], w_ref[h, i], NT)
        piece = pdot(xt, jnp.concatenate(g_main, -1)) + pdot(xh, jnp.concatenate(g_head, -1))
        piece = piece.astype(BF16)
        places = (
            (keep_ref.at[0], keep_ref.at[1]),
            (x_ref.at[1], late_x_ref),
            (late_y_ref, y2_ref.at[1]),
            (x_ref.at[0], y2_ref.at[0]),
        )
        for j, (a, b) in enumerate(places):

            @pl.when(ctx ^ j == h)
            def _(a=a, b=b, j=j, piece=piece):
                a[...] = piece[:, : 2 * HD]
                b[:, :HD] = piece[:, 2 * HD :]
                b[:, HD:] = og_ref[j]

    logits = logits.astype(BF16)
    part_ref[:rows] = part + pdot(logits, bw_ref[...], NT)
    part_ref[rows:ext] = ahead
    part_ref[ext:] = jnp.zeros((PAD, width), F32)
    part_ref[ext : ext + 1, :HD] = sm_ref[1:2, :HD]
    bg_ref[...] = lax.dot_general(logits, xt, (((0,), (1,)), ((), ())), preferred_element_type=F32)[:PAD]


def last_kernel(x_ref, gain_ref, part_ref, other_ref, rim_ref, gm_ref, sm_ref, st_ref, bg_ref, cg_ref, grad_ref, out_ref, small_ref):
    rows, width = x_ref.shape
    heads = cg_ref.shape[0]
    total = part_ref[...] + other_ref[...]
    grad = jnp.concatenate([total[: rows - PAD], total[rows - PAD : rows] + rim_ref[...]])
    value_grad, gain_grad = norm_back(x_ref[...].astype(F32), gain_ref[...], grad)
    grad_ref[...] = gm_ref[...] + value_grad
    small_ref[...] = jnp.zeros_like(small_ref)
    small_ref[0:1] = gain_grad
    small_ref[1:2] = sm_ref[0:1]
    small_ref[2 : 2 + heads] = bg_ref[:heads]
    small_ref[6:9] = st_ref[0:3]
    small_ref[9:11] = sm_ref[2:4]
    small_ref[11:12] = sm_ref[4:5]
    at = WIDE_ROWS + 6
    for h in range(heads):
        small_ref[at : at + 3 * CONV, h * HD : (h + 1) * HD] = cg_ref[h, : 3 * CONV]
    at += 3 * CONV
    small_ref[at : at + 1, :HD] = total[rows + PAD : rows + PAD + 1, :HD]
    out_ref[...] = small_ref[...].astype(BF16)


def mixer_sum_kernel(meta, keep_ref, x_ref, y_ref, late_y_ref, late_x_ref, s0, s1, s2, s3, *outs, n_fsdp):
    width, half = x_ref.shape[1:]
    d_loc = width // n_fsdp
    grouped = len(outs) < n_fsdp
    small = (s0[...].astype(F32) + s1[...].astype(F32)) + (s2[...].astype(F32) + s3[...].astype(F32))
    rows, lanes = iota((SMALL_ROWS, 2 * half), 0), iota((SMALL_ROWS, 2 * half), 1)
    stats = jnp.sum(small, -1, keepdims=True)
    high = stats.astype(BF16).astype(F32)
    common = jnp.where(rows < WIDE_ROWS + 6, jnp.where(lanes < half + HD, high, stats - high), small[:, : 2 * half])
    for r in range(n_fsdp):
        shard = r if grouped else lax.rem(meta[1] + r, n_fsdp)
        ref, first = (outs[0], r * (d_loc + SMALL_ROWS)) if grouped else (outs[r], 0)
        at = pl.ds(r * d_loc if grouped else pl.multiple_of(shard * d_loc, d_loc), d_loc)
        a = keep_ref[0, at, :].astype(F32) + x_ref[1, at, :].astype(F32) + late_y_ref[at, :].astype(F32)
        b = keep_ref[1, at, :].astype(F32) + y_ref[1, at, :].astype(F32) + late_x_ref[at, :].astype(F32)
        ref[first : first + d_loc, :half] = a.astype(BF16)
        ref[first : first + d_loc, half:] = b.astype(BF16)
        slices = [small[:, k * d_loc : (k + 1) * d_loc] for k in ([r] if grouped else range(n_fsdp))]
        mine = slices[0]
        for k in range(1, len(slices)):
            mine = jnp.where(shard == k, slices[k], mine)
        mine = jnp.concatenate([mine, jnp.zeros((SMALL_ROWS, 2 * half - d_loc), F32)], -1)
        ref[first + d_loc : first + d_loc + SMALL_ROWS] = jnp.where(rows < WIDE_ROWS, mine, common).astype(BF16)


def mixer_total_kernel(meta, own_ref, *refs, width):
    far, (mix_ref, first_ref, second_ref, beta_ref, conv_ref, head_ref, rms_ref) = refs[:-7], refs[-7:]
    count, rows = len(far) + 1, mix_ref.shape[0]
    heads, hd_loc = conv_ref.shape[1:]
    total = None
    for f in range(count):
        part = own_ref[...]
        for r, ref in enumerate(far):
            part = jnp.where(lax.rem(meta[1] + count - (r + 1), count) == f, ref[...], part)
        part = part.astype(F32)
        total = part if total is None else total + part
    mix_ref[...] = total[:rows].astype(BF16)
    small = total[rows:]
    first_ref[...] = small[0:1, :rows]
    second_ref[...] = small[1:2, :rows]
    beta_ref[...] = small[:8, :rows].T[:, 2 : 2 + heads]
    for h in range(heads):
        lanes = small[WIDE_ROWS + 6 :, h * HD : (h + 1) * HD]
        mine = lanes[:, :hd_loc]
        for k in range(1, HD // hd_loc):
            mine = jnp.where(meta[1] == k, lanes[:, k * hd_loc : (k + 1) * hd_loc], mine)
        conv_ref[:, h, :] = mine[: 3 * CONV]
        if h == 0:
            head_ref[...] = mine[3 * CONV : 3 * CONV + 1]
    stats = small[WIDE_ROWS : WIDE_ROWS + 6, 2 * HD : 2 * HD + 1] + small[WIDE_ROWS : WIDE_ROWS + 6, 3 * HD : 3 * HD + 1]
    rms_ref[...] = jnp.sqrt(stats[:5] / (stats[5:] * width))


def gate_up_whole_kernel(p_ref, d0, d1, e0, e1, gu_ref, down_ref):
    units = gu_ref.shape[2]
    down_ref[: d0.shape[0]] = d0[...].astype(F32) + d1[...].astype(F32)
    down_ref[d0.shape[0] :] = e0[...].astype(F32) + e1[...].astype(F32)
    for q in range(p_ref.shape[0]):
        for k in range(GU_BLOCKS):
            at = (q * GU_BLOCKS + k) * HD
            if at < 2 * units:
                gu_ref[at // units, :, at % units : at % units + HD] = p_ref[q, :, k * HD : (k + 1) * HD].astype(F32)


def mixer_whole_kernel(meta, p0, p1, p2, p3, qkv_ref, out_ref):
    ctx = meta[0]
    for q in range(4):
        for j, ref in enumerate((p0, p1, p2, p3)):

            @pl.when(ctx ^ j == q)
            def _(ref=ref, q=q):
                for i in range(3):
                    qkv_ref[i, :, q * HD : (q + 1) * HD] = ref[:, i * HD : (i + 1) * HD].astype(F32)
                out_ref[q * HD : (q + 1) * HD, :] = ref[:, 3 * HD :].T.astype(F32)


def sds(*shape, dtype=F32):
    return jax.ShapeDtypeStruct(shape, dtype)


def call(body, name, out_shape, in_specs, args, scratch=(), gflops=1, mbytes=4):
    return pl.pallas_call(
        body,
        name=name,
        in_specs=in_specs,
        out_specs=jax.tree.map(lambda _: VMEM, out_shape),
        out_shape=out_shape,
        scratch_shapes=list(scratch),
        compiler_params=pltpu.CompilerParams(vmem_limit_bytes=56 * 1024 * 1024),
        cost_estimate=pl.CostEstimate(flops=int(COST * US[name] * 1_150_000_000), bytes_accessed=10**6, transcendentals=0),
    )(*args)


def shifted(value, axis, steps):
    count = lax.axis_size(axis)
    first, end = max(0, -steps), min(count, count - steps)
    return lax.ppermute(value, axis, [(s, s + steps) for s in range(first, end)])


def swapped(value, axis, mask):
    return lax.ppermute(value, axis, [(s, s ^ mask) for s in range(lax.axis_size(axis))])


def far_shards(value):
    count = lax.axis_size("fsdp")
    if count <= 4:
        turns = [[(s, (s + r) % count) for s in range(count)] for r in range(1, count)]
        return [lax.ppermute(value, "fsdp", turn)[None] for turn in turns]
    return [others(lax.all_gather(value, "fsdp", axis=0))]


def others(value):
    return jnp.concatenate([other(value, r) for r in range(1, lax.axis_size("fsdp"))])


def other(value, r):
    count, here = lax.axis_size("fsdp"), lax.axis_index("fsdp")
    return lax.dynamic_index_in_dim(value, (here + count - r) % count, 0)


def local(
    tokens, lengths, norm_gain, qkv_weight, beta_weight, conv_weight, head_gain, out_weight, mlp_gain, gate_up_weight, down_weight, cotangent
):
    rows, width = tokens.shape
    n_ctx, n_fsdp = lax.axis_size("ctx"), lax.axis_size("fsdp")
    ctx, fsdp = lax.axis_index("ctx"), lax.axis_index("fsdp")
    d_loc = qkv_weight.shape[1]
    heads = beta_weight.shape[1]
    units = down_weight.shape[0]
    hd_loc = head_gain.shape[0]
    n_len = lengths.shape[1]
    step = GU_BLOCKS * HD
    ext = rows + PAD
    meta = jnp.concatenate([jnp.stack([ctx, fsdp]).astype(jnp.int32), lengths[0]])

    small = jnp.concatenate([norm_gain, mlp_gain, head_gain, beta_weight.reshape(-1), conv_weight.reshape(-1)])
    small_rows = -(-small.shape[0] // (HD * 16)) * 16
    small = jnp.pad(small, (0, small_rows * HD - small.shape[0])).reshape(small_rows, HD)
    qkv_part = lax.dynamic_slice_in_dim(qkv_weight, ctx * HD, HD, 2).reshape(3 * d_loc, HD)
    out_part = lax.dynamic_slice_in_dim(out_weight, ctx * HD, HD, 0).T
    pack = jnp.concatenate([qkv_part, small])
    packs = lax.all_gather(pack, "fsdp", axis=0)
    pack_far = others(packs)
    out_local = out_weight.T
    gu_local = jnp.concatenate(
        [gate_up_weight[0], gate_up_weight[1], jnp.zeros((d_loc, n_ctx * step - 2 * units), BF16)], -1
    )
    gu_part = lax.dynamic_slice_in_dim(gu_local, ctx * step, step, 1)
    gu_own = lax.all_gather(gu_part, "fsdp", axis=0)
    gu_far = others(gu_own)
    down_full = lax.all_gather(down_weight, "fsdp", axis=1, tiled=True)
    x_ext = jnp.concatenate([shifted(tokens[rows - PAD :], "ctx", 1), tokens])

    cut = 3 * d_loc // 2
    pack_far, out_part = lax.optimization_barrier((pack_far, out_part))
    one, two = swapped(pack_far, "ctx", 1), swapped(pack_far, "ctx", 2)
    out_far = far_shards(out_part)
    three_a, three_b = swapped(one[:, :cut], "ctx", 2), swapped(two[:, cut:], "ctx", 1)
    three_a, three_b, out_far = lax.optimization_barrier((three_a, three_b, out_far))
    out_far = jnp.concatenate(out_far)
    out_pieces = [swapped(out_far, "ctx", j) for j in range(1, n_ctx)]

    flat = packs[:, 3 * d_loc :].reshape(n_fsdp, -1)
    at = 0
    first_gain = flat[:, at : at + d_loc].reshape(1, width).astype(F32)
    at += d_loc
    second_gain = flat[:, at : at + d_loc].reshape(1, width).astype(F32)
    at += d_loc
    head_full = flat[:, at : at + hd_loc].reshape(1, HD).astype(F32)
    at += hd_loc
    beta_full = jnp.pad(flat[:, at : at + d_loc * heads].reshape(width, heads), ((0, 0), (0, HD - heads)))
    at += d_loc * heads
    conv_full = flat[:, at : at + 3 * CONV * heads * hd_loc].reshape(n_fsdp, 3, CONV, heads, hd_loc)
    conv_full = conv_full.transpose(3, 1, 2, 0, 4).reshape(heads, 3, CONV, HD).astype(F32)

    qkv_full, pre, acts, turned, solved, ends_map, normed_t, normed_far, beta = call(
        functools.partial(terms_kernel, lengths=n_len, n_fsdp=n_fsdp, cut=cut),
        "delta_terms",
        (
            sds(heads, 3, width, HD, dtype=BF16),
            sds(heads, 3, ext, HD, dtype=BF16),
            sds(heads, 3, rows, HD, dtype=BF16),
            sds(heads, rows, rows),
            sds(heads, rows, 2 * HD),
            sds(heads, 2, HD, HD, dtype=BF16),
            sds(width, rows, dtype=BF16),
            sds(width, PAD, dtype=BF16),
            sds(rows, HD),
        ),
        [SMEM] + [VMEM] * 4 + [ANY] * 6,
        (meta, x_ext, first_gain, beta_full, conv_full, qkv_weight, packs, one, two, three_a, three_b),
        [pltpu.SemaphoreType.DMA],
        gflops=15,
        mbytes=8,
    )
    arrived = [swapped(ends_map, "ctx", j) for j in range(1, n_ctx)]
    gu_one, gu_two = lax.optimization_barrier((swapped(gu_far, "ctx", 1), swapped(gu_far, "ctx", 2)))
    gu_three = (swapped(gu_one[:, :, : step // 2], "ctx", 2), swapped(gu_two[:, :, step // 2 :], "ctx", 1))
    out_full, mixed, fresh, state, head_out, attn_part = call(
        functools.partial(output_kernel, lengths=n_len, sources=n_ctx - 1, n_fsdp=n_fsdp),
        "delta_outputs",
        (
            sds(heads, width, HD, dtype=BF16),
            sds(heads, rows, HD),
            sds(heads, rows, HD),
            sds(heads, HD, HD),
            sds(rows, heads * HD, dtype=BF16),
            sds(rows, width),
        ),
        [SMEM] + [VMEM] * 3 + [ANY] * (1 + n_ctx) + [VMEM] * len(arrived),
        (meta, solved, acts, head_full, out_local, out_far, *out_pieces, *arrived),
        [pltpu.SemaphoreType.DMA],
        gflops=6,
        mbytes=6,
    )
    attn_other = swapped(attn_part, "tp", 1)

    middle, normed_mid_t, act_t, g_gu, g_ffn, mlp_part, stats, gu_x3, gu_y3 = call(
        functools.partial(mlp_kernel, lengths=n_len, n_fsdp=n_fsdp),
        "mlp",
        (
            sds(rows, width),
            sds(width, rows, dtype=BF16),
            sds(units, rows, dtype=BF16),
            sds(n_ctx, rows, step, dtype=BF16),
            sds(rows, width, dtype=BF16),
            sds(2 * rows, width),
            sds(8, width),
            sds(width, step // 2, dtype=BF16),
            sds(width, step // 2, dtype=BF16),
        ),
        [SMEM] + [VMEM] * 5 + [ANY] * 6 + [VMEM],
        (
            meta, tokens, attn_part, attn_other, second_gain, cotangent, gu_local, gu_own, gu_one, gu_two, *gu_three, down_full,
        ),
        [pltpu.VMEM((n_ctx, width, step), BF16), pltpu.VMEM((rows, n_ctx * step), F32), pltpu.SemaphoreType.DMA],
        gflops=10,
        mbytes=14,
    )
    mlp_other = swapped(mlp_part, "tp", 1)
    quarter = sds(width, step // 2, dtype=BF16)
    double = sds(2, width, step // 2, dtype=BF16)
    gu_grads = call(
        mlp_grads_kernel,
        "mlp_grads",
        (quarter,) * 4 + (double, sds(units, width, dtype=BF16)),
        [VMEM] * 4,
        (normed_mid_t, g_gu, act_t, g_ffn),
        gflops=4,
        mbytes=12,
    )
    mlp_other, gu_grads = lax.optimization_barrier((mlp_other, gu_grads))
    gu_x1, gu_y2, gu_late_x, gu_late_y, gu_keep, down_grad = gu_grads
    from_x3, from_y3 = swapped(gu_x3, "ctx", 1), swapped(gu_y3, "ctx", 2)

    result, g_middle, out_grads, d_mixed, d_fresh, d_state, sums = call(
        functools.partial(middle_kernel, lengths=n_len),
        "middle_back",
        (
            sds(rows, width, dtype=BF16),
            sds(rows, width),
            sds(n_ctx, width, HD, dtype=BF16),
            sds(heads, rows, HD),
            sds(heads, rows, HD),
            sds(heads, HD, HD, dtype=BF16),
            sds(8, width),
        ),
        [SMEM] + [VMEM] * 11,
        (
            meta, mlp_part, mlp_other, middle, cotangent, second_gain, head_full, out_full, head_out, mixed, acts,
            solved,
        ),
        gflops=6,
        mbytes=12,
    )
    behind = [swapped(d_state, "ctx", j) for j in range(1, n_ctx)]

    down_sh = lax.psum_scatter(down_grad, "fsdp", scatter_dimension=1, tiled=True)

    def add(left, right):
        return (left.astype(F32) + right.astype(F32)).astype(BF16)

    gu_x1, gu_y2, _ = lax.optimization_barrier((gu_x1, gu_y2, d_state))
    from_x1, from_y2 = swapped(gu_x1, "ctx", 1), swapped(gu_y2, "ctx", 2)
    gu_late_y, gu_late_x = add(gu_late_y, from_x3), add(gu_late_x, from_y3)
    behind, gu_late_x, gu_late_y = lax.optimization_barrier((behind, gu_late_x, gu_late_y))
    gu_late_y, gu_late_x = swapped(gu_late_y, "ctx", 2), swapped(gu_late_x, "ctx", 1)
    half = sds(width, 2 * HD, dtype=BF16)
    double = sds(2, width, 2 * HD, dtype=BF16)
    back = call(
        functools.partial(delta_back_kernel, lengths=n_len, sources=n_ctx - 1),
        "delta_back",
        (double, double, double, half, half, sds(ext + PAD, width), sds(PAD, width), sds(heads, 16, HD)),
        [SMEM] + [VMEM] * (2 * n_ctx - 2 + 16),
        (
            meta, *behind, *arrived, pre, acts, turned, solved, fresh, state, d_mixed, d_fresh, beta, conv_full, qkv_full, beta_full,
            normed_t, normed_far, sums, out_grads,
        ),
        gflops=16,
        mbytes=16,
    )

    mix_keep, mix_x, mix_y, mix_late_x, mix_late_y, in_part, beta_grad, conv_grad = back
    from_x1, from_y2, gu_late_x, gu_late_y, mix_keep, down_sh = lax.optimization_barrier(
        (from_x1, from_y2, gu_late_x, gu_late_y, mix_keep, down_sh)
    )
    in_other = swapped(in_part, "tp", 1)
    rim = shifted(in_part[rows:ext] + in_other[rows:ext], "ctx", -1)
    mix_from_x, mix_from_y = swapped(mix_x, "ctx", 1), swapped(mix_y, "ctx", 2)
    mix_from_x, mix_from_y, rim, down_sh = lax.optimization_barrier((mix_from_x, mix_from_y, rim, down_sh))
    input_grad, smalls = call(
        last_kernel,
        "input_back",
        (sds(rows, width), sds(SMALL_ROWS, width, dtype=BF16)),
        [VMEM] * 10,
        (tokens, first_gain, in_part, in_other, rim, g_middle, sums, stats, beta_grad, conv_grad),
        [pltpu.VMEM((SMALL_ROWS, width), F32)],
        gflops=1,
        mbytes=6,
    )
    small_pieces = [smalls] + [swapped(smalls, "ctx", j) for j in range(1, n_ctx)]
    gu_sum = [
        (gu_keep[0].astype(F32) + from_x1.astype(F32) + gu_late_y.astype(F32)).astype(BF16),
        (gu_keep[1].astype(F32) + from_y2.astype(F32) + gu_late_x.astype(F32)).astype(BF16),
    ]
    gu_sh = lax.psum_scatter(jnp.concatenate(gu_sum, -1), "fsdp", scatter_dimension=0, tiled=True)

    mix_late_y, mix_late_x = add(mix_late_y, mix_from_x[0]), add(mix_late_x, mix_from_y[0])
    mix_late_y, mix_late_x = lax.optimization_barrier((swapped(mix_late_y, "ctx", 2), swapped(mix_late_x, "ctx", 1)))
    side = units // 2
    down_a, down_b = down_sh[:side], down_sh[side:]
    down_other = swapped(down_a, "ctx", 1), swapped(down_b, "ctx", 2)
    count = n_fsdp if n_fsdp <= 4 else 1
    mix_rows = n_fsdp // count * (d_loc + SMALL_ROWS)
    mix_own, *mix_far = call(
        functools.partial(mixer_sum_kernel, n_fsdp=n_fsdp),
        "mixer_sum",
        (sds(mix_rows, 4 * HD, dtype=BF16),) * count,
        [SMEM] + [VMEM] * (5 + n_ctx),
        (meta, mix_keep, mix_from_x, mix_from_y, mix_late_y, mix_late_x, *small_pieces),
        gflops=1,
        mbytes=6,
    )
    mix_own, down_other, gu_sh = lax.optimization_barrier((mix_own, down_other, gu_sh))
    down_a, down_b = add(down_a, down_other[0]), add(down_b, down_other[1])
    down_parts = (down_a, swapped(down_a, "ctx", 2), down_b, swapped(down_b, "ctx", 1))
    gu_all = lax.all_gather(gu_sh, "ctx", axis=0)
    if count > 1:
        turns = [[(i, (i + r) % n_fsdp) for i in range(n_fsdp)] for r in range(1, n_fsdp)]
        mix_far = [lax.ppermute(part, "fsdp", turn) for part, turn in zip(mix_far, turns, strict=True)]
        mix_far, down_parts = lax.optimization_barrier((mix_far, down_parts))
    else:
        mix_own = lax.psum_scatter(mix_own, "fsdp", scatter_dimension=0, tiled=True)
    mix_sh, first_out, second_out, beta_out, conv_out, head_out_grad, rms = call(
        functools.partial(mixer_total_kernel, width=width),
        "mixer_total",
        (
            sds(d_loc, 4 * HD, dtype=BF16),
            sds(1, d_loc),
            sds(1, d_loc),
            sds(d_loc, heads),
            sds(3 * CONV, heads, hd_loc),
            sds(1, hd_loc),
            sds(5, 1),
        ),
        [SMEM] + [VMEM] * count,
        (meta, mix_own, *mix_far),
        gflops=1,
        mbytes=1,
    )
    def pieces(part):
        return [part] + [swapped(part, "ctx", j) for j in range(1, n_ctx)]

    gu_out, down_out = call(
        gate_up_whole_kernel,
        "gate_up_whole",
        (sds(2, d_loc, units), sds(units, d_loc)),
        [VMEM] * 5,
        (gu_all, *down_parts),
        gflops=1,
        mbytes=6,
    )
    qkv_out, out_out = call(
        mixer_whole_kernel,
        "mixer_whole",
        (sds(3, d_loc, heads * HD), sds(heads * HD, d_loc)),
        [SMEM] + [VMEM] * n_ctx,
        (meta, *pieces(mix_sh)),
        gflops=1,
        mbytes=4,
    )
    return (
        result,
        input_grad,
        first_out.reshape(-1),
        qkv_out,
        beta_out,
        conv_out.reshape(3, CONV, heads, hd_loc),
        head_out_grad.reshape(-1),
        out_out,
        second_out.reshape(-1),
        gu_out,
        down_out,
        rms.reshape(-1),
    )


def solution(mesh):
    return jax.shard_map(
        local,
        mesh=mesh,
        in_specs=(
            P(("fsdp", "ctx"), None),
            P("fsdp", None),
            P("fsdp"),
            P(None, "fsdp", "tp"),
            P("fsdp", "tp"),
            P(None, None, "tp", "fsdp"),
            P("fsdp"),
            P("tp", "fsdp"),
            P("fsdp"),
            P(None, "fsdp", "tp"),
            P("tp", "fsdp"),
            P(("fsdp", "ctx"), None),
        ),
        out_specs=(
            P(("fsdp", "ctx"), None),
            P(("fsdp", "ctx"), None),
            P("fsdp"),
            P(None, "fsdp", "tp"),
            P("fsdp", "tp"),
            P(None, None, "tp", "fsdp"),
            P("fsdp"),
            P("tp", "fsdp"),
            P("fsdp"),
            P(None, "fsdp", "tp"),
            P("tp", "fsdp"),
            P(),
        ),
        check_vma=False,
    )
```
